32 devices in a mesh: cand: 8 (over y, x, core), ref: 4 (over z).
Axes of the slice: x: 2, y: 2, z: 4, core: 2. Of those that a mesh axis runs over, the one named last changes fastest.
Arguments:
- cand_factor: float32 [8192, 512], P('cand'), may hold values from -6 to 6
- ref_factor: float32 [2048, 512], P('ref'), may hold values from -6 to 6
- cand_plan: float32 [8192, 128], P('cand'), may hold values from 0.0625 to 16
- ref_plan: float32 [2048, 128], P('ref'), may hold values from 0.0625 to 16
- weights: float32 [128], replicated, may hold values from 0.5 to 2
Outputs:
- new_cand_plan: float32 [8192, 128], P('cand')
- new_ref_plan: float32 [2048, 128], P('ref')
- new_weights: float32 [128], replicated
The draws below stay inside these ranges and needn't reach their ends.
All inputs are finite; a program needn't handle non-finite values. Where the reference program divides by a largest or mean magnitude, that divisor is 1e-20 or more.
Results may differ from the reference program's by a relative error of at most 0.00019.
Values sent between devices are 32-bit elements; how exact they have to be, the bound alone decides.
No kernel may reach another device: no remote copies, remote signals or barrier semaphores. Data moves between devices by JAX's collectives and lax.ppermute only.
A program may use at most 64 MiB of HBM per device.

```python
import math
import jax
import jax.numpy as jnp
from jax import lax

D = 512
RK = 128
ITERS = 3
NQ = 8192
NR = 2048


def offset_factor(key, row_count, with_offset):
    noise = jax.random.normal(jax.random.fold_in(key, 201), (row_count, D), jnp.float32)
    if with_offset:
        shared = 0.5 * jax.random.normal(jax.random.fold_in(key, 202), (D,), jnp.float32)
        noise = noise + shared[None, :]
    return jnp.clip(noise, -6.0, 6.0)


def column_blocks(key):
    return jax.random.permutation(jax.random.fold_in(key, 101), RK) % 4


def block_plan(key, row_count, salt):
    col_block = column_blocks(key)
    counts = jax.random.randint(jax.random.fold_in(key, salt), (4,), 1, 5)
    picks = jax.random.randint(jax.random.fold_in(key, salt + 1), (row_count,), 0, jnp.sum(counts))
    bounds = jnp.cumsum(counts)
    row_block = jnp.sum((picks[:, None] >= bounds[None, :]).astype(jnp.int32), axis=1)
    base = jnp.exp(jax.random.uniform(jax.random.fold_in(key, salt + 2), (row_count, RK), jnp.float32, math.log(0.25), math.log(4.0)))
    boost = jnp.where(row_block[:, None] == col_block[None, :], 4.0, 0.25)
    return (base * boost).astype(jnp.float32)


def draw_cand_factor(key, part):
    return offset_factor(key, NQ, True)


def draw_ref_factor(key, part):
    return offset_factor(jax.random.fold_in(key, 7), NR, False)


def draw_cand_plan(key, part):
    return block_plan(key, NQ, 300)


def draw_ref_plan(key, part):
    return block_plan(key, NR, 400)


def setup_inputs(seed: int = 0) -> dict:
    key_of = jax.random.split(jax.random.key(seed), 6)
    cand_factor = draw_cand_factor(jax.random.fold_in(key_of[5], 71), 0)
    ref_factor = draw_ref_factor(jax.random.fold_in(key_of[5], 71), 0)
    cand_plan = draw_cand_plan(jax.random.fold_in(key_of[5], 71), 0)
    ref_plan = draw_ref_plan(jax.random.fold_in(key_of[5], 71), 0)
    weights = jnp.clip(jnp.exp(jax.random.uniform(key_of[4], (RK,), jnp.float32, math.log(0.5), math.log(2.0))), 0.5, 2.0)
    return {"cand_factor": cand_factor, "ref_factor": ref_factor, "cand_plan": cand_plan, "ref_plan": ref_plan, "weights": weights}


step_size = 3.0
tiny_value = 1e-6


def contract_rows(left, right):
    return lax.dot_general(left, right, (((0,), (0,)), ((), ())), precision=lax.Precision.HIGHEST, preferred_element_type=jnp.float32)


def reference(cand_factor, ref_factor, cand_plan, ref_plan, weights):
    cand_moment = contract_rows(cand_factor, cand_plan) / NQ
    ref_moment = contract_rows(ref_factor, ref_plan) / NR
    grad_cand = jnp.dot(cand_factor, ref_moment, precision=lax.Precision.HIGHEST) / weights[None, :]
    grad_ref = jnp.dot(ref_factor, cand_moment, precision=lax.Precision.HIGHEST) / weights[None, :]
    grad_weights = -jnp.sum(cand_moment * ref_moment, axis=0) / (weights * weights)
    top = jnp.maximum(jnp.maximum(jnp.max(jnp.abs(grad_cand)), jnp.max(jnp.abs(grad_ref))), jnp.max(jnp.abs(grad_weights))) + tiny_value
    kernel_cand = cand_plan * jnp.exp(-step_size * grad_cand / top)
    kernel_ref = ref_plan * jnp.exp(-step_size * grad_ref / top)
    kernel_weights = weights * jnp.exp(-step_size * grad_weights / top)
    scale_cand = jnp.ones((RK,), jnp.float32)
    scale_ref = jnp.ones((RK,), jnp.float32)
    for repeat_index in range(ITERS):
        row_cand = RK / jnp.dot(kernel_cand, scale_cand, precision=lax.Precision.HIGHEST)
        row_ref = RK / jnp.dot(kernel_ref, scale_ref, precision=lax.Precision.HIGHEST)
        mass_cand = jnp.dot(row_cand, kernel_cand, precision=lax.Precision.HIGHEST) / NQ
        mass_ref = jnp.dot(row_ref, kernel_ref, precision=lax.Precision.HIGHEST) / NR
        new_weights = jnp.cbrt(kernel_weights * scale_cand * mass_cand * scale_ref * mass_ref)
        scale_cand = new_weights / mass_cand
        scale_ref = new_weights / mass_ref
    new_cand_plan = row_cand[:, None] * kernel_cand * scale_cand[None, :]
    new_ref_plan = row_ref[:, None] * kernel_ref * scale_ref[None, :]
    return new_cand_plan, new_ref_plan, new_weights
```

```python
import jax
import jax.numpy as jnp
from jax import lax
from jax.sharding import Mesh, PartitionSpec as P

ITERS = 3

step_size = 3.0
tiny_value = 1e-06

HIGH = lax.Precision.HIGH
f32 = jnp.float32


def dot_nt(left, right):
    return lax.dot_general(
        left, right, (((1,), (1,)), ((), ())), precision=HIGH, preferred_element_type=f32
    )


def dot_tn(left, right):
    return lax.dot_general(
        left, right, (((0,), (0,)), ((), ())), precision=HIGH, preferred_element_type=f32
    )


def partner_lists(count):
    if count & (count - 1) == 0:
        return [[(i, i ^ k) for i in range(count)] for k in range(1, count)]
    return [[(i, (i + k) % count) for i in range(count)] for k in range(1, count)]


def swap_core(array, core_count):
    if core_count == 1:
        return None
    return lax.ppermute(array, "core", [(0, 1), (1, 0)])


def share(array, axes, count):
    pieces = jnp.broadcast_to(array[None], (count,) + array.shape)
    return lax.all_to_all(pieces, axes, 0, 0)


def on_device(cand_factor, ref_factor, cand_plan, ref_plan, weights):
    chips, cores, refs = (lax.axis_size(a) for a in ("chip", "core", "ref"))
    chip, core, ref = (lax.axis_index(a) for a in ("chip", "core", "ref"))
    cand_rows, width = cand_factor.shape
    ref_rows = ref_factor.shape[0]
    rank = weights.shape[0]
    cand_total = cand_rows * chips * cores
    ref_total = ref_rows * refs
    half = width // cores
    cand_cols, ref_cols = rank // chips, rank // refs

    ref_half = lax.dynamic_slice_in_dim(ref_factor, core * half, half, 1)
    ref_part = dot_tn(ref_plan, ref_half) / ref_total
    blocks = ref_part.reshape(refs, ref_cols, half)
    ref_block = lax.dynamic_index_in_dim(blocks, ref, 0, False)
    arrived = []
    for pairs in partner_lists(refs):
        goes_to = jnp.array([b for _, b in pairs], jnp.int32)[ref]
        arrived.append(lax.ppermute(lax.dynamic_index_in_dim(blocks, goes_to, 0, False), "ref", pairs))

    cand_part = dot_tn(cand_plan, cand_factor) / cand_total
    mine = lax.dynamic_slice_in_dim(cand_part, core * half, half, 1)
    if cores > 1:
        mine = mine + swap_core(lax.dynamic_slice_in_dim(cand_part, (1 - core) * half, half, 1), cores)
    pieces = lax.all_to_all(mine.reshape(chips, cand_cols, half), "chip", 0, 0)
    cand_block = jnp.sum(pieces, axis=0)
    for piece in arrived:
        ref_block = ref_block + piece

    def whole_width(part):
        if cores == 1:
            return part
        other = swap_core(part, cores)
        low = jnp.where(core == 0, part, other)
        high = jnp.where(core == 0, other, part)
        return jnp.concatenate([low, high], axis=-1)

    both = whole_width(jnp.concatenate([cand_block, ref_block], axis=0))
    cand_cols_moment, ref_cols_moment = both[:cand_cols], both[cand_cols:]
    w_ref = lax.dynamic_slice_in_dim(weights, ref * ref_cols, ref_cols, 0)
    w_cand = lax.dynamic_slice_in_dim(weights, chip * cand_cols, cand_cols, 0)
    ref_share = lax.dynamic_slice_in_dim(ref_factor, core * (ref_rows // cores), ref_rows // cores, 0)
    local_top = jnp.maximum(
        jnp.max(jnp.abs(dot_nt(cand_factor, ref_cols_moment) / w_ref[None, :])),
        jnp.max(jnp.abs(dot_nt(ref_share, cand_cols_moment) / w_cand[None, :])),
    )

    if cand_cols % refs == 0 and ref_cols % chips == 0:
        a, b = cand_cols // refs, ref_cols // chips
        cand_piece = lax.dynamic_slice_in_dim(cand_block, ref * a, a, 0)
        ref_piece = lax.dynamic_slice_in_dim(ref_block, chip * b, b, 0)
        piece = jnp.concatenate([cand_piece, ref_piece, jnp.broadcast_to(local_top, (8, half))], axis=0)
        got = share(piece, ("chip", "ref"), chips * refs).reshape(chips, refs, a + b + 8, half)
        cand_m = got[:, :, :a].reshape(rank, half)
        ref_m = jnp.swapaxes(got[:, :, a : a + b], 0, 1).reshape(rank, half)
        tops = got[:, :, a + b :, :]
    else:
        a, b = half // refs, half // chips
        cand_piece = lax.dynamic_slice_in_dim(cand_block, ref * a, a, 1).reshape(-1)
        ref_piece = lax.dynamic_slice_in_dim(ref_block, chip * b, b, 1).reshape(-1)
        piece = jnp.concatenate([cand_piece, ref_piece, local_top[None]])
        got = share(piece, ("chip", "ref"), chips * refs).reshape(chips, refs, -1)
        n = cand_piece.shape[0]
        cand_m = got[:, :, :n].reshape(chips, refs, cand_cols, a).transpose(0, 2, 1, 3).reshape(rank, half)
        ref_m = got[:, :, n:-1].reshape(chips, refs, ref_cols, b).transpose(1, 2, 0, 3).reshape(rank, half)
        tops = got[:, :, -1:]
    top_here = jnp.max(tops)
    both = whole_width(jnp.concatenate([cand_m, ref_m, jnp.broadcast_to(top_here, (8, half))], axis=0))
    cand_moment, ref_moment = both[:rank], both[rank : 2 * rank]
    global_top = jnp.max(both[2 * rank :])

    grad_weights = -jnp.sum(cand_moment * ref_moment, axis=1) / (weights * weights)
    top = jnp.maximum(global_top, jnp.max(jnp.abs(grad_weights))) + tiny_value
    kernel_weights = weights * jnp.exp(-step_size * grad_weights / top)
    kernel_cand = cand_plan * jnp.exp(-step_size * (dot_nt(cand_factor, ref_moment) / weights[None, :]) / top)
    kernel_ref = ref_plan * jnp.exp(-step_size * (dot_nt(ref_factor, cand_moment) / weights[None, :]) / top)

    cand_sub = cand_rows // refs
    ref_sub = ref_rows // (chips * cores)
    mine_cand = lax.dynamic_slice_in_dim(kernel_cand, ref * cand_sub, cand_sub, 0)
    mine_ref = lax.dynamic_slice_in_dim(kernel_ref, (chip * cores + core) * ref_sub, ref_sub, 0)
    scale_cand = jnp.ones((rank,), f32)
    scale_ref = jnp.ones((rank,), f32)
    for _ in range(ITERS):
        last_cand, last_ref = scale_cand, scale_ref
        row_cand = rank / jnp.sum(mine_cand * scale_cand[None, :], axis=1, keepdims=True)
        row_ref = rank / jnp.sum(mine_ref * scale_ref[None, :], axis=1, keepdims=True)
        part = jnp.stack(
            [jnp.sum(row_cand * mine_cand, axis=0) / cand_total, jnp.sum(row_ref * mine_ref, axis=0) / ref_total]
        )
        mass = jnp.sum(share(part, ("chip", "core", "ref"), chips * cores * refs), axis=0)
        mass_cand, mass_ref = mass[0], mass[1]
        new_weights = jnp.cbrt(kernel_weights * scale_cand * mass_cand * scale_ref * mass_ref)
        scale_cand = new_weights / mass_cand
        scale_ref = new_weights / mass_ref
    row_cand = rank / jnp.sum(kernel_cand * last_cand[None, :], axis=1, keepdims=True)
    row_ref = rank / jnp.sum(kernel_ref * last_ref[None, :], axis=1, keepdims=True)
    new_cand_plan = row_cand * kernel_cand * scale_cand[None, :]
    new_ref_plan = row_ref * kernel_ref * scale_ref[None, :]
    return (new_cand_plan, new_ref_plan, new_weights)


def solution(mesh):
    cand, ref = mesh.shape["cand"], mesh.shape["ref"]
    cores = 2 if cand % 2 == 0 else 1
    finer = Mesh(mesh.devices.reshape(cand // cores, cores, ref), ("chip", "core", "ref"))
    rows = ("chip", "core")
    in_specs = (P(rows, None), P("ref", None), P(rows, None), P("ref", None), P())
    out_specs = (P(rows, None), P("ref", None), P())
    return jax.shard_map(on_device, mesh=finer, in_specs=in_specs, out_specs=out_specs, check_vma=False)
```

```python
import jax
import jax.numpy as jnp
from jax import lax
from jax.experimental import pallas as pl
from jax.experimental.pallas import tpu as pltpu
from jax.sharding import Mesh, PartitionSpec as P

ITERS = 3

step_size = 3.0
tiny_value = 1e-06

HIGH = lax.Precision.HIGH
f32 = jnp.float32


def dot_nt(left, right):
    return lax.dot_general(
        left, right, (((1,), (1,)), ((), ())), precision=HIGH, preferred_element_type=f32
    )


def dot_tn(left, right):
    return lax.dot_general(
        left, right, (((0,), (0,)), ((), ())), precision=HIGH, preferred_element_type=f32
    )


def partner_lists(count):
    if count & (count - 1) == 0:
        return [[(i, i ^ k) for i in range(count)] for k in range(1, count)]
    return [[(i, (i + k) % count) for i in range(count)] for k in range(1, count)]


def swap_core(array, core_count):
    if core_count == 1:
        return None
    return lax.ppermute(array, "core", [(0, 1), (1, 0)])


def share(array, axes, count):
    pieces = jnp.broadcast_to(array[None], (count,) + array.shape)
    return lax.all_to_all(pieces, axes, 0, 0)


def on_device_any(cand_factor, ref_factor, cand_plan, ref_plan, weights):
    chips, cores, refs = (lax.axis_size(a) for a in ("chip", "core", "ref"))
    chip, core, ref = (lax.axis_index(a) for a in ("chip", "core", "ref"))
    cand_rows, width = cand_factor.shape
    ref_rows = ref_factor.shape[0]
    rank = weights.shape[0]
    cand_total = cand_rows * chips * cores
    ref_total = ref_rows * refs
    half = width // cores
    cand_cols, ref_cols = rank // chips, rank // refs

    ref_half = lax.dynamic_slice_in_dim(ref_factor, core * half, half, 1)
    ref_part = dot_tn(ref_plan, ref_half) / ref_total
    blocks = ref_part.reshape(refs, ref_cols, half)
    ref_block = lax.dynamic_index_in_dim(blocks, ref, 0, False)
    arrived = []
    for pairs in partner_lists(refs):
        goes_to = jnp.array([b for _, b in pairs], jnp.int32)[ref]
        arrived.append(lax.ppermute(lax.dynamic_index_in_dim(blocks, goes_to, 0, False), "ref", pairs))

    cand_part = dot_tn(cand_plan, cand_factor) / cand_total
    mine = lax.dynamic_slice_in_dim(cand_part, core * half, half, 1)
    if cores > 1:
        mine = mine + swap_core(lax.dynamic_slice_in_dim(cand_part, (1 - core) * half, half, 1), cores)
    pieces = lax.all_to_all(mine.reshape(chips, cand_cols, half), "chip", 0, 0)
    cand_block = jnp.sum(pieces, axis=0)
    for piece in arrived:
        ref_block = ref_block + piece

    def whole_width(part):
        if cores == 1:
            return part
        other = swap_core(part, cores)
        low = jnp.where(core == 0, part, other)
        high = jnp.where(core == 0, other, part)
        return jnp.concatenate([low, high], axis=-1)

    both = whole_width(jnp.concatenate([cand_block, ref_block], axis=0))
    cand_cols_moment, ref_cols_moment = both[:cand_cols], both[cand_cols:]
    w_ref = lax.dynamic_slice_in_dim(weights, ref * ref_cols, ref_cols, 0)
    w_cand = lax.dynamic_slice_in_dim(weights, chip * cand_cols, cand_cols, 0)
    ref_share = lax.dynamic_slice_in_dim(ref_factor, core * (ref_rows // cores), ref_rows // cores, 0)
    local_top = jnp.maximum(
        jnp.max(jnp.abs(dot_nt(cand_factor, ref_cols_moment) / w_ref[None, :])),
        jnp.max(jnp.abs(dot_nt(ref_share, cand_cols_moment) / w_cand[None, :])),
    )

    if cand_cols % refs == 0 and ref_cols % chips == 0:
        a, b = cand_cols // refs, ref_cols // chips
        cand_piece = lax.dynamic_slice_in_dim(cand_block, ref * a, a, 0)
        ref_piece = lax.dynamic_slice_in_dim(ref_block, chip * b, b, 0)
        piece = jnp.concatenate([cand_piece, ref_piece, jnp.broadcast_to(local_top, (8, half))], axis=0)
        got = share(piece, ("chip", "ref"), chips * refs).reshape(chips, refs, a + b + 8, half)
        cand_m = got[:, :, :a].reshape(rank, half)
        ref_m = jnp.swapaxes(got[:, :, a : a + b], 0, 1).reshape(rank, half)
        tops = got[:, :, a + b :, :]
    else:
        a, b = half // refs, half // chips
        cand_piece = lax.dynamic_slice_in_dim(cand_block, ref * a, a, 1).reshape(-1)
        ref_piece = lax.dynamic_slice_in_dim(ref_block, chip * b, b, 1).reshape(-1)
        piece = jnp.concatenate([cand_piece, ref_piece, local_top[None]])
        got = share(piece, ("chip", "ref"), chips * refs).reshape(chips, refs, -1)
        n = cand_piece.shape[0]
        cand_m = got[:, :, :n].reshape(chips, refs, cand_cols, a).transpose(0, 2, 1, 3).reshape(rank, half)
        ref_m = got[:, :, n:-1].reshape(chips, refs, ref_cols, b).transpose(1, 2, 0, 3).reshape(rank, half)
        tops = got[:, :, -1:]
    top_here = jnp.max(tops)
    both = whole_width(jnp.concatenate([cand_m, ref_m, jnp.broadcast_to(top_here, (8, half))], axis=0))
    cand_moment, ref_moment = both[:rank], both[rank : 2 * rank]
    global_top = jnp.max(both[2 * rank :])

    grad_weights = -jnp.sum(cand_moment * ref_moment, axis=1) / (weights * weights)
    top = jnp.maximum(global_top, jnp.max(jnp.abs(grad_weights))) + tiny_value
    kernel_weights = weights * jnp.exp(-step_size * grad_weights / top)
    kernel_cand = cand_plan * jnp.exp(-step_size * (dot_nt(cand_factor, ref_moment) / weights[None, :]) / top)
    kernel_ref = ref_plan * jnp.exp(-step_size * (dot_nt(ref_factor, cand_moment) / weights[None, :]) / top)

    cand_sub = cand_rows // refs
    ref_sub = ref_rows // (chips * cores)
    mine_cand = lax.dynamic_slice_in_dim(kernel_cand, ref * cand_sub, cand_sub, 0)
    mine_ref = lax.dynamic_slice_in_dim(kernel_ref, (chip * cores + core) * ref_sub, ref_sub, 0)
    scale_cand = jnp.ones((rank,), f32)
    scale_ref = jnp.ones((rank,), f32)
    for _ in range(ITERS):
        last_cand, last_ref = scale_cand, scale_ref
        row_cand = rank / jnp.sum(mine_cand * scale_cand[None, :], axis=1, keepdims=True)
        row_ref = rank / jnp.sum(mine_ref * scale_ref[None, :], axis=1, keepdims=True)
        part = jnp.stack(
            [jnp.sum(row_cand * mine_cand, axis=0) / cand_total, jnp.sum(row_ref * mine_ref, axis=0) / ref_total]
        )
        mass = jnp.sum(share(part, ("chip", "core", "ref"), chips * cores * refs), axis=0)
        mass_cand, mass_ref = mass[0], mass[1]
        new_weights = jnp.cbrt(kernel_weights * scale_cand * mass_cand * scale_ref * mass_ref)
        scale_cand = new_weights / mass_cand
        scale_ref = new_weights / mass_ref
    row_cand = rank / jnp.sum(kernel_cand * last_cand[None, :], axis=1, keepdims=True)
    row_ref = rank / jnp.sum(kernel_ref * last_ref[None, :], axis=1, keepdims=True)
    new_cand_plan = row_cand * kernel_cand * scale_cand[None, :]
    new_ref_plan = row_ref * kernel_ref * scale_ref[None, :]
    return (new_cand_plan, new_ref_plan, new_weights)


bf16 = jnp.bfloat16


def split(x):
    high = x.astype(bf16)
    return high, (x - high.astype(f32)).astype(bf16)


def mxu(left, right, dims):
    return lax.dot_general(left, right, (dims, ((), ())), preferred_element_type=f32)


def rows_by_cols(left, right):
    lh, ll = split(left)
    rh, rl = split(right)
    nn = ((1,), (0,))
    return mxu(lh, rh, nn) + (mxu(lh, rl, nn) + mxu(ll, rh, nn))


def rows_by_rows(left, right):
    n = right.shape[0]
    lh, ll = split(left)
    rh, rl = split(right)
    nt = ((1,), (1,))
    wide = mxu(lh, jnp.concatenate([rh, rl], axis=0), nt)
    return wide[:, :n] + (wide[:, n:] + mxu(ll, rh, nt))


def call(body, out_shapes, *args, scratch=()):
    outs = [jax.ShapeDtypeStruct(s, f32) for s in out_shapes]
    return pl.pallas_call(
        body,
        out_shape=outs,
        in_specs=[pl.BlockSpec(memory_space=pltpu.VMEM) for _ in args],
        out_specs=[pl.BlockSpec(memory_space=pltpu.VMEM) for _ in outs],
        scratch_shapes=[pltpu.VMEM(s, f32) for s in scratch],
        compiler_params=pltpu.CompilerParams(vmem_limit_bytes=40 << 20),
    )(*args)


def largest(x):
    return jnp.max(jnp.max(jnp.abs(x), axis=0, keepdims=True), axis=1, keepdims=True)


def cube_root(x):
    return jnp.exp(jnp.log(x) * (1.0 / 3.0))


def on_device_tiled(cand_factor, ref_factor, cand_plan, ref_plan, weights):
    chips, cores, refs = (lax.axis_size(a) for a in ("chip", "core", "ref"))
    cand_rows, width = cand_factor.shape
    ref_rows = ref_factor.shape[0]
    rank = weights.shape[0]
    cand_total = cand_rows * chips * cores
    ref_total = ref_rows * refs
    half = width // cores
    ca, ra = rank // chips, rank // refs
    cb, rb = ca // refs, ra // chips
    lanes = half // 128
    cand_sub = cand_rows // refs
    ref_sub = ref_rows // (chips * cores)
    everyone = chips * cores * refs
    pairs = partner_lists(refs)
    xor = refs & (refs - 1) == 0
    weights_row = weights[None, :]

    def moment_parts(factor_ref, plan_ref, *rest):
        outs, full = rest[:-1], rest[-1]
        core, ref = lax.axis_index("core"), lax.axis_index("ref")
        here = factor_ref[:, pl.ds(pl.multiple_of(core * half, half), half)]
        full[...] = rows_by_cols(plan_ref[...].T, here) / ref_total
        for k in range(refs):
            to = ref ^ k if xor else (ref + k) % refs
            outs[k][...] = full[pl.ds(pl.multiple_of(to * ra, ra), ra), :]

    blocks = call(
        moment_parts, [(ra, half)] * refs, ref_factor, ref_plan, scratch=[(rank, half)]
    )
    arrived = [lax.ppermute(b, "ref", p) for b, p in zip(blocks[1:], pairs)]

    def cand_parts(factor_ref, plan_ref, out):
        whole = rows_by_cols(plan_ref[...].T, factor_ref[...]) / cand_total
        for i in range(chips):
            for j in range(cores):
                out[i * cores + j] = whole[i * ca : (i + 1) * ca, j * half : (j + 1) * half]

    (parts,) = call(cand_parts, [(chips * cores, ca, half)], cand_factor, cand_plan)
    pieces = lax.all_to_all(parts, ("chip", "core"), 0, 0)

    def own_blocks(pieces_ref, *rest):
        out = rest[-1]
        out[:ca, :] = jnp.sum(pieces_ref[...], axis=0)
        total = rest[0][...]
        for other in rest[1:-1]:
            total = total + other[...]
        out[ca:, :] = total

    (mine,) = call(own_blocks, [(ca + ra, half)], pieces, blocks[0], *arrived)
    other = swap_core(mine, cores)

    def column_tops(mine_ref, other_ref, cand_ref, ref_ref, w_ref, out, ref_cols, cand_cols):
        chip, core, ref = (lax.axis_index(a) for a in ("chip", "core", "ref"))
        here, there = mine_ref[...], other_ref[...]
        low = jnp.where(core == 0, here, there)
        high = jnp.where(core == 0, there, here)
        ref_cols[...] = jnp.zeros_like(ref_cols)
        cand_cols[...] = jnp.zeros_like(cand_cols)
        at_ref = pl.ds(pl.multiple_of(ref * ra, ra), ra)
        at_cand = pl.ds(pl.multiple_of(chip * ca, ca), ca)
        ref_cols[at_ref, :half] = low[ca:]
        ref_cols[at_ref, half:] = high[ca:]
        cand_cols[at_cand, :half] = low[:ca]
        cand_cols[at_cand, half:] = high[:ca]
        w = w_ref[...]
        grad_cand = rows_by_rows(cand_ref[...], ref_cols[...])
        share_rows = ref_rows // cores
        ref_share = ref_ref[pl.ds(pl.multiple_of(core * share_rows, share_rows), share_rows), :]
        grad_ref = rows_by_rows(ref_share, cand_cols[...])
        tall = jnp.maximum(
            jnp.max(jnp.abs(grad_cand), axis=0, keepdims=True), jnp.max(jnp.abs(grad_ref), axis=0, keepdims=True)
        )
        top = jnp.broadcast_to(tall / w, (8, rank))
        cand_piece = mine_ref[pl.ds(pl.multiple_of(ref * cb, cb), cb), :]
        ref_piece = mine_ref[pl.ds(pl.multiple_of(ca + chip * rb, rb), rb), :]
        for to in range(chips * refs):
            for lane in range(lanes):
                at = slice(lane * 128, (lane + 1) * 128)
                out[to, lane * cb : (lane + 1) * cb, :] = cand_piece[:, at]
                out[to, lanes * cb + lane * rb : lanes * cb + (lane + 1) * rb, :] = ref_piece[:, at]
            out[to, lanes * (cb + rb) :, :] = top

    tall_piece = lanes * (cb + rb) + 8
    (to_all,) = call(
        column_tops,
        [(chips * refs, tall_piece, 128)],
        mine,
        other,
        cand_factor,
        ref_factor,
        weights_row,
        scratch=[(rank, width), (rank, width)],
    )
    got = lax.all_to_all(to_all, ("chip", "ref"), 0, 0)
    got_other = swap_core(got, cores)

    def mass_part(kernel_cand, kernel_ref, scale_cand, scale_ref, out):
        row_cand = rank / jnp.sum(kernel_cand * scale_cand, axis=1, keepdims=True)
        row_ref = rank / jnp.sum(kernel_ref * scale_ref, axis=1, keepdims=True)
        mass_cand = jnp.sum(row_cand * kernel_cand, axis=0, keepdims=True) / cand_total
        mass_ref = jnp.sum(row_ref * kernel_ref, axis=0, keepdims=True) / ref_total
        both = jnp.concatenate([mass_cand, mass_ref], axis=0)
        out[...] = jnp.broadcast_to(both[None], (everyone, 2, rank))

    def first_kernels(
        got_ref, got_other_ref, cand_ref, cand_plan_ref, ref_ref, ref_plan_ref, w_ref,
        cand_moment, ref_moment, state, sub_cand, sub_ref, out,
    ):
        chip, core, ref = (lax.axis_index(a) for a in ("chip", "core", "ref"))
        tops = None
        for i in range(chips):
            for k in range(refs):
                here, there = got_ref[i * refs + k], got_other_ref[i * refs + k]
                low = jnp.where(core == 0, here, there)
                high = jnp.where(core == 0, there, here)
                for part, side in enumerate((low, high)):
                    for lane in range(lanes):
                        at = slice(part * half + lane * 128, part * half + (lane + 1) * 128)
                        row = i * ca + k * cb
                        cand_moment[row : row + cb, at] = side[lane * cb : (lane + 1) * cb]
                        row = k * ra + i * rb
                        start = lanes * cb + lane * rb
                        ref_moment[row : row + rb, at] = side[start : start + rb]
                    top = side[lanes * (cb + rb) :]
                    tops = top if tops is None else jnp.maximum(tops, top)
        w = w_ref[...]
        product = cand_moment[...] * ref_moment[...]
        folded = product[:, :128]
        for lane in range(1, width // 128):
            folded = folded + product[:, lane * 128 : (lane + 1) * 128]
        grad_weights = -jnp.sum(folded.T, axis=0, keepdims=True) / (w * w)
        top = jnp.maximum(jnp.max(tops[:1], axis=1, keepdims=True), largest(grad_weights)) + tiny_value
        kernel_weights = w * jnp.exp(-step_size * grad_weights / top)
        state[0:1, :] = kernel_weights
        state[1:2, :] = jnp.broadcast_to(top, (1, rank))
        state[2:8, :] = jnp.ones((6, rank), f32)
        at = pl.ds(pl.multiple_of(ref * cand_sub, cand_sub), cand_sub)
        grad = rows_by_rows(cand_ref[at, :], ref_moment[...]) / w
        kernel_cand = cand_plan_ref[at, :] * jnp.exp(-step_size * grad / top)
        at = pl.ds(pl.multiple_of((chip * cores + core) * ref_sub, ref_sub), ref_sub)
        grad = rows_by_rows(ref_ref[at, :], cand_moment[...]) / w
        kernel_ref = ref_plan_ref[at, :] * jnp.exp(-step_size * grad / top)
        sub_cand[...] = kernel_cand
        sub_ref[...] = kernel_ref
        ones = jnp.ones((1, rank), f32)
        mass_part(kernel_cand, kernel_ref, ones, ones, out)

    cand_moment, ref_moment, state, sub_cand, sub_ref, out = call(
        first_kernels,
        [(rank, width), (rank, width), (8, rank), (cand_sub, rank), (ref_sub, rank), (everyone, 2, rank)],
        got, got_other, cand_factor, cand_plan, ref_factor, ref_plan, weights_row,
    )

    def update(mass_ref, state):
        mass = jnp.sum(mass_ref[...], axis=0)
        mass_cand, mass_ref = mass[0:1], mass[1:2]
        kernel_weights, scale_cand, scale_ref = state[0:1, :], state[2:3, :], state[3:4, :]
        new_weights = cube_root(kernel_weights * scale_cand * mass_cand * scale_ref * mass_ref)
        return new_weights, new_weights / mass_cand, new_weights / mass_ref

    def next_masses(mass_ref, state_ref, sub_cand_ref, sub_ref_ref, new_state, out):
        _, scale_cand, scale_ref = update(mass_ref, state_ref)
        new_state[...] = state_ref[...]
        new_state[2:3, :] = scale_cand
        new_state[3:4, :] = scale_ref
        mass_part(sub_cand_ref[...], sub_ref_ref[...], scale_cand, scale_ref, out)

    for _ in range(ITERS - 1):
        mass = lax.all_to_all(out, ("chip", "core", "ref"), 0, 0)
        state, out = call(next_masses, [(8, rank), (everyone, 2, rank)], mass, state, sub_cand, sub_ref)
    mass = lax.all_to_all(out, ("chip", "core", "ref"), 0, 0)

    def scaled_rows(
        cand_moment_ref, ref_moment_ref, state_ref, cand_ref, cand_plan_ref, ref_ref, ref_plan_ref, w_ref,
        cand_out, ref_out,
    ):
        w = w_ref[...]
        top = state_ref[1:2, :]
        grad = rows_by_rows(cand_ref[...], ref_moment_ref[...]) / w
        kernel_cand = cand_plan_ref[...] * jnp.exp(-step_size * grad / top)
        cand_out[...] = kernel_cand * (rank / jnp.sum(kernel_cand * state_ref[2:3, :], axis=1, keepdims=True))
        grad = rows_by_rows(ref_ref[...], cand_moment_ref[...]) / w
        kernel_ref = ref_plan_ref[...] * jnp.exp(-step_size * grad / top)
        ref_out[...] = kernel_ref * (rank / jnp.sum(kernel_ref * state_ref[3:4, :], axis=1, keepdims=True))

    rows_cand, rows_ref = call(
        scaled_rows, [(cand_rows, rank), (ref_rows, rank)],
        cand_moment, ref_moment, state, cand_factor, cand_plan, ref_factor, ref_plan, weights_row,
    )

    def finish(mass_ref, state_ref, rows_cand_ref, rows_ref_ref, cand_out, ref_out, w_out):
        new_weights, scale_cand, scale_ref = update(mass_ref, state_ref)
        cand_out[...] = rows_cand_ref[...] * scale_cand
        ref_out[...] = rows_ref_ref[...] * scale_ref
        w_out[...] = new_weights

    new_cand_plan, new_ref_plan, new_weights = call(
        finish, [(cand_rows, rank), (ref_rows, rank), (1, rank)], mass, state, rows_cand, rows_ref
    )
    return new_cand_plan, new_ref_plan, new_weights.reshape(rank)


def on_device(*args):
    chips, cores, refs = (lax.axis_size(a) for a in ("chip", "core", "ref"))
    rank, width = args[4].shape[0], args[0].shape[1]
    rows = (args[0].shape[0] // refs, args[1].shape[0] // (chips * cores))
    tiled = cores == 2 and rank == 128 and rank % (8 * chips * refs) == 0 and width % (128 * cores) == 0
    tiled = tiled and all(n % 8 == 0 for n in rows)
    return (on_device_tiled if tiled else on_device_any)(*args)


def solution(mesh):
    cand, ref = mesh.shape["cand"], mesh.shape["ref"]
    cores = 2 if cand % 2 == 0 else 1
    finer = Mesh(mesh.devices.reshape(cand // cores, cores, ref), ("chip", "core", "ref"))
    rows = ("chip", "core")
    in_specs = (P(rows, None), P("ref", None), P(rows, None), P("ref", None), P())
    out_specs = (P(rows, None), P("ref", None), P())
    return jax.shard_map(on_device, mesh=finer, in_specs=in_specs, out_specs=out_specs, check_vma=False)
```

```python
import jax
import jax.numpy as jnp
from jax import lax
from jax.experimental import pallas as pl
from jax.experimental.pallas import tpu as pltpu
from jax.sharding import Mesh, PartitionSpec as P

ITERS = 3

step_size = 3.0
tiny_value = 1e-06

HIGH = lax.Precision.HIGH
f32 = jnp.float32


def dot_nt(left, right):
    return lax.dot_general(
        left, right, (((1,), (1,)), ((), ())), precision=HIGH, preferred_element_type=f32
    )


def dot_tn(left, right):
    return lax.dot_general(
        left, right, (((0,), (0,)), ((), ())), precision=HIGH, preferred_element_type=f32
    )


def partner_lists(count):
    if count & (count - 1) == 0:
        return [[(i, i ^ k) for i in range(count)] for k in range(1, count)]
    return [[(i, (i + k) % count) for i in range(count)] for k in range(1, count)]


def swap_core(array, core_count):
    if core_count == 1:
        return None
    return lax.ppermute(array, "core", [(0, 1), (1, 0)])


def share(array, axes, count):
    pieces = jnp.broadcast_to(array[None], (count,) + array.shape)
    return lax.all_to_all(pieces, axes, 0, 0)


def on_device_any(cand_factor, ref_factor, cand_plan, ref_plan, weights):
    chips, cores, refs = (lax.axis_size(a) for a in ("chip", "core", "ref"))
    chip, core, ref = (lax.axis_index(a) for a in ("chip", "core", "ref"))
    cand_rows, width = cand_factor.shape
    ref_rows = ref_factor.shape[0]
    rank = weights.shape[0]
    cand_total = cand_rows * chips * cores
    ref_total = ref_rows * refs
    half = width // cores
    cand_cols, ref_cols = rank // chips, rank // refs

    ref_half = lax.dynamic_slice_in_dim(ref_factor, core * half, half, 1)
    ref_part = dot_tn(ref_plan, ref_half) / ref_total
    blocks = ref_part.reshape(refs, ref_cols, half)
    ref_block = lax.dynamic_index_in_dim(blocks, ref, 0, False)
    arrived = []
    for pairs in partner_lists(refs):
        goes_to = jnp.array([b for _, b in pairs], jnp.int32)[ref]
        arrived.append(lax.ppermute(lax.dynamic_index_in_dim(blocks, goes_to, 0, False), "ref", pairs))

    cand_part = dot_tn(cand_plan, cand_factor) / cand_total
    mine = lax.dynamic_slice_in_dim(cand_part, core * half, half, 1)
    if cores > 1:
        mine = mine + swap_core(lax.dynamic_slice_in_dim(cand_part, (1 - core) * half, half, 1), cores)
    pieces = lax.all_to_all(mine.reshape(chips, cand_cols, half), "chip", 0, 0)
    cand_block = jnp.sum(pieces, axis=0)
    for piece in arrived:
        ref_block = ref_block + piece

    def whole_width(part):
        if cores == 1:
            return part
        other = swap_core(part, cores)
        low = jnp.where(core == 0, part, other)
        high = jnp.where(core == 0, other, part)
        return jnp.concatenate([low, high], axis=-1)

    both = whole_width(jnp.concatenate([cand_block, ref_block], axis=0))
    cand_cols_moment, ref_cols_moment = both[:cand_cols], both[cand_cols:]
    w_ref = lax.dynamic_slice_in_dim(weights, ref * ref_cols, ref_cols, 0)
    w_cand = lax.dynamic_slice_in_dim(weights, chip * cand_cols, cand_cols, 0)
    ref_share = lax.dynamic_slice_in_dim(ref_factor, core * (ref_rows // cores), ref_rows // cores, 0)
    local_top = jnp.maximum(
        jnp.max(jnp.abs(dot_nt(cand_factor, ref_cols_moment) / w_ref[None, :])),
        jnp.max(jnp.abs(dot_nt(ref_share, cand_cols_moment) / w_cand[None, :])),
    )

    if cand_cols % refs == 0 and ref_cols % chips == 0:
        a, b = cand_cols // refs, ref_cols // chips
        cand_piece = lax.dynamic_slice_in_dim(cand_block, ref * a, a, 0)
        ref_piece = lax.dynamic_slice_in_dim(ref_block, chip * b, b, 0)
        piece = jnp.concatenate([cand_piece, ref_piece, jnp.broadcast_to(local_top, (8, half))], axis=0)
        got = share(piece, ("chip", "ref"), chips * refs).reshape(chips, refs, a + b + 8, half)
        cand_m = got[:, :, :a].reshape(rank, half)
        ref_m = jnp.swapaxes(got[:, :, a : a + b], 0, 1).reshape(rank, half)
        tops = got[:, :, a + b :, :]
    else:
        a, b = half // refs, half // chips
        cand_piece = lax.dynamic_slice_in_dim(cand_block, ref * a, a, 1).reshape(-1)
        ref_piece = lax.dynamic_slice_in_dim(ref_block, chip * b, b, 1).reshape(-1)
        piece = jnp.concatenate([cand_piece, ref_piece, local_top[None]])
        got = share(piece, ("chip", "ref"), chips * refs).reshape(chips, refs, -1)
        n = cand_piece.shape[0]
        cand_m = got[:, :, :n].reshape(chips, refs, cand_cols, a).transpose(0, 2, 1, 3).reshape(rank, half)
        ref_m = got[:, :, n:-1].reshape(chips, refs, ref_cols, b).transpose(1, 2, 0, 3).reshape(rank, half)
        tops = got[:, :, -1:]
    top_here = jnp.max(tops)
    both = whole_width(jnp.concatenate([cand_m, ref_m, jnp.broadcast_to(top_here, (8, half))], axis=0))
    cand_moment, ref_moment = both[:rank], both[rank : 2 * rank]
    global_top = jnp.max(both[2 * rank :])

    grad_weights = -jnp.sum(cand_moment * ref_moment, axis=1) / (weights * weights)
    top = jnp.maximum(global_top, jnp.max(jnp.abs(grad_weights))) + tiny_value
    kernel_weights = weights * jnp.exp(-step_size * grad_weights / top)
    kernel_cand = cand_plan * jnp.exp(-step_size * (dot_nt(cand_factor, ref_moment) / weights[None, :]) / top)
    kernel_ref = ref_plan * jnp.exp(-step_size * (dot_nt(ref_factor, cand_moment) / weights[None, :]) / top)

    cand_sub = cand_rows // refs
    ref_sub = ref_rows // (chips * cores)
    mine_cand = lax.dynamic_slice_in_dim(kernel_cand, ref * cand_sub, cand_sub, 0)
    mine_ref = lax.dynamic_slice_in_dim(kernel_ref, (chip * cores + core) * ref_sub, ref_sub, 0)
    scale_cand = jnp.ones((rank,), f32)
    scale_ref = jnp.ones((rank,), f32)
    for _ in range(ITERS):
        last_cand, last_ref = scale_cand, scale_ref
        row_cand = rank / jnp.sum(mine_cand * scale_cand[None, :], axis=1, keepdims=True)
        row_ref = rank / jnp.sum(mine_ref * scale_ref[None, :], axis=1, keepdims=True)
        part = jnp.stack(
            [jnp.sum(row_cand * mine_cand, axis=0) / cand_total, jnp.sum(row_ref * mine_ref, axis=0) / ref_total]
        )
        mass = jnp.sum(share(part, ("chip", "core", "ref"), chips * cores * refs), axis=0)
        mass_cand, mass_ref = mass[0], mass[1]
        new_weights = jnp.cbrt(kernel_weights * scale_cand * mass_cand * scale_ref * mass_ref)
        scale_cand = new_weights / mass_cand
        scale_ref = new_weights / mass_ref
    row_cand = rank / jnp.sum(kernel_cand * last_cand[None, :], axis=1, keepdims=True)
    row_ref = rank / jnp.sum(kernel_ref * last_ref[None, :], axis=1, keepdims=True)
    new_cand_plan = row_cand * kernel_cand * scale_cand[None, :]
    new_ref_plan = row_ref * kernel_ref * scale_ref[None, :]
    return (new_cand_plan, new_ref_plan, new_weights)


ORDER = 1
STEPS = 2
bf16 = jnp.bfloat16


def split(x):
    high = x.astype(bf16)
    return high, (x - high.astype(f32)).astype(bf16)


def mxu(left, right, dims):
    return lax.dot_general(left, right, (dims, ((), ())), preferred_element_type=f32)


def rows_by_cols(left, right):
    lh, ll = split(left)
    rh, rl = split(right)
    nn = ((1,), (0,))
    return mxu(lh, rh, nn) + (mxu(lh, rl, nn) + mxu(ll, rh, nn))


def rows_by_rows(left, right):
    n = right.shape[0]
    lh, ll = left
    rh, rl = split(right)
    nt = ((1,), (1,))
    wide = mxu(lh, jnp.concatenate([rh, rl], axis=0), nt)
    return wide[:, :n] + (wide[:, n:] + mxu(ll, rh, nt))


FAST = pl.BlockSpec(memory_space=pltpu.VMEM)
SLOW = pl.BlockSpec(memory_space=pltpu.HBM)


def call(body, outs, *args, scratch=(), slow=(), slow_outs=(), short_outs=(), room=4):
    args = [pltpu.with_memory_space_constraint(a, pltpu.HBM) if i in slow else a for i, a in enumerate(args)]
    return pl.pallas_call(
        body,
        out_shape=[
            pltpu.HBM(s, f32) if i in slow_outs else jax.ShapeDtypeStruct(s, bf16 if i in short_outs else f32)
            for i, s in enumerate(outs)
        ],
        in_specs=[SLOW if i in slow else FAST for i in range(len(args))],
        out_specs=[SLOW if i in slow_outs else FAST for i in range(len(outs))],
        scratch_shapes=[pltpu.VMEM(s, f32) if isinstance(s, tuple) else s for s in scratch],
        compiler_params=pltpu.CompilerParams(vmem_limit_bytes=room << 20),
    )(*args)


def copies(pairs, sems):
    made = [pltpu.make_async_copy(src, dst, sems.at[i]) for i, (src, dst) in enumerate(pairs)]
    for c in made:
        c.start()
    return made


def largest(x):
    return jnp.max(jnp.max(jnp.abs(x), axis=0, keepdims=True), axis=1, keepdims=True)


def cube_root(x):
    return jnp.exp(jnp.log(x) * (1.0 / 3.0))


def on_device_tiled(cand_factor, ref_factor, cand_plan, ref_plan, weights):
    chips, cores, refs = (lax.axis_size(a) for a in ("chip", "core", "ref"))
    cand_rows, width = cand_factor.shape
    ref_rows = ref_factor.shape[0]
    rank = weights.shape[0]
    cand_total = cand_rows * chips * cores
    ref_total = ref_rows * refs
    half = width // cores
    ca, ra = rank // chips, rank // refs
    cb, rb = ca // refs, ra // chips
    lanes = half // 128
    cand_sub = cand_rows // refs
    ref_sub = ref_rows // (chips * cores)
    everyone = chips * cores * refs
    pairs = partner_lists(refs)
    xor = refs & (refs - 1) == 0
    weights_row = weights[None, :]

    steps = STEPS
    step = cand_rows // steps
    dma = pltpu.SemaphoreType.DMA

    share_rows = ref_rows // cores

    def parts(
        cand_hbm, cand_plan_hbm, ref_hbm, ref_plan_hbm,
        out, cand_high, cand_low, share_high, share_low, *rest,
    ):
        blocks = rest[:refs]
        cand, cand_plan, ref_in, ref_plan, whole, ref_whole, sems, ref_sems, out_sems = rest[refs:]
        core, ref = lax.axis_index("core"), lax.axis_index("ref")
        loads = copies(
            [(cand_plan_hbm, cand_plan)]
            + [(cand_hbm.at[pl.ds(i * step, step)], cand.at[pl.ds(i * step, step)]) for i in range(steps)],
            sems,
        )
        loads[0].wait()
        plan_high, plan_low = split(cand_plan[...].T)
        nn = ((1,), (0,))
        total = None
        for i in range(steps):
            loads[1 + i].wait()
            if i == 0:
                ref_loads = copies([(ref_plan_hbm, ref_plan), (ref_hbm, ref_in)], ref_sems)
            rows = slice(i * step, (i + 1) * step)
            high, low = split(cand[rows, :])
            cand_high[rows, :], cand_low[rows, :] = high, low
            part = mxu(plan_high[:, rows], high, nn) + (
                mxu(plan_high[:, rows], low, nn) + mxu(plan_low[:, rows], high, nn)
            )
            total = part if total is None else total + part
        total = total / cand_total
        for i in range(chips):
            for j in range(cores):
                whole[i * cores + j] = total[i * ca : (i + 1) * ca, j * half : (j + 1) * half]
        stores = copies([(whole, out)], out_sems)
        for c in ref_loads:
            c.wait()
        here = ref_in[:, pl.ds(pl.multiple_of(core * half, half), half)]
        ref_whole[...] = rows_by_cols(ref_plan[...].T, here) / ref_total
        for k in range(refs):
            to = ref ^ k if xor else (ref + k) % refs
            blocks[k][...] = ref_whole[pl.ds(pl.multiple_of(to * ra, ra), ra), :]
        share = ref_in[pl.ds(pl.multiple_of(core * share_rows, share_rows), share_rows), :]
        share_high[...], share_low[...] = split(share)
        for c in stores:
            c.wait()

    to_plane, cand_high, cand_low, share_high, share_low, *blocks = call(
        parts,
        [(chips * cores, ca, half), (cand_rows, width), (cand_rows, width), (share_rows, width), (share_rows, width)]
        + [(ra, half)] * refs,
        cand_factor, cand_plan, ref_factor, ref_plan,
        scratch=[
            (cand_rows, width), (cand_rows, rank), (ref_rows, width), (ref_rows, rank), (chips * cores, ca, half),
            (rank, half), dma((steps + 1,)), dma((2,)), dma((1,)),
        ],
        slow=(0, 1, 2, 3),
        slow_outs=(0,),
        short_outs=(1, 2, 3, 4),
        room=16,
    )
    pieces = lax.all_to_all(to_plane, ("chip", "core"), 0, 0)
    order = list(range(1, refs))[::ORDER]
    blocks = [blocks[0]] + [lax.ppermute(blocks[k], "ref", pairs[k - 1]) for k in order]

    def own_blocks(pieces_ref, *rest):
        out = rest[-1]
        out[:ca, :] = jnp.sum(pieces_ref[...], axis=0)
        if len(rest) == 2:
            out[ca:, :] = jnp.sum(rest[0][...], axis=0)
        else:
            total = rest[0][...]
            for other in rest[1:-1]:
                total = total + other[...]
            out[ca:, :] = total

    (mine,) = call(own_blocks, [(ca + ra, half)], pieces, *blocks)
    other = swap_core(mine, cores)

    def column_tops(
        mine_ref, other_ref, cand_high, cand_low, share_high, share_low, w_ref, out, ref_cols, cand_cols
    ):
        chip, core, ref = (lax.axis_index(a) for a in ("chip", "core", "ref"))
        here, there = mine_ref[...], other_ref[...]
        low = jnp.where(core == 0, here, there)
        high = jnp.where(core == 0, there, here)
        ref_cols[...] = jnp.zeros_like(ref_cols)
        cand_cols[...] = jnp.zeros_like(cand_cols)
        at_ref = pl.ds(pl.multiple_of(ref * ra, ra), ra)
        at_cand = pl.ds(pl.multiple_of(chip * ca, ca), ca)
        ref_cols[at_ref, :half] = low[ca:]
        ref_cols[at_ref, half:] = high[ca:]
        cand_cols[at_cand, :half] = low[:ca]
        cand_cols[at_cand, half:] = high[:ca]
        w = w_ref[...]
        grad_cand = rows_by_rows((cand_high[...], cand_low[...]), ref_cols[...])
        grad_ref = rows_by_rows((share_high[...], share_low[...]), cand_cols[...])
        tall = jnp.maximum(
            jnp.max(jnp.abs(grad_cand), axis=0, keepdims=True), jnp.max(jnp.abs(grad_ref), axis=0, keepdims=True)
        )
        top = jnp.broadcast_to(tall / w, (8, rank))
        cand_piece = mine_ref[pl.ds(pl.multiple_of(ref * cb, cb), cb), :]
        ref_piece = mine_ref[pl.ds(pl.multiple_of(ca + chip * rb, rb), rb), :]
        for to in range(chips * refs):
            for lane in range(lanes):
                at = slice(lane * 128, (lane + 1) * 128)
                out[to, lane * cb : (lane + 1) * cb, :] = cand_piece[:, at]
                out[to, lanes * cb + lane * rb : lanes * cb + (lane + 1) * rb, :] = ref_piece[:, at]
            out[to, lanes * (cb + rb) :, :] = top

    tall_piece = lanes * (cb + rb) + 8
    (to_all,) = call(
        column_tops,
        [(chips * refs, tall_piece, 128)],
        mine,
        other,
        cand_high,
        cand_low,
        share_high,
        share_low,
        weights_row,
        scratch=[(rank, width), (rank, width)],
        room=12,
    )
    got = lax.all_to_all(to_all, ("chip", "ref"), 0, 0)
    got_other = swap_core(got, cores)

    def mass_part(kernel_cand, kernel_ref, scale_cand, scale_ref, out):
        row_cand = rank / jnp.sum(kernel_cand * scale_cand, axis=1, keepdims=True)
        row_ref = rank / jnp.sum(kernel_ref * scale_ref, axis=1, keepdims=True)
        mass_cand = jnp.sum(row_cand * kernel_cand, axis=0, keepdims=True) / cand_total
        mass_ref = jnp.sum(row_ref * kernel_ref, axis=0, keepdims=True) / ref_total
        both = jnp.concatenate([mass_cand, mass_ref], axis=0)
        out[...] = jnp.broadcast_to(both[None], (everyone, 2, rank))

    def first_kernels(
        got_ref, got_other_ref, cand_high, cand_low, cand_plan_ref, share_high, share_low, ref_plan_ref, w_ref,
        cand_moment, full_cand, state, sub_cand, sub_ref, out, ref_moment,
    ):
        chip, core, ref = (lax.axis_index(a) for a in ("chip", "core", "ref"))
        tops = None
        for i in range(chips):
            for k in range(refs):
                here, there = got_ref[i * refs + k], got_other_ref[i * refs + k]
                low = jnp.where(core == 0, here, there)
                high = jnp.where(core == 0, there, here)
                for part, side in enumerate((low, high)):
                    for lane in range(lanes):
                        at = slice(part * half + lane * 128, part * half + (lane + 1) * 128)
                        row = i * ca + k * cb
                        cand_moment[row : row + cb, at] = side[lane * cb : (lane + 1) * cb]
                        row = k * ra + i * rb
                        start = lanes * cb + lane * rb
                        ref_moment[row : row + rb, at] = side[start : start + rb]
                    top = side[lanes * (cb + rb) :]
                    tops = top if tops is None else jnp.maximum(tops, top)
        w = w_ref[...]
        product = cand_moment[...] * ref_moment[...]
        folded = product[:, :128]
        for lane in range(1, width // 128):
            folded = folded + product[:, lane * 128 : (lane + 1) * 128]
        grad_weights = -jnp.sum(folded.T, axis=0, keepdims=True) / (w * w)
        top = jnp.maximum(jnp.max(tops[:1], axis=1, keepdims=True), largest(grad_weights)) + tiny_value
        kernel_weights = w * jnp.exp(-step_size * grad_weights / top)
        state[0:1, :] = kernel_weights
        state[1:2, :] = jnp.broadcast_to(top, (1, rank))
        state[2:8, :] = jnp.ones((6, rank), f32)
        grad = rows_by_rows((cand_high[...], cand_low[...]), ref_moment[...]) / w
        full_cand[...] = cand_plan_ref[...] * jnp.exp(-step_size * grad / top)
        kernel_cand = full_cand[pl.ds(pl.multiple_of(ref * cand_sub, cand_sub), cand_sub), :]
        at = pl.ds(pl.multiple_of(chip * ref_sub, ref_sub), ref_sub)
        grad = rows_by_rows((share_high[at, :], share_low[at, :]), cand_moment[...]) / w
        at = pl.ds(pl.multiple_of(core * share_rows + chip * ref_sub, ref_sub), ref_sub)
        kernel_ref = ref_plan_ref[at, :] * jnp.exp(-step_size * grad / top)
        sub_cand[...] = kernel_cand
        sub_ref[...] = kernel_ref
        ones = jnp.ones((1, rank), f32)
        mass_part(kernel_cand, kernel_ref, ones, ones, out)

    cand_moment, full_cand, state, sub_cand, sub_ref, out = call(
        first_kernels,
        [(rank, width), (cand_rows, rank), (8, rank), (cand_sub, rank), (ref_sub, rank), (everyone, 2, rank)],
        got, got_other, cand_high, cand_low, cand_plan, share_high, share_low, ref_plan, weights_row,
        scratch=[(rank, width)],
        room=12,
    )

    def update(mass_ref, state):
        mass = jnp.sum(mass_ref[...], axis=0)
        mass_cand, mass_ref = mass[0:1], mass[1:2]
        kernel_weights, scale_cand, scale_ref = state[0:1, :], state[2:3, :], state[3:4, :]
        new_weights = cube_root(kernel_weights * scale_cand * mass_cand * scale_ref * mass_ref)
        return new_weights, new_weights / mass_cand, new_weights / mass_ref

    def next_masses(mass_ref, state_ref, sub_cand_ref, sub_ref_ref, new_state, out):
        _, scale_cand, scale_ref = update(mass_ref, state_ref)
        new_state[...] = state_ref[...]
        new_state[2:3, :] = scale_cand
        new_state[3:4, :] = scale_ref
        mass_part(sub_cand_ref[...], sub_ref_ref[...], scale_cand, scale_ref, out)

    for _ in range(ITERS - 1):
        mass = lax.all_to_all(out, ("chip", "core", "ref"), 0, 0)
        state, out = call(next_masses, [(8, rank), (everyone, 2, rank)], mass, state, sub_cand, sub_ref)
    mass = lax.all_to_all(out, ("chip", "core", "ref"), 0, 0)

    def finish(
        mass_ref, cand_moment, state_ref, full_cand, ref_ref, ref_plan_ref, w_ref,
        cand_out, ref_out, w_out, cand_done, ref_done, w_done, sems,
    ):
        new_weights, scale_cand, scale_ref = update(mass_ref, state_ref)
        top = state_ref[1:2, :]
        kernel = full_cand[...]
        row = rank / jnp.sum(kernel * state_ref[2:3, :], axis=1, keepdims=True)
        cand_done[...] = row * kernel * scale_cand
        stores = [pltpu.make_async_copy(cand_done, cand_out, sems.at[0])]
        stores[0].start()
        w_done[...] = new_weights
        stores += [pltpu.make_async_copy(w_done, w_out, sems.at[1])]
        stores[1].start()
        grad = rows_by_rows(split(ref_ref[...]), cand_moment[...]) / w_ref[...]
        kernel = ref_plan_ref[...] * jnp.exp(-step_size * grad / top)
        row = rank / jnp.sum(kernel * state_ref[3:4, :], axis=1, keepdims=True)
        ref_done[...] = row * kernel * scale_ref
        stores += [pltpu.make_async_copy(ref_done, ref_out, sems.at[2])]
        stores[2].start()
        for c in stores:
            c.wait()

    new_cand_plan, new_ref_plan, new_weights = call(
        finish,
        [(cand_rows, rank), (ref_rows, rank), (1, rank)],
        mass, cand_moment, state, full_cand, ref_factor, ref_plan, weights_row,
        scratch=[(cand_rows, rank), (ref_rows, rank), (1, rank), dma((3,))],
        slow_outs=(0, 1, 2),
        room=8,
    )
    return new_cand_plan, new_ref_plan, new_weights.reshape(rank)


def on_device(*args):
    chips, cores, refs = (lax.axis_size(a) for a in ("chip", "core", "ref"))
    rank, width = args[4].shape[0], args[0].shape[1]
    rows = (args[0].shape[0] // refs, args[1].shape[0] // (chips * cores))
    tiled = cores == 2 and rank == 128 and rank % (8 * chips * refs) == 0 and width % (128 * cores) == 0
    tiled = tiled and all(n % 8 == 0 for n in rows)
    return (on_device_tiled if tiled else on_device_any)(*args)


def solution(mesh):
    cand, ref = mesh.shape["cand"], mesh.shape["ref"]
    cores = 2 if cand % 2 == 0 else 1
    finer = Mesh(mesh.devices.reshape(cand // cores, cores, ref), ("chip", "core", "ref"))
    rows = ("chip", "core")
    in_specs = (P(rows, None), P("ref", None), P(rows, None), P("ref", None), P())
    out_specs = (P(rows, None), P("ref", None), P())
    return jax.shard_map(on_device, mesh=finer, in_specs=in_specs, out_specs=out_specs, check_vma=False)
```

```python
import jax
import jax.numpy as jnp
from jax import lax
from jax.experimental import pallas as pl
from jax.experimental.pallas import tpu as pltpu
from jax.sharding import Mesh, PartitionSpec as P

ITERS = 3

step_size = 3.0
tiny_value = 1e-06

HIGH = lax.Precision.HIGH
f32 = jnp.float32


def dot_nt(left, right):
    return lax.dot_general(
        left, right, (((1,), (1,)), ((), ())), precision=HIGH, preferred_element_type=f32
    )


def dot_tn(left, right):
    return lax.dot_general(
        left, right, (((0,), (0,)), ((), ())), precision=HIGH, preferred_element_type=f32
    )


def partner_lists(count):
    if count & (count - 1) == 0:
        return [[(i, i ^ k) for i in range(count)] for k in range(1, count)]
    return [[(i, (i + k) % count) for i in range(count)] for k in range(1, count)]


def swap_core(array, core_count):
    if core_count == 1:
        return None
    return lax.ppermute(array, "core", [(0, 1), (1, 0)])


def share(array, axes, count):
    pieces = jnp.broadcast_to(array[None], (count,) + array.shape)
    return lax.all_to_all(pieces, axes, 0, 0)


def on_device_any(cand_factor, ref_factor, cand_plan, ref_plan, weights):
    chips, cores, refs = (lax.axis_size(a) for a in ("chip", "core", "ref"))
    chip, core, ref = (lax.axis_index(a) for a in ("chip", "core", "ref"))
    cand_rows, width = cand_factor.shape
    ref_rows = ref_factor.shape[0]
    rank = weights.shape[0]
    cand_total = cand_rows * chips * cores
    ref_total = ref_rows * refs
    half = width // cores
    cand_cols, ref_cols = rank // chips, rank // refs

    ref_half = lax.dynamic_slice_in_dim(ref_factor, core * half, half, 1)
    ref_part = dot_tn(ref_plan, ref_half) / ref_total
    blocks = ref_part.reshape(refs, ref_cols, half)
    ref_block = lax.dynamic_index_in_dim(blocks, ref, 0, False)
    arrived = []
    for pairs in partner_lists(refs):
        goes_to = jnp.array([b for _, b in pairs], jnp.int32)[ref]
        arrived.append(lax.ppermute(lax.dynamic_index_in_dim(blocks, goes_to, 0, False), "ref", pairs))

    cand_part = dot_tn(cand_plan, cand_factor) / cand_total
    mine = lax.dynamic_slice_in_dim(cand_part, core * half, half, 1)
    if cores > 1:
        mine = mine + swap_core(lax.dynamic_slice_in_dim(cand_part, (1 - core) * half, half, 1), cores)
    pieces = lax.all_to_all(mine.reshape(chips, cand_cols, half), "chip", 0, 0)
    cand_block = jnp.sum(pieces, axis=0)
    for piece in arrived:
        ref_block = ref_block + piece

    def whole_width(part):
        if cores == 1:
            return part
        other = swap_core(part, cores)
        low = jnp.where(core == 0, part, other)
        high = jnp.where(core == 0, other, part)
        return jnp.concatenate([low, high], axis=-1)

    both = whole_width(jnp.concatenate([cand_block, ref_block], axis=0))
    cand_cols_moment, ref_cols_moment = both[:cand_cols], both[cand_cols:]
    w_ref = lax.dynamic_slice_in_dim(weights, ref * ref_cols, ref_cols, 0)
    w_cand = lax.dynamic_slice_in_dim(weights, chip * cand_cols, cand_cols, 0)
    ref_share = lax.dynamic_slice_in_dim(ref_factor, core * (ref_rows // cores), ref_rows // cores, 0)
    local_top = jnp.maximum(
        jnp.max(jnp.abs(dot_nt(cand_factor, ref_cols_moment) / w_ref[None, :])),
        jnp.max(jnp.abs(dot_nt(ref_share, cand_cols_moment) / w_cand[None, :])),
    )

    if cand_cols % refs == 0 and ref_cols % chips == 0:
        a, b = cand_cols // refs, ref_cols // chips
        cand_piece = lax.dynamic_slice_in_dim(cand_block, ref * a, a, 0)
        ref_piece = lax.dynamic_slice_in_dim(ref_block, chip * b, b, 0)
        piece = jnp.concatenate([cand_piece, ref_piece, jnp.broadcast_to(local_top, (8, half))], axis=0)
        got = share(piece, ("chip", "ref"), chips * refs).reshape(chips, refs, a + b + 8, half)
        cand_m = got[:, :, :a].reshape(rank, half)
        ref_m = jnp.swapaxes(got[:, :, a : a + b], 0, 1).reshape(rank, half)
        tops = got[:, :, a + b :, :]
    else:
        a, b = half // refs, half // chips
        cand_piece = lax.dynamic_slice_in_dim(cand_block, ref * a, a, 1).reshape(-1)
        ref_piece = lax.dynamic_slice_in_dim(ref_block, chip * b, b, 1).reshape(-1)
        piece = jnp.concatenate([cand_piece, ref_piece, local_top[None]])
        got = share(piece, ("chip", "ref"), chips * refs).reshape(chips, refs, -1)
        n = cand_piece.shape[0]
        cand_m = got[:, :, :n].reshape(chips, refs, cand_cols, a).transpose(0, 2, 1, 3).reshape(rank, half)
        ref_m = got[:, :, n:-1].reshape(chips, refs, ref_cols, b).transpose(1, 2, 0, 3).reshape(rank, half)
        tops = got[:, :, -1:]
    top_here = jnp.max(tops)
    both = whole_width(jnp.concatenate([cand_m, ref_m, jnp.broadcast_to(top_here, (8, half))], axis=0))
    cand_moment, ref_moment = both[:rank], both[rank : 2 * rank]
    global_top = jnp.max(both[2 * rank :])

    grad_weights = -jnp.sum(cand_moment * ref_moment, axis=1) / (weights * weights)
    top = jnp.maximum(global_top, jnp.max(jnp.abs(grad_weights))) + tiny_value
    kernel_weights = weights * jnp.exp(-step_size * grad_weights / top)
    kernel_cand = cand_plan * jnp.exp(-step_size * (dot_nt(cand_factor, ref_moment) / weights[None, :]) / top)
    kernel_ref = ref_plan * jnp.exp(-step_size * (dot_nt(ref_factor, cand_moment) / weights[None, :]) / top)

    cand_sub = cand_rows // refs
    ref_sub = ref_rows // (chips * cores)
    mine_cand = lax.dynamic_slice_in_dim(kernel_cand, ref * cand_sub, cand_sub, 0)
    mine_ref = lax.dynamic_slice_in_dim(kernel_ref, (chip * cores + core) * ref_sub, ref_sub, 0)
    scale_cand = jnp.ones((rank,), f32)
    scale_ref = jnp.ones((rank,), f32)
    for _ in range(ITERS):
        last_cand, last_ref = scale_cand, scale_ref
        row_cand = rank / jnp.sum(mine_cand * scale_cand[None, :], axis=1, keepdims=True)
        row_ref = rank / jnp.sum(mine_ref * scale_ref[None, :], axis=1, keepdims=True)
        part = jnp.stack(
            [jnp.sum(row_cand * mine_cand, axis=0) / cand_total, jnp.sum(row_ref * mine_ref, axis=0) / ref_total]
        )
        mass = jnp.sum(share(part, ("chip", "core", "ref"), chips * cores * refs), axis=0)
        mass_cand, mass_ref = mass[0], mass[1]
        new_weights = jnp.cbrt(kernel_weights * scale_cand * mass_cand * scale_ref * mass_ref)
        scale_cand = new_weights / mass_cand
        scale_ref = new_weights / mass_ref
    row_cand = rank / jnp.sum(kernel_cand * last_cand[None, :], axis=1, keepdims=True)
    row_ref = rank / jnp.sum(kernel_ref * last_ref[None, :], axis=1, keepdims=True)
    new_cand_plan = row_cand * kernel_cand * scale_cand[None, :]
    new_ref_plan = row_ref * kernel_ref * scale_ref[None, :]
    return (new_cand_plan, new_ref_plan, new_weights)


ORDER = 1
STEPS = 4
bf16 = jnp.bfloat16


def split(x):
    high = x.astype(bf16)
    return high, (x - high.astype(f32)).astype(bf16)


def mxu(left, right, dims):
    return lax.dot_general(left, right, (dims, ((), ())), preferred_element_type=f32)


def rows_by_cols(left, right):
    lh, ll = split(left)
    rh, rl = split(right)
    m, nn = left.shape[0], ((1,), (0,))
    tall = mxu(jnp.concatenate([lh, ll], axis=0), rh, nn)
    return tall[:m] + (tall[m:] + mxu(lh, rl, nn))


def rows_by_rows(left, right):
    n = right.shape[0]
    lh, ll = left
    rh, rl = split(right)
    nt = ((1,), (1,))
    wide = mxu(lh, jnp.concatenate([rh, rl], axis=0), nt)
    return wide[:, :n] + (wide[:, n:] + mxu(ll, rh, nt))


FAST = pl.BlockSpec(memory_space=pltpu.VMEM)
SLOW = pl.BlockSpec(memory_space=pltpu.HBM)


def call(body, outs, *args, scratch=(), slow=(), slow_outs=(), short_outs=(), room=4):
    args = [pltpu.with_memory_space_constraint(a, pltpu.HBM) if i in slow else a for i, a in enumerate(args)]
    return pl.pallas_call(
        body,
        out_shape=[
            pltpu.HBM(s, f32) if i in slow_outs else jax.ShapeDtypeStruct(s, bf16 if i in short_outs else f32)
            for i, s in enumerate(outs)
        ],
        in_specs=[SLOW if i in slow else FAST for i in range(len(args))],
        out_specs=[SLOW if i in slow_outs else FAST for i in range(len(outs))],
        scratch_shapes=[pltpu.VMEM(s, f32) if isinstance(s, tuple) else s for s in scratch],
        compiler_params=pltpu.CompilerParams(vmem_limit_bytes=room << 20),
    )(*args)


def copies(pairs, sems):
    made = [pltpu.make_async_copy(src, dst, sems.at[i]) for i, (src, dst) in enumerate(pairs)]
    for c in made:
        c.start()
    return made


def largest(x):
    return jnp.max(jnp.max(jnp.abs(x), axis=0, keepdims=True), axis=1, keepdims=True)


def cube_root(x):
    return jnp.exp(jnp.log(x) * (1.0 / 3.0))


def on_device_tiled(cand_factor, ref_factor, cand_plan, ref_plan, weights):
    chips, cores, refs = (lax.axis_size(a) for a in ("chip", "core", "ref"))
    cand_rows, width = cand_factor.shape
    ref_rows = ref_factor.shape[0]
    rank = weights.shape[0]
    cand_total = cand_rows * chips * cores
    ref_total = ref_rows * refs
    half = width // cores
    ca, ra = rank // chips, rank // refs
    cb, rb = ca // refs, ra // chips
    lanes = half // 128
    cand_sub = cand_rows // refs
    ref_sub = ref_rows // (chips * cores)
    everyone = chips * cores * refs
    pairs = partner_lists(refs)
    xor = refs & (refs - 1) == 0
    weights_row = weights[None, :]

    steps = STEPS
    step = cand_rows // steps
    dma = pltpu.SemaphoreType.DMA

    share_rows = ref_rows // cores

    def parts(
        cand_hbm, cand_plan_hbm, ref_hbm, ref_plan_hbm,
        out, cand_high, cand_low, share_high, share_low, *rest,
    ):
        blocks = rest[:refs]
        cand, cand_plan, ref_in, ref_plan, whole, ref_whole, sems, ref_sems, out_sem = rest[refs:]
        core, ref = lax.axis_index("core"), lax.axis_index("ref")
        loads = copies(
            [(cand_plan_hbm, cand_plan)]
            + [(cand_hbm.at[pl.ds(i * step, step)], cand.at[pl.ds(i * step, step)]) for i in range(steps)],
            sems,
        )
        ref_loads = []
        loads[0].wait()
        plan = jnp.concatenate(split(cand_plan[...].T), axis=0)
        nn = ((1,), (0,))
        total = None
        for i in range(steps):
            loads[1 + i].wait()
            if i == 0:
                ref_loads = copies([(ref_plan_hbm, ref_plan), (ref_hbm, ref_in)], ref_sems)
            rows = slice(i * step, (i + 1) * step)
            high, low = split(cand[rows, :])
            cand_high[rows, :], cand_low[rows, :] = high, low
            tall = mxu(plan[:, rows], high, nn)
            part = tall[:rank] + (tall[rank:] + mxu(plan[:rank, rows], low, nn))
            total = part if total is None else total + part
        total = total / cand_total
        for i in range(chips):
            for j in range(cores):
                whole[i * cores + j] = total[i * ca : (i + 1) * ca, j * half : (j + 1) * half]
        store = pltpu.make_async_copy(whole, out, out_sem)
        store.start()

        for c in ref_loads:
            c.wait()
        @pl.when(core < cores)
        def _():
            here = ref_in[:, pl.ds(pl.multiple_of(core * half, half), half)]
            ref_whole[...] = rows_by_cols(ref_plan[...].T, here) / ref_total
            for k in range(refs):
                to = ref ^ k if xor else (ref + k) % refs
                blocks[k][...] = ref_whole[pl.ds(pl.multiple_of(to * ra, ra), ra), :]
            share = ref_in[pl.ds(pl.multiple_of(core * share_rows, share_rows), share_rows), :]
            share_high[...], share_low[...] = split(share)

        store.wait()

    to_plane, cand_high, cand_low, share_high, share_low, *blocks = call(
        parts,
        [(chips * cores, ca, half), (cand_rows, width), (cand_rows, width), (share_rows, width), (share_rows, width)]
        + [(ra, half)] * refs,
        cand_factor, cand_plan, ref_factor, ref_plan,
        scratch=[
            (cand_rows, width), (cand_rows, rank), (ref_rows, width), (ref_rows, rank), (chips * cores, ca, half),
            (rank, half), dma((steps + 1,)), dma((2,)), dma(()),
        ],
        slow=(0, 1, 2, 3),
        slow_outs=(0,),
        short_outs=(1, 2, 3, 4),
        room=16,
    )
    pieces = lax.all_to_all(to_plane, ("chip", "core"), 0, 0)
    order = list(range(1, refs))[::ORDER]
    blocks = [blocks[0]] + [lax.ppermute(blocks[k], "ref", pairs[k - 1]) for k in order]

    def own_blocks(pieces_ref, *rest):
        out = rest[-1]
        out[:ca, :] = jnp.sum(pieces_ref[...], axis=0)
        if len(rest) == 2:
            out[ca:, :] = jnp.sum(rest[0][...], axis=0)
        else:
            total = rest[0][...]
            for other in rest[1:-1]:
                total = total + other[...]
            out[ca:, :] = total

    (mine,) = call(own_blocks, [(ca + ra, half)], pieces, *blocks)
    other = swap_core(mine, cores)

    def columns_at(moment, at, columns, padded):
        padded[...] = jnp.zeros_like(padded)
        padded[pl.ds(pl.multiple_of(at * columns, columns), columns), :] = moment
        return padded[...]

    def own_lanes(factor, core):
        return factor[:, pl.ds(pl.multiple_of(core * half, half), half)]

    def half_columns(mine_ref, cand_high, cand_low, share_high, share_low, cand_out, share_out, padded):
        chip, core, ref = (lax.axis_index(a) for a in ("chip", "core", "ref"))
        moment = columns_at(mine_ref[ca:, :], ref, ra, padded)
        cand_out[...] = rows_by_rows((own_lanes(cand_high, core), own_lanes(cand_low, core)), moment)
        moment = columns_at(mine_ref[:ca, :], chip, ca, padded)
        share_out[...] = rows_by_rows((own_lanes(share_high, core), own_lanes(share_low, core)), moment)

    cand_cols_part, share_cols_part = call(
        half_columns,
        [(cand_rows, rank), (share_rows, rank)],
        mine, cand_high, cand_low, share_high, share_low,
        scratch=[(rank, half)],
        room=12,
    )

    def column_tops(
        mine_ref, other_ref, cand_high, cand_low, share_high, share_low, cand_part, share_part, w_ref, out, padded
    ):
        chip, core, ref = (lax.axis_index(a) for a in ("chip", "core", "ref"))
        w = w_ref[...]
        moment = columns_at(other_ref[ca:, :], ref, ra, padded)
        factor = (own_lanes(cand_high, 1 - core), own_lanes(cand_low, 1 - core))
        grad_cand = cand_part[...] + rows_by_rows(factor, moment)
        moment = columns_at(other_ref[:ca, :], chip, ca, padded)
        factor = (own_lanes(share_high, 1 - core), own_lanes(share_low, 1 - core))
        grad_ref = share_part[...] + rows_by_rows(factor, moment)
        tall = jnp.maximum(
            jnp.max(jnp.abs(grad_cand), axis=0, keepdims=True), jnp.max(jnp.abs(grad_ref), axis=0, keepdims=True)
        )
        cand_piece = mine_ref[pl.ds(pl.multiple_of(ref * cb, cb), cb), :]
        ref_piece = mine_ref[pl.ds(pl.multiple_of(ca + chip * rb, rb), rb), :]
        tiles = [p[:, lane * 128 : (lane + 1) * 128] for p in (cand_piece, ref_piece) for lane in range(lanes)]
        piece = jnp.concatenate(tiles + [tall / w], axis=0)
        for to in range(chips * refs):
            out[to * tall_piece : (to + 1) * tall_piece, :] = piece

    tall_piece = lanes * (cb + rb) + 1
    (to_all,) = call(
        column_tops,
        [(chips * refs * tall_piece, 128)],
        mine,
        other,
        cand_high,
        cand_low,
        share_high,
        share_low,
        cand_cols_part,
        share_cols_part,
        weights_row,
        scratch=[(rank, half)],
        room=12,
    )
    to_all = to_all.reshape(chips * refs, tall_piece, 1, 128)
    got = lax.all_to_all(to_all, ("chip", "ref"), 0, 0).reshape(-1, 128)
    got_other = swap_core(got, cores)

    def mass_part(kernel_cand, kernel_ref, scale_cand, scale_ref, out):
        row_cand = rank / jnp.sum(kernel_cand * scale_cand, axis=1, keepdims=True)
        row_ref = rank / jnp.sum(kernel_ref * scale_ref, axis=1, keepdims=True)
        mass_cand = jnp.sum(row_cand * kernel_cand, axis=0, keepdims=True) / cand_total
        mass_ref = jnp.sum(row_ref * kernel_ref, axis=0, keepdims=True) / ref_total
        both = jnp.concatenate([mass_cand, mass_ref], axis=0)
        out[...] = jnp.broadcast_to(both[None], (everyone, 2, rank))

    def assemble(pieces_ref, cand_half, ref_half):
        tops = None
        for i in range(chips):
            for k in range(refs):
                start = (i * refs + k) * tall_piece
                piece = pieces_ref[start : start + tall_piece, :]
                for lane in range(lanes):
                    at = slice(lane * 128, (lane + 1) * 128)
                    row, start = i * ca + k * cb, lane * cb
                    cand_half[row : row + cb, at] = piece[start : start + cb]
                    row, start = k * ra + i * rb, lanes * cb + lane * rb
                    ref_half[row : row + rb, at] = piece[start : start + rb]
                top = piece[tall_piece - 1 :]
                tops = top if tops is None else jnp.maximum(tops, top)
        product = cand_half[...] * ref_half[...]
        folded = product[:, :128]
        for lane in range(1, lanes):
            folded = folded + product[:, lane * 128 : (lane + 1) * 128]
        return tops, jnp.sum(folded.T, axis=0, keepdims=True)

    def half_kernels(
        got_ref, cand_high, cand_low, share_high, share_low, cand_half, cand_out, share_out, rows_out, ref_half
    ):
        chip, core = lax.axis_index("chip"), lax.axis_index("core")
        tops, inner = assemble(got_ref, cand_half, ref_half)
        rows_out[0:1, :] = tops
        rows_out[1:2, :] = inner
        cand_out[...] = rows_by_rows((own_lanes(cand_high, core), own_lanes(cand_low, core)), ref_half[...])
        at = pl.ds(pl.multiple_of(chip * ref_sub, ref_sub), ref_sub)
        lane = pl.ds(pl.multiple_of(core * half, half), half)
        share_out[...] = rows_by_rows((share_high[at, lane], share_low[at, lane]), cand_half[...])

    cand_half, cand_part, share_part, rows_part = call(
        half_kernels,
        [(rank, half), (cand_rows, rank), (ref_sub, rank), (8, rank)],
        got, cand_high, cand_low, share_high, share_low,
        scratch=[(rank, half)],
        room=12,
    )

    def first_kernels(
        got_ref, cand_high, cand_low, cand_plan_ref, share_high, share_low, ref_plan_ref, w_ref,
        cand_half, cand_part, share_part, rows_part,
        cand_moment, full_cand, state, sub_cand, sub_ref, out, other_half, ref_half,
    ):
        chip, core, ref = (lax.axis_index(a) for a in ("chip", "core", "ref"))
        tops, inner = assemble(got_ref, other_half, ref_half)
        tops = jnp.maximum(tops, rows_part[0:1, :])
        cand_moment[:, :half] = jnp.where(core == 0, cand_half[...], other_half[...])
        cand_moment[:, half:] = jnp.where(core == 0, other_half[...], cand_half[...])
        w = w_ref[...]
        grad_weights = -(inner + rows_part[1:2, :]) / (w * w)
        top = jnp.maximum(jnp.max(tops, axis=1, keepdims=True), largest(grad_weights)) + tiny_value
        kernel_weights = w * jnp.exp(-step_size * grad_weights / top)
        state[0:1, :] = kernel_weights
        state[1:2, :] = jnp.broadcast_to(top, (1, rank))
        state[2:8, :] = jnp.ones((6, rank), f32)
        factor = (own_lanes(cand_high, 1 - core), own_lanes(cand_low, 1 - core))
        grad = (cand_part[...] + rows_by_rows(factor, ref_half[...])) / w
        full_cand[...] = cand_plan_ref[...] * jnp.exp(-step_size * grad / top)
        kernel_cand = full_cand[pl.ds(pl.multiple_of(ref * cand_sub, cand_sub), cand_sub), :]
        at = pl.ds(pl.multiple_of(chip * ref_sub, ref_sub), ref_sub)
        lane = pl.ds(pl.multiple_of((1 - core) * half, half), half)
        grad = (share_part[...] + rows_by_rows((share_high[at, lane], share_low[at, lane]), other_half[...])) / w
        at = pl.ds(pl.multiple_of(core * share_rows + chip * ref_sub, ref_sub), ref_sub)
        kernel_ref = ref_plan_ref[at, :] * jnp.exp(-step_size * grad / top)
        sub_cand[...] = kernel_cand
        sub_ref[...] = kernel_ref
        ones = jnp.ones((1, rank), f32)
        mass_part(kernel_cand, kernel_ref, ones, ones, out)

    cand_moment, full_cand, state, sub_cand, sub_ref, out = call(
        first_kernels,
        [(rank, width), (cand_rows, rank), (8, rank), (cand_sub, rank), (ref_sub, rank), (everyone, 2, rank)],
        got_other, cand_high, cand_low, cand_plan, share_high, share_low, ref_plan, weights_row,
        cand_half, cand_part, share_part, rows_part,
        scratch=[(rank, half), (rank, half)],
        room=12,
    )

    def update(mass_ref, state):
        mass = jnp.sum(mass_ref[...], axis=0)
        mass_cand, mass_ref = mass[0:1], mass[1:2]
        kernel_weights, scale_cand, scale_ref = state[0:1, :], state[2:3, :], state[3:4, :]
        new_weights = cube_root(kernel_weights * scale_cand * mass_cand * scale_ref * mass_ref)
        return new_weights, new_weights / mass_cand, new_weights / mass_ref

    def next_masses(mass_ref, state_ref, sub_cand_ref, sub_ref_ref, new_state, out):
        _, scale_cand, scale_ref = update(mass_ref, state_ref)
        new_state[...] = state_ref[...]
        new_state[2:3, :] = scale_cand
        new_state[3:4, :] = scale_ref
        mass_part(sub_cand_ref[...], sub_ref_ref[...], scale_cand, scale_ref, out)

    for _ in range(ITERS - 1):
        mass = lax.all_to_all(out, ("chip", "core", "ref"), 0, 0)
        state, out = call(next_masses, [(8, rank), (everyone, 2, rank)], mass, state, sub_cand, sub_ref)
    mass = lax.all_to_all(out, ("chip", "core", "ref"), 0, 0)

    def finish(
        mass_ref, cand_moment, state_ref, full_cand, ref_ref, ref_plan_ref, w_ref,
        cand_out, ref_out, w_out, cand_done, ref_done, w_done, sems,
    ):
        new_weights, scale_cand, scale_ref = update(mass_ref, state_ref)
        top = state_ref[1:2, :]
        kernel = full_cand[...]
        row = rank / jnp.sum(kernel * state_ref[2:3, :], axis=1, keepdims=True)
        cand_done[...] = row * kernel * scale_cand
        stores = [pltpu.make_async_copy(cand_done, cand_out, sems.at[0])]
        stores[0].start()
        w_done[...] = new_weights
        stores += [pltpu.make_async_copy(w_done, w_out, sems.at[1])]
        stores[1].start()
        grad = rows_by_rows(split(ref_ref[...]), cand_moment[...]) / w_ref[...]
        kernel = ref_plan_ref[...] * jnp.exp(-step_size * grad / top)
        row = rank / jnp.sum(kernel * state_ref[3:4, :], axis=1, keepdims=True)
        ref_done[...] = row * kernel * scale_ref
        stores += [pltpu.make_async_copy(ref_done, ref_out, sems.at[2])]
        stores[2].start()
        for c in stores:
            c.wait()

    new_cand_plan, new_ref_plan, new_weights = call(
        finish,
        [(cand_rows, rank), (ref_rows, rank), (1, rank)],
        mass, cand_moment, state, full_cand, ref_factor, ref_plan, weights_row,
        scratch=[(cand_rows, rank), (ref_rows, rank), (1, rank), dma((3,))],
        slow_outs=(0, 1, 2),
        room=8,
    )
    return new_cand_plan, new_ref_plan, new_weights.reshape(rank)


def on_device(*args):
    chips, cores, refs = (lax.axis_size(a) for a in ("chip", "core", "ref"))
    rank, width = args[4].shape[0], args[0].shape[1]
    rows = (args[0].shape[0] // refs, args[1].shape[0] // (chips * cores))
    tiled = cores == 2 and rank == 128 and rank % (8 * chips * refs) == 0 and width % (128 * cores) == 0
    tiled = tiled and all(n % 8 == 0 for n in rows)
    return (on_device_tiled if tiled else on_device_any)(*args)


def solution(mesh):
    cand, ref = mesh.shape["cand"], mesh.shape["ref"]
    cores = 2 if cand % 2 == 0 else 1
    finer = Mesh(mesh.devices.reshape(cand // cores, cores, ref), ("chip", "core", "ref"))
    rows = ("chip", "core")
    in_specs = (P(rows, None), P("ref", None), P(rows, None), P("ref", None), P())
    out_specs = (P(rows, None), P("ref", None), P())
    return jax.shard_map(on_device, mesh=finer, in_specs=in_specs, out_specs=out_specs, check_vma=False)
```

```python
import jax
import jax.numpy as jnp
from jax import lax
from jax.experimental import pallas as pl
from jax.experimental.pallas import tpu as pltpu
from jax.sharding import Mesh, PartitionSpec as P

ITERS = 3

step_size = 3.0
tiny_value = 1e-06

HIGH = lax.Precision.HIGH
f32 = jnp.float32


def dot_nt(left, right):
    return lax.dot_general(
        left, right, (((1,), (1,)), ((), ())), precision=HIGH, preferred_element_type=f32
    )


def dot_tn(left, right):
    return lax.dot_general(
        left, right, (((0,), (0,)), ((), ())), precision=HIGH, preferred_element_type=f32
    )


def partner_lists(count):
    if count & (count - 1) == 0:
        return [[(i, i ^ k) for i in range(count)] for k in range(1, count)]
    return [[(i, (i + k) % count) for i in range(count)] for k in range(1, count)]


def swap_core(array, core_count):
    if core_count == 1:
        return None
    return lax.ppermute(array, "core", [(0, 1), (1, 0)])


def share(array, axes, count):
    pieces = jnp.broadcast_to(array[None], (count,) + array.shape)
    return lax.all_to_all(pieces, axes, 0, 0)


def on_device_any(cand_factor, ref_factor, cand_plan, ref_plan, weights):
    chips, cores, refs = (lax.axis_size(a) for a in ("chip", "core", "ref"))
    chip, core, ref = (lax.axis_index(a) for a in ("chip", "core", "ref"))
    cand_rows, width = cand_factor.shape
    ref_rows = ref_factor.shape[0]
    rank = weights.shape[0]
    cand_total = cand_rows * chips * cores
    ref_total = ref_rows * refs
    half = width // cores
    cand_cols, ref_cols = rank // chips, rank // refs

    ref_half = lax.dynamic_slice_in_dim(ref_factor, core * half, half, 1)
    ref_part = dot_tn(ref_plan, ref_half) / ref_total
    blocks = ref_part.reshape(refs, ref_cols, half)
    ref_block = lax.dynamic_index_in_dim(blocks, ref, 0, False)
    arrived = []
    for pairs in partner_lists(refs):
        goes_to = jnp.array([b for _, b in pairs], jnp.int32)[ref]
        arrived.append(lax.ppermute(lax.dynamic_index_in_dim(blocks, goes_to, 0, False), "ref", pairs))

    cand_part = dot_tn(cand_plan, cand_factor) / cand_total
    mine = lax.dynamic_slice_in_dim(cand_part, core * half, half, 1)
    if cores > 1:
        mine = mine + swap_core(lax.dynamic_slice_in_dim(cand_part, (1 - core) * half, half, 1), cores)
    pieces = lax.all_to_all(mine.reshape(chips, cand_cols, half), "chip", 0, 0)
    cand_block = jnp.sum(pieces, axis=0)
    for piece in arrived:
        ref_block = ref_block + piece

    def whole_width(part):
        if cores == 1:
            return part
        other = swap_core(part, cores)
        low = jnp.where(core == 0, part, other)
        high = jnp.where(core == 0, other, part)
        return jnp.concatenate([low, high], axis=-1)

    both = whole_width(jnp.concatenate([cand_block, ref_block], axis=0))
    cand_cols_moment, ref_cols_moment = both[:cand_cols], both[cand_cols:]
    w_ref = lax.dynamic_slice_in_dim(weights, ref * ref_cols, ref_cols, 0)
    w_cand = lax.dynamic_slice_in_dim(weights, chip * cand_cols, cand_cols, 0)
    ref_share = lax.dynamic_slice_in_dim(ref_factor, core * (ref_rows // cores), ref_rows // cores, 0)
    local_top = jnp.maximum(
        jnp.max(jnp.abs(dot_nt(cand_factor, ref_cols_moment) / w_ref[None, :])),
        jnp.max(jnp.abs(dot_nt(ref_share, cand_cols_moment) / w_cand[None, :])),
    )

    if cand_cols % refs == 0 and ref_cols % chips == 0:
        a, b = cand_cols // refs, ref_cols // chips
        cand_piece = lax.dynamic_slice_in_dim(cand_block, ref * a, a, 0)
        ref_piece = lax.dynamic_slice_in_dim(ref_block, chip * b, b, 0)
        piece = jnp.concatenate([cand_piece, ref_piece, jnp.broadcast_to(local_top, (8, half))], axis=0)
        got = share(piece, ("chip", "ref"), chips * refs).reshape(chips, refs, a + b + 8, half)
        cand_m = got[:, :, :a].reshape(rank, half)
        ref_m = jnp.swapaxes(got[:, :, a : a + b], 0, 1).reshape(rank, half)
        tops = got[:, :, a + b :, :]
    else:
        a, b = half // refs, half // chips
        cand_piece = lax.dynamic_slice_in_dim(cand_block, ref * a, a, 1).reshape(-1)
        ref_piece = lax.dynamic_slice_in_dim(ref_block, chip * b, b, 1).reshape(-1)
        piece = jnp.concatenate([cand_piece, ref_piece, local_top[None]])
        got = share(piece, ("chip", "ref"), chips * refs).reshape(chips, refs, -1)
        n = cand_piece.shape[0]
        cand_m = got[:, :, :n].reshape(chips, refs, cand_cols, a).transpose(0, 2, 1, 3).reshape(rank, half)
        ref_m = got[:, :, n:-1].reshape(chips, refs, ref_cols, b).transpose(1, 2, 0, 3).reshape(rank, half)
        tops = got[:, :, -1:]
    top_here = jnp.max(tops)
    both = whole_width(jnp.concatenate([cand_m, ref_m, jnp.broadcast_to(top_here, (8, half))], axis=0))
    cand_moment, ref_moment = both[:rank], both[rank : 2 * rank]
    global_top = jnp.max(both[2 * rank :])

    grad_weights = -jnp.sum(cand_moment * ref_moment, axis=1) / (weights * weights)
    top = jnp.maximum(global_top, jnp.max(jnp.abs(grad_weights))) + tiny_value
    kernel_weights = weights * jnp.exp(-step_size * grad_weights / top)
    kernel_cand = cand_plan * jnp.exp(-step_size * (dot_nt(cand_factor, ref_moment) / weights[None, :]) / top)
    kernel_ref = ref_plan * jnp.exp(-step_size * (dot_nt(ref_factor, cand_moment) / weights[None, :]) / top)

    cand_sub = cand_rows // refs
    ref_sub = ref_rows // (chips * cores)
    mine_cand = lax.dynamic_slice_in_dim(kernel_cand, ref * cand_sub, cand_sub, 0)
    mine_ref = lax.dynamic_slice_in_dim(kernel_ref, (chip * cores + core) * ref_sub, ref_sub, 0)
    scale_cand = jnp.ones((rank,), f32)
    scale_ref = jnp.ones((rank,), f32)
    for _ in range(ITERS):
        last_cand, last_ref = scale_cand, scale_ref
        row_cand = rank / jnp.sum(mine_cand * scale_cand[None, :], axis=1, keepdims=True)
        row_ref = rank / jnp.sum(mine_ref * scale_ref[None, :], axis=1, keepdims=True)
        part = jnp.stack(
            [jnp.sum(row_cand * mine_cand, axis=0) / cand_total, jnp.sum(row_ref * mine_ref, axis=0) / ref_total]
        )
        mass = jnp.sum(share(part, ("chip", "core", "ref"), chips * cores * refs), axis=0)
        mass_cand, mass_ref = mass[0], mass[1]
        new_weights = jnp.cbrt(kernel_weights * scale_cand * mass_cand * scale_ref * mass_ref)
        scale_cand = new_weights / mass_cand
        scale_ref = new_weights / mass_ref
    row_cand = rank / jnp.sum(kernel_cand * last_cand[None, :], axis=1, keepdims=True)
    row_ref = rank / jnp.sum(kernel_ref * last_ref[None, :], axis=1, keepdims=True)
    new_cand_plan = row_cand * kernel_cand * scale_cand[None, :]
    new_ref_plan = row_ref * kernel_ref * scale_ref[None, :]
    return (new_cand_plan, new_ref_plan, new_weights)


ORDER = 1
STEPS = 4
bf16 = jnp.bfloat16


def split(x):
    high = x.astype(bf16)
    return high, (x - high.astype(f32)).astype(bf16)


def mxu(left, right, dims):
    return lax.dot_general(left, right, (dims, ((), ())), preferred_element_type=f32)


def rows_by_cols(left, right):
    lh, ll = split(left)
    rh, rl = split(right)
    m, nn = left.shape[0], ((1,), (0,))
    tall = mxu(jnp.concatenate([lh, ll], axis=0), rh, nn)
    return tall[:m] + (tall[m:] + mxu(lh, rl, nn))


def rows_by_rows(left, right):
    n = right.shape[0]
    lh, ll = left
    rh, rl = split(right)
    nt = ((1,), (1,))
    wide = mxu(lh, jnp.concatenate([rh, rl], axis=0), nt)
    return wide[:, :n] + (wide[:, n:] + mxu(ll, rh, nt))


FAST = pl.BlockSpec(memory_space=pltpu.VMEM)
SLOW = pl.BlockSpec(memory_space=pltpu.HBM)


def call(body, outs, *args, scratch=(), slow=(), slow_outs=(), short_outs=(), room=4):
    args = [pltpu.with_memory_space_constraint(a, pltpu.HBM) if i in slow else a for i, a in enumerate(args)]
    return pl.pallas_call(
        body,
        out_shape=[
            pltpu.HBM(s, f32) if i in slow_outs else jax.ShapeDtypeStruct(s, bf16 if i in short_outs else f32)
            for i, s in enumerate(outs)
        ],
        in_specs=[SLOW if i in slow else FAST for i in range(len(args))],
        out_specs=[SLOW if i in slow_outs else FAST for i in range(len(outs))],
        scratch_shapes=[pltpu.VMEM(s, f32) if isinstance(s, tuple) else s for s in scratch],
        compiler_params=pltpu.CompilerParams(vmem_limit_bytes=room << 20),
    )(*args)


def copies(pairs, sems):
    made = [pltpu.make_async_copy(src, dst, sems.at[i]) for i, (src, dst) in enumerate(pairs)]
    for c in made:
        c.start()
    return made


def largest(x):
    return jnp.max(jnp.max(jnp.abs(x), axis=0, keepdims=True), axis=1, keepdims=True)


def cube_root(x):
    return jnp.exp(jnp.log(x) * (1.0 / 3.0))


def on_device_tiled(cand_factor, ref_factor, cand_plan, ref_plan, weights):
    chips, cores, refs = (lax.axis_size(a) for a in ("chip", "core", "ref"))
    cand_rows, width = cand_factor.shape
    ref_rows = ref_factor.shape[0]
    rank = weights.shape[0]
    cand_total = cand_rows * chips * cores
    ref_total = ref_rows * refs
    half = width // cores
    ca, ra = rank // chips, rank // refs
    cb, rb = ca // refs, ra // chips
    lanes = half // 128
    block_rows = lanes * ca
    few = -(-block_rows // (refs + 1))
    last = few * (refs - 1)
    tall_piece = 2 * few + 1
    cand_sub = cand_rows // refs
    ref_sub = ref_rows // (chips * cores)
    everyone = chips * cores * refs
    pairs = partner_lists(refs)
    xor = refs & (refs - 1) == 0
    weights_row = weights[None, :]

    steps = STEPS
    step = cand_rows // steps
    dma = pltpu.SemaphoreType.DMA

    share_rows = ref_rows // cores

    def parts(
        cand_hbm, cand_plan_hbm, ref_hbm, ref_plan_hbm,
        out, cand_high, cand_low, share_high, share_low, *rest,
    ):
        blocks = rest[:refs]
        cand, cand_plan, ref_in, ref_plan, whole, ref_whole, sems, ref_sems, out_sem = rest[refs:]
        core, ref = lax.axis_index("core"), lax.axis_index("ref")
        loads = copies(
            [(cand_plan_hbm, cand_plan)]
            + [(cand_hbm.at[pl.ds(i * step, step)], cand.at[pl.ds(i * step, step)]) for i in range(steps)],
            sems,
        )
        ref_loads = []
        loads[0].wait()
        plan = jnp.concatenate(split(cand_plan[...].T), axis=0)
        nn = ((1,), (0,))
        total = None
        for i in range(steps):
            loads[1 + i].wait()
            if i == 0:
                ref_loads = copies([(ref_plan_hbm, ref_plan), (ref_hbm, ref_in)], ref_sems)
            rows = slice(i * step, (i + 1) * step)
            high, low = split(cand[rows, :])
            cand_high[rows, :], cand_low[rows, :] = high, low
            tall = mxu(plan[:, rows], high, nn)
            part = tall[:rank] + (tall[rank:] + mxu(plan[:rank, rows], low, nn))
            total = part if total is None else total + part
        total = total / cand_total
        for i in range(chips):
            for j in range(cores):
                whole[i * cores + j] = total[i * ca : (i + 1) * ca, j * half : (j + 1) * half]
        store = pltpu.make_async_copy(whole, out, out_sem)
        store.start()

        for c in ref_loads:
            c.wait()
        @pl.when(core < cores)
        def _():
            here = ref_in[:, pl.ds(pl.multiple_of(core * half, half), half)]
            ref_whole[...] = rows_by_cols(ref_plan[...].T, here) / ref_total
            for k in range(refs):
                to = ref ^ k if xor else (ref + k) % refs
                blocks[k][...] = ref_whole[pl.ds(pl.multiple_of(to * ra, ra), ra), :]
            share = ref_in[pl.ds(pl.multiple_of(core * share_rows, share_rows), share_rows), :]
            share_high[...], share_low[...] = split(share)

        store.wait()

    to_plane, cand_high, cand_low, share_high, share_low, *blocks = call(
        parts,
        [(chips * cores, ca, half), (cand_rows, width), (cand_rows, width), (share_rows, width), (share_rows, width)]
        + [(ra, half)] * refs,
        cand_factor, cand_plan, ref_factor, ref_plan,
        scratch=[
            (cand_rows, width), (cand_rows, rank), (ref_rows, width), (ref_rows, rank), (chips * cores, ca, half),
            (rank, half), dma((steps + 1,)), dma((2,)), dma(()),
        ],
        slow=(0, 1, 2, 3),
        slow_outs=(0,),
        short_outs=(1, 2, 3, 4),
        room=16,
    )
    pieces = lax.all_to_all(to_plane, ("chip", "core"), 0, 0)
    order = list(range(1, refs))[::ORDER]
    blocks = [blocks[0]] + [lax.ppermute(blocks[k], "ref", pairs[k - 1]) for k in order]

    def own_blocks(pieces_ref, *rest):
        out = rest[-1]
        out[:ca, :] = jnp.sum(pieces_ref[...], axis=0)
        if len(rest) == 2:
            out[ca:, :] = jnp.sum(rest[0][...], axis=0)
        else:
            total = rest[0][...]
            for other in rest[1:-1]:
                total = total + other[...]
            out[ca:, :] = total

    (mine,) = call(own_blocks, [(ca + ra, half)], pieces, *blocks)
    other = swap_core(mine, cores)

    def columns_at(moment, at, columns, padded):
        padded[...] = jnp.zeros_like(padded)
        padded[pl.ds(pl.multiple_of(at * columns, columns), columns), :] = moment
        return padded[...]

    def own_lanes(factor, core):
        return factor[:, pl.ds(pl.multiple_of(core * half, half), half)]

    def half_columns(mine_ref, cand_high, cand_low, share_high, share_low, cand_out, share_out, padded):
        chip, core, ref = (lax.axis_index(a) for a in ("chip", "core", "ref"))
        moment = columns_at(mine_ref[ca:, :], ref, ra, padded)
        cand_out[...] = rows_by_rows((own_lanes(cand_high, core), own_lanes(cand_low, core)), moment)
        moment = columns_at(mine_ref[:ca, :], chip, ca, padded)
        share_out[...] = rows_by_rows((own_lanes(share_high, core), own_lanes(share_low, core)), moment)

    cand_cols_part, share_cols_part = call(
        half_columns,
        [(cand_rows, rank), (share_rows, rank)],
        mine, cand_high, cand_low, share_high, share_low,
        scratch=[(rank, half)],
        room=12,
    )

    def column_tops(
        mine_ref, other_ref, cand_high, cand_low, share_high, share_low, cand_part, share_part, w_ref, out, padded, rows
    ):
        chip, core, ref = (lax.axis_index(a) for a in ("chip", "core", "ref"))
        w = w_ref[...]
        moment = columns_at(other_ref[ca:, :], ref, ra, padded)
        factor = (own_lanes(cand_high, 1 - core), own_lanes(cand_low, 1 - core))
        grad_cand = cand_part[...] + rows_by_rows(factor, moment)
        moment = columns_at(other_ref[:ca, :], chip, ca, padded)
        factor = (own_lanes(share_high, 1 - core), own_lanes(share_low, 1 - core))
        grad_ref = share_part[...] + rows_by_rows(factor, moment)
        tall = jnp.maximum(
            jnp.max(jnp.abs(grad_cand), axis=0, keepdims=True), jnp.max(jnp.abs(grad_ref), axis=0, keepdims=True)
        )
        for lane in range(lanes):
            at = slice(lane * 128, (lane + 1) * 128)
            rows[lane * ca : (lane + 1) * ca, :] = mine_ref[:ca, at]
            rows[block_rows + lane * ra : block_rows + (lane + 1) * ra, :] = mine_ref[ca:, at]
        top = tall / w
        for e in range(chips):
            for d in range(refs):
                to = lax.rem(chip + chips - e, chips) * refs + lax.rem(ref + refs - d, refs)
                if e and d:
                    part = [rows[few * (d - 1) : few * d, :]]
                    part += [rows[block_rows + few * (e - 1) : block_rows + few * e, :]]
                elif e:
                    part = [rows[last:block_rows, :]]
                else:
                    part = [rows[block_rows + last : 2 * block_rows, :]]
                short = 2 * few - sum(p.shape[0] for p in part)
                part += [jnp.zeros((short, rank), f32)] if short else []
                out[pl.ds(to * tall_piece, tall_piece), :] = jnp.concatenate(part + [top], axis=0)

    (to_all,) = call(
        column_tops,
        [(chips * refs * tall_piece, 128)],
        mine,
        other,
        cand_high,
        cand_low,
        share_high,
        share_low,
        cand_cols_part,
        share_cols_part,
        weights_row,
        scratch=[(rank, half), (2 * block_rows, 128)],
        room=12,
    )
    to_all = to_all.reshape(chips * refs, tall_piece, 1, 128)
    got = lax.all_to_all(to_all, ("chip", "ref"), 0, 0).reshape(-1, 128)
    got_other = swap_core(got, cores)

    def mass_part(kernel_cand, kernel_ref, scale_cand, scale_ref, out):
        row_cand = rank / jnp.sum(kernel_cand * scale_cand, axis=1, keepdims=True)
        row_ref = rank / jnp.sum(kernel_ref * scale_ref, axis=1, keepdims=True)
        mass_cand = jnp.sum(row_cand * kernel_cand, axis=0, keepdims=True) / cand_total
        mass_ref = jnp.sum(row_ref * kernel_ref, axis=0, keepdims=True) / ref_total
        both = jnp.concatenate([mass_cand, mass_ref], axis=0)
        out[...] = jnp.broadcast_to(both[None], (everyone, 2, rank))

    def assemble(pieces_ref, own_ref, cand_half, ref_half, rows):
        chip, ref = lax.axis_index("chip"), lax.axis_index("ref")

        def piece(e, d, start, count):
            at = lax.rem(chip + e, chips) * refs + lax.rem(ref + d, refs)
            return pieces_ref[pl.ds(at * tall_piece + start, count), :]

        def spread(half_ref, at, columns):
            at = pl.ds(pl.multiple_of(at * columns, columns), columns)
            for lane in range(lanes):
                half_ref[at, lane * 128 : (lane + 1) * 128] = rows[lane * columns : (lane + 1) * columns, :]

        cand_half[pl.ds(pl.multiple_of(chip * ca, ca), ca), :] = own_ref[:ca, :]
        ref_half[pl.ds(pl.multiple_of(ref * ra, ra), ra), :] = own_ref[ca:, :]
        for e in range(1, chips):
            rows[last:, :] = piece(e, 0, 0, block_rows - last)
            for d in range(1, refs):
                rows[few * (d - 1) : few * d, :] = piece(e, d, 0, few)
            spread(cand_half, lax.rem(chip + e, chips), ca)
        for d in range(1, refs):
            rows[last:, :] = piece(0, d, 0, block_rows - last)
            for e in range(1, chips):
                rows[few * (e - 1) : few * e, :] = piece(e, d, few, few)
            spread(ref_half, lax.rem(ref + d, refs), ra)
        tops = pieces_ref[tall_piece - 1 : tall_piece, :]
        for i in range(1, chips * refs):
            tops = jnp.maximum(tops, pieces_ref[(i + 1) * tall_piece - 1 : (i + 1) * tall_piece, :])
        product = cand_half[...] * ref_half[...]
        folded = product[:, :128]
        for lane in range(1, lanes):
            folded = folded + product[:, lane * 128 : (lane + 1) * 128]
        return tops, jnp.sum(folded.T, axis=0, keepdims=True)

    def half_kernels(
        got_ref, own_ref, cand_high, cand_low, share_high, share_low,
        cand_half, cand_out, share_out, rows_out, ref_half, rows,
    ):
        chip, core = lax.axis_index("chip"), lax.axis_index("core")
        tops, inner = assemble(got_ref, own_ref, cand_half, ref_half, rows)
        rows_out[0:1, :] = tops
        rows_out[1:2, :] = inner
        cand_out[...] = rows_by_rows((own_lanes(cand_high, core), own_lanes(cand_low, core)), ref_half[...])
        at = pl.ds(pl.multiple_of(chip * ref_sub, ref_sub), ref_sub)
        lane = pl.ds(pl.multiple_of(core * half, half), half)
        share_out[...] = rows_by_rows((share_high[at, lane], share_low[at, lane]), cand_half[...])

    cand_half, cand_part, share_part, rows_part = call(
        half_kernels,
        [(rank, half), (cand_rows, rank), (ref_sub, rank), (8, rank)],
        got, mine, cand_high, cand_low, share_high, share_low,
        scratch=[(rank, half), (block_rows, 128)],
        room=12,
    )

    def first_kernels(
        got_ref, own_ref, cand_high, cand_low, cand_plan_ref, share_high, share_low, ref_plan_ref, w_ref,
        cand_half, cand_part, share_part, rows_part,
        cand_moment, full_cand, state, sub_cand, sub_ref, out, other_half, ref_half, rows,
    ):
        chip, core, ref = (lax.axis_index(a) for a in ("chip", "core", "ref"))
        tops, inner = assemble(got_ref, own_ref, other_half, ref_half, rows)
        tops = jnp.maximum(tops, rows_part[0:1, :])
        cand_moment[:, :half] = jnp.where(core == 0, cand_half[...], other_half[...])
        cand_moment[:, half:] = jnp.where(core == 0, other_half[...], cand_half[...])
        w = w_ref[...]
        grad_weights = -(inner + rows_part[1:2, :]) / (w * w)
        top = jnp.maximum(jnp.max(tops, axis=1, keepdims=True), largest(grad_weights)) + tiny_value
        kernel_weights = w * jnp.exp(-step_size * grad_weights / top)
        state[0:1, :] = kernel_weights
        state[1:2, :] = jnp.broadcast_to(top, (1, rank))
        state[2:8, :] = jnp.ones((6, rank), f32)
        factor = (own_lanes(cand_high, 1 - core), own_lanes(cand_low, 1 - core))
        grad = (cand_part[...] + rows_by_rows(factor, ref_half[...])) / w
        full_cand[...] = cand_plan_ref[...] * jnp.exp(-step_size * grad / top)
        kernel_cand = full_cand[pl.ds(pl.multiple_of(ref * cand_sub, cand_sub), cand_sub), :]
        at = pl.ds(pl.multiple_of(chip * ref_sub, ref_sub), ref_sub)
        lane = pl.ds(pl.multiple_of((1 - core) * half, half), half)
        grad = (share_part[...] + rows_by_rows((share_high[at, lane], share_low[at, lane]), other_half[...])) / w
        at = pl.ds(pl.multiple_of(core * share_rows + chip * ref_sub, ref_sub), ref_sub)
        kernel_ref = ref_plan_ref[at, :] * jnp.exp(-step_size * grad / top)
        sub_cand[...] = kernel_cand
        sub_ref[...] = kernel_ref
        ones = jnp.ones((1, rank), f32)
        mass_part(kernel_cand, kernel_ref, ones, ones, out)

    cand_moment, full_cand, state, sub_cand, sub_ref, out = call(
        first_kernels,
        [(rank, width), (cand_rows, rank), (8, rank), (cand_sub, rank), (ref_sub, rank), (everyone, 2, rank)],
        got_other, other, cand_high, cand_low, cand_plan, share_high, share_low, ref_plan, weights_row,
        cand_half, cand_part, share_part, rows_part,
        scratch=[(rank, half), (rank, half), (block_rows, 128)],
        room=12,
    )

    def update(mass_ref, state):
        mass = jnp.sum(mass_ref[...], axis=0)
        mass_cand, mass_ref = mass[0:1], mass[1:2]
        kernel_weights, scale_cand, scale_ref = state[0:1, :], state[2:3, :], state[3:4, :]
        new_weights = cube_root(kernel_weights * scale_cand * mass_cand * scale_ref * mass_ref)
        return new_weights, new_weights / mass_cand, new_weights / mass_ref

    def next_masses(mass_ref, state_ref, sub_cand_ref, sub_ref_ref, new_state, out):
        _, scale_cand, scale_ref = update(mass_ref, state_ref)
        new_state[...] = state_ref[...]
        new_state[2:3, :] = scale_cand
        new_state[3:4, :] = scale_ref
        mass_part(sub_cand_ref[...], sub_ref_ref[...], scale_cand, scale_ref, out)

    for _ in range(ITERS - 1):
        mass = lax.all_to_all(out, ("chip", "core", "ref"), 0, 0)
        state, out = call(next_masses, [(8, rank), (everyone, 2, rank)], mass, state, sub_cand, sub_ref)
    mass = lax.all_to_all(out, ("chip", "core", "ref"), 0, 0)

    def finish(
        mass_ref, cand_moment, state_ref, full_cand, ref_ref, ref_plan_ref, w_ref,
        cand_out, ref_out, w_out, cand_done, ref_done, w_done, sems,
    ):
        new_weights, scale_cand, scale_ref = update(mass_ref, state_ref)
        top = state_ref[1:2, :]
        kernel = full_cand[...]
        row = rank / jnp.sum(kernel * state_ref[2:3, :], axis=1, keepdims=True)
        cand_done[...] = row * kernel * scale_cand
        stores = [pltpu.make_async_copy(cand_done, cand_out, sems.at[0])]
        stores[0].start()
        w_done[...] = new_weights
        stores += [pltpu.make_async_copy(w_done, w_out, sems.at[1])]
        stores[1].start()
        grad = rows_by_rows(split(ref_ref[...]), cand_moment[...]) / w_ref[...]
        kernel = ref_plan_ref[...] * jnp.exp(-step_size * grad / top)
        row = rank / jnp.sum(kernel * state_ref[3:4, :], axis=1, keepdims=True)
        ref_done[...] = row * kernel * scale_ref
        stores += [pltpu.make_async_copy(ref_done, ref_out, sems.at[2])]
        stores[2].start()
        for c in stores:
            c.wait()

    new_cand_plan, new_ref_plan, new_weights = call(
        finish,
        [(cand_rows, rank), (ref_rows, rank), (1, rank)],
        mass, cand_moment, state, full_cand, ref_factor, ref_plan, weights_row,
        scratch=[(cand_rows, rank), (ref_rows, rank), (1, rank), dma((3,))],
        slow_outs=(0, 1, 2),
        room=8,
    )
    return new_cand_plan, new_ref_plan, new_weights.reshape(rank)


def on_device(*args):
    chips, cores, refs = (lax.axis_size(a) for a in ("chip", "core", "ref"))
    rank, width = args[4].shape[0], args[0].shape[1]
    rows = (args[0].shape[0] // refs, args[1].shape[0] // (chips * cores))
    tiled = cores == 2 and chips == refs and rank == 128 and rank % (8 * chips * refs) == 0 and width % (128 * cores) == 0
    tiled = tiled and all(n % 8 == 0 for n in rows)
    return (on_device_tiled if tiled else on_device_any)(*args)


def solution(mesh):
    cand, ref = mesh.shape["cand"], mesh.shape["ref"]
    cores = 2 if cand % 2 == 0 else 1
    finer = Mesh(mesh.devices.reshape(cand // cores, cores, ref), ("chip", "core", "ref"))
    rows = ("chip", "core")
    in_specs = (P(rows, None), P("ref", None), P(rows, None), P("ref", None), P())
    out_specs = (P(rows, None), P("ref", None), P())
    return jax.shard_map(on_device, mesh=finer, in_specs=in_specs, out_specs=out_specs, check_vma=False)
```

```python
import jax
import jax.numpy as jnp
from jax import lax
from jax.experimental import pallas as pl
from jax.experimental.pallas import tpu as pltpu
from jax.sharding import Mesh, PartitionSpec as P

ITERS = 3

step_size = 3.0
tiny_value = 1e-06

HIGH = lax.Precision.HIGH
f32 = jnp.float32


def dot_nt(left, right):
    return lax.dot_general(
        left, right, (((1,), (1,)), ((), ())), precision=HIGH, preferred_element_type=f32
    )


def dot_tn(left, right):
    return lax.dot_general(
        left, right, (((0,), (0,)), ((), ())), precision=HIGH, preferred_element_type=f32
    )


def partner_lists(count):
    if count & (count - 1) == 0:
        return [[(i, i ^ k) for i in range(count)] for k in range(1, count)]
    return [[(i, (i + k) % count) for i in range(count)] for k in range(1, count)]


def swap_core(array, core_count):
    if core_count == 1:
        return None
    return lax.ppermute(array, "core", [(0, 1), (1, 0)])


def share(array, axes, count):
    pieces = jnp.broadcast_to(array[None], (count,) + array.shape)
    return lax.all_to_all(pieces, axes, 0, 0)


def on_device_any(cand_factor, ref_factor, cand_plan, ref_plan, weights):
    chips, cores, refs = (lax.axis_size(a) for a in ("chip", "core", "ref"))
    chip, core, ref = (lax.axis_index(a) for a in ("chip", "core", "ref"))
    cand_rows, width = cand_factor.shape
    ref_rows = ref_factor.shape[0]
    rank = weights.shape[0]
    cand_total = cand_rows * chips * cores
    ref_total = ref_rows * refs
    half = width // cores
    cand_cols, ref_cols = rank // chips, rank // refs

    ref_half = lax.dynamic_slice_in_dim(ref_factor, core * half, half, 1)
    ref_part = dot_tn(ref_plan, ref_half) / ref_total
    blocks = ref_part.reshape(refs, ref_cols, half)
    ref_block = lax.dynamic_index_in_dim(blocks, ref, 0, False)
    arrived = []
    for pairs in partner_lists(refs):
        goes_to = jnp.array([b for _, b in pairs], jnp.int32)[ref]
        arrived.append(lax.ppermute(lax.dynamic_index_in_dim(blocks, goes_to, 0, False), "ref", pairs))

    cand_part = dot_tn(cand_plan, cand_factor) / cand_total
    mine = lax.dynamic_slice_in_dim(cand_part, core * half, half, 1)
    if cores > 1:
        mine = mine + swap_core(lax.dynamic_slice_in_dim(cand_part, (1 - core) * half, half, 1), cores)
    pieces = lax.all_to_all(mine.reshape(chips, cand_cols, half), "chip", 0, 0)
    cand_block = jnp.sum(pieces, axis=0)
    for piece in arrived:
        ref_block = ref_block + piece

    def whole_width(part):
        if cores == 1:
            return part
        other = swap_core(part, cores)
        low = jnp.where(core == 0, part, other)
        high = jnp.where(core == 0, other, part)
        return jnp.concatenate([low, high], axis=-1)

    both = whole_width(jnp.concatenate([cand_block, ref_block], axis=0))
    cand_cols_moment, ref_cols_moment = both[:cand_cols], both[cand_cols:]
    w_ref = lax.dynamic_slice_in_dim(weights, ref * ref_cols, ref_cols, 0)
    w_cand = lax.dynamic_slice_in_dim(weights, chip * cand_cols, cand_cols, 0)
    ref_share = lax.dynamic_slice_in_dim(ref_factor, core * (ref_rows // cores), ref_rows // cores, 0)
    local_top = jnp.maximum(
        jnp.max(jnp.abs(dot_nt(cand_factor, ref_cols_moment) / w_ref[None, :])),
        jnp.max(jnp.abs(dot_nt(ref_share, cand_cols_moment) / w_cand[None, :])),
    )

    if cand_cols % refs == 0 and ref_cols % chips == 0:
        a, b = cand_cols // refs, ref_cols // chips
        cand_piece = lax.dynamic_slice_in_dim(cand_block, ref * a, a, 0)
        ref_piece = lax.dynamic_slice_in_dim(ref_block, chip * b, b, 0)
        piece = jnp.concatenate([cand_piece, ref_piece, jnp.broadcast_to(local_top, (8, half))], axis=0)
        got = share(piece, ("chip", "ref"), chips * refs).reshape(chips, refs, a + b + 8, half)
        cand_m = got[:, :, :a].reshape(rank, half)
        ref_m = jnp.swapaxes(got[:, :, a : a + b], 0, 1).reshape(rank, half)
        tops = got[:, :, a + b :, :]
    else:
        a, b = half // refs, half // chips
        cand_piece = lax.dynamic_slice_in_dim(cand_block, ref * a, a, 1).reshape(-1)
        ref_piece = lax.dynamic_slice_in_dim(ref_block, chip * b, b, 1).reshape(-1)
        piece = jnp.concatenate([cand_piece, ref_piece, local_top[None]])
        got = share(piece, ("chip", "ref"), chips * refs).reshape(chips, refs, -1)
        n = cand_piece.shape[0]
        cand_m = got[:, :, :n].reshape(chips, refs, cand_cols, a).transpose(0, 2, 1, 3).reshape(rank, half)
        ref_m = got[:, :, n:-1].reshape(chips, refs, ref_cols, b).transpose(1, 2, 0, 3).reshape(rank, half)
        tops = got[:, :, -1:]
    top_here = jnp.max(tops)
    both = whole_width(jnp.concatenate([cand_m, ref_m, jnp.broadcast_to(top_here, (8, half))], axis=0))
    cand_moment, ref_moment = both[:rank], both[rank : 2 * rank]
    global_top = jnp.max(both[2 * rank :])

    grad_weights = -jnp.sum(cand_moment * ref_moment, axis=1) / (weights * weights)
    top = jnp.maximum(global_top, jnp.max(jnp.abs(grad_weights))) + tiny_value
    kernel_weights = weights * jnp.exp(-step_size * grad_weights / top)
    kernel_cand = cand_plan * jnp.exp(-step_size * (dot_nt(cand_factor, ref_moment) / weights[None, :]) / top)
    kernel_ref = ref_plan * jnp.exp(-step_size * (dot_nt(ref_factor, cand_moment) / weights[None, :]) / top)

    cand_sub = cand_rows // refs
    ref_sub = ref_rows // (chips * cores)
    mine_cand = lax.dynamic_slice_in_dim(kernel_cand, ref * cand_sub, cand_sub, 0)
    mine_ref = lax.dynamic_slice_in_dim(kernel_ref, (chip * cores + core) * ref_sub, ref_sub, 0)
    scale_cand = jnp.ones((rank,), f32)
    scale_ref = jnp.ones((rank,), f32)
    for _ in range(ITERS):
        last_cand, last_ref = scale_cand, scale_ref
        row_cand = rank / jnp.sum(mine_cand * scale_cand[None, :], axis=1, keepdims=True)
        row_ref = rank / jnp.sum(mine_ref * scale_ref[None, :], axis=1, keepdims=True)
        part = jnp.stack(
            [jnp.sum(row_cand * mine_cand, axis=0) / cand_total, jnp.sum(row_ref * mine_ref, axis=0) / ref_total]
        )
        mass = jnp.sum(share(part, ("chip", "core", "ref"), chips * cores * refs), axis=0)
        mass_cand, mass_ref = mass[0], mass[1]
        new_weights = jnp.cbrt(kernel_weights * scale_cand * mass_cand * scale_ref * mass_ref)
        scale_cand = new_weights / mass_cand
        scale_ref = new_weights / mass_ref
    row_cand = rank / jnp.sum(kernel_cand * last_cand[None, :], axis=1, keepdims=True)
    row_ref = rank / jnp.sum(kernel_ref * last_ref[None, :], axis=1, keepdims=True)
    new_cand_plan = row_cand * kernel_cand * scale_cand[None, :]
    new_ref_plan = row_ref * kernel_ref * scale_ref[None, :]
    return (new_cand_plan, new_ref_plan, new_weights)


load_steps = 4
ref_order = [2, 3, 1]
chip_order = [1, 3, 2]
bf16 = jnp.bfloat16


def split(x):
    high = x.astype(bf16)
    return high, (x - high.astype(f32)).astype(bf16)


def mxu(left, right, dims):
    return lax.dot_general(left, right, (dims, ((), ())), preferred_element_type=f32)


def rows_by_cols(left, right):
    lh, ll = split(left)
    rh, rl = split(right)
    m, nn = left.shape[0], ((1,), (0,))
    tall = mxu(jnp.concatenate([lh, ll], axis=0), rh, nn)
    return tall[:m] + (tall[m:] + mxu(lh, rl, nn))


def rows_by_rows(left, right):
    n = right.shape[0]
    lh, ll = left
    rh, rl = split(right)
    nt = ((1,), (1,))
    wide = mxu(lh, jnp.concatenate([rh, rl], axis=0), nt)
    return wide[:, :n] + (wide[:, n:] + mxu(ll, rh, nt))


FAST = pl.BlockSpec(memory_space=pltpu.VMEM)
SLOW = pl.BlockSpec(memory_space=pltpu.HBM)


def call(body, outs, *args, scratch=(), slow=(), slow_outs=(), short_outs=(), room=4):
    args = [pltpu.with_memory_space_constraint(a, pltpu.HBM) if i in slow else a for i, a in enumerate(args)]
    return pl.pallas_call(
        body,
        out_shape=[
            pltpu.HBM(s, f32) if i in slow_outs else jax.ShapeDtypeStruct(s, bf16 if i in short_outs else f32)
            for i, s in enumerate(outs)
        ],
        in_specs=[SLOW if i in slow else FAST for i in range(len(args))],
        out_specs=[SLOW if i in slow_outs else FAST for i in range(len(outs))],
        scratch_shapes=[pltpu.VMEM(s, f32) if isinstance(s, tuple) else s for s in scratch],
        compiler_params=pltpu.CompilerParams(vmem_limit_bytes=room << 20),
    )(*args)


def copies(pairs, sems):
    made = [pltpu.make_async_copy(src, dst, sems.at[i]) for i, (src, dst) in enumerate(pairs)]
    for c in made:
        c.start()
    return made


def largest(x):
    return jnp.max(jnp.max(jnp.abs(x), axis=0, keepdims=True), axis=1, keepdims=True)


def cube_root(x):
    return jnp.exp(jnp.log(x) * (1.0 / 3.0))


def on_device_tiled(cand_factor, ref_factor, cand_plan, ref_plan, weights):
    chips, cores, refs = (lax.axis_size(a) for a in ("chip", "core", "ref"))
    cand_rows, width = cand_factor.shape
    ref_rows = ref_factor.shape[0]
    rank = weights.shape[0]
    cand_total = cand_rows * chips * cores
    ref_total = ref_rows * refs
    half = width // cores
    ca, ra = rank // chips, rank // refs
    cb, rb = ca // refs, ra // chips
    lanes = half // 128
    block_rows = lanes * ca
    few = -(-block_rows // (refs + 1))
    last = few * (refs - 1)
    tall_piece = 2 * few + 1
    cand_sub = cand_rows // refs
    ref_sub = ref_rows // (chips * cores)
    everyone = chips * cores * refs
    pairs = partner_lists(refs)
    xor = refs & (refs - 1) == 0
    weights_row = weights[None, :]

    steps = load_steps
    step = cand_rows // steps
    dma = pltpu.SemaphoreType.DMA

    share_rows = ref_rows // cores

    def cand_parts(cand_hbm, cand_plan_hbm, keep, send, cand_high, cand_low, cand, cand_plan, sems):
        core = lax.axis_index("core")
        loads = copies(
            [(cand_plan_hbm, cand_plan)]
            + [(cand_hbm.at[pl.ds(i * step, step)], cand.at[pl.ds(i * step, step)]) for i in range(steps)],
            sems,
        )
        loads[0].wait()
        plan = jnp.concatenate(split(cand_plan[...].T), axis=0)
        nn = ((1,), (0,))
        total = None
        for i in range(steps):
            loads[1 + i].wait()
            rows = slice(i * step, (i + 1) * step)
            high, low = split(cand[rows, :])
            cand_high[rows, :], cand_low[rows, :] = high, low
            tall = mxu(plan[:, rows], high, nn)
            part = tall[:rank] + (tall[rank:] + mxu(plan[:rank, rows], low, nn))
            total = part if total is None else total + part
        total = total / cand_total
        keep[...] = jnp.where(core == 0, total[:, :half], total[:, half:])
        send[...] = jnp.where(core == 0, total[:, half:], total[:, :half])

    keep, send, cand_high, cand_low = call(
        cand_parts,
        [(rank, half)] * 2 + [(cand_rows, width)] * 2,
        cand_factor, cand_plan,
        scratch=[(cand_rows, width), (cand_rows, rank), dma((steps + 1,))],
        slow=(0, 1),
        short_outs=(2, 3),
        room=16,
    )
    came = swap_core(send, cores)

    def ref_parts(ref_in, ref_plan_in, share_high, share_low, *rest):
        blocks, whole = rest[:refs], rest[refs]
        core, ref = lax.axis_index("core"), lax.axis_index("ref")
        here = ref_in[:, pl.ds(pl.multiple_of(core * half, half), half)]
        whole[...] = rows_by_cols(ref_plan_in[...].T, here) / ref_total
        for k in range(refs):
            to = ref ^ k if xor else (ref + k) % refs
            blocks[k][...] = whole[pl.ds(pl.multiple_of(to * ra, ra), ra), :]
        share = ref_in[pl.ds(pl.multiple_of(core * share_rows, share_rows), share_rows), :]
        share_high[...], share_low[...] = split(share)

    share_high, share_low, *blocks = call(
        ref_parts,
        [(share_rows, width)] * 2 + [(ra, half)] * refs,
        ref_factor, ref_plan,
        scratch=[(rank, half)],
        short_outs=(0, 1),
        room=8,
    )
    order = ref_order if refs == 4 else list(range(1, refs))
    blocks = [blocks[0]] + [lax.ppermute(blocks[k], "ref", pairs[k - 1]) for k in order]

    def chip_blocks(keep_ref, came_ref, *rest):
        outs, full = rest[:-1], rest[-1]
        chip = lax.axis_index("chip")
        full[...] = keep_ref[...] + came_ref[...]
        for k in range(chips):
            outs[k][...] = full[pl.ds(pl.multiple_of((chip ^ k) * ca, ca), ca), :]

    cand_blocks = call(chip_blocks, [(ca, half)] * chips, keep, came, scratch=[(rank, half)])
    chip_pairs = partner_lists(chips)
    cand_blocks = [cand_blocks[0]] + [
        lax.ppermute(cand_blocks[k], "chip", chip_pairs[k - 1]) for k in (chip_order if chips == 4 else range(1, chips))
    ]

    def own_blocks(*rest):
        out = rest[-1]
        for start, count, terms in ((0, ca, rest[:chips]), (ca, ra, rest[chips:-1])):
            total = terms[0][...]
            for term in terms[1:]:
                total = total + term[...]
            out[start : start + count, :] = total

    (mine,) = call(own_blocks, [(ca + ra, half)], *cand_blocks, *blocks)
    other = swap_core(mine, cores)

    def columns_at(moment, at, columns, padded):
        padded[...] = jnp.zeros_like(padded)
        padded[pl.ds(pl.multiple_of(at * columns, columns), columns), :] = moment
        return padded[...]

    def own_lanes(factor, core):
        return factor[:, pl.ds(pl.multiple_of(core * half, half), half)]

    def half_columns(mine_ref, cand_high, cand_low, share_high, share_low, cand_out, share_out, padded):
        chip, core, ref = (lax.axis_index(a) for a in ("chip", "core", "ref"))
        moment = columns_at(mine_ref[ca:, :], ref, ra, padded)
        cand_out[...] = rows_by_rows((own_lanes(cand_high, core), own_lanes(cand_low, core)), moment)
        moment = columns_at(mine_ref[:ca, :], chip, ca, padded)
        share_out[...] = rows_by_rows((own_lanes(share_high, core), own_lanes(share_low, core)), moment)

    cand_cols_part, share_cols_part = call(
        half_columns,
        [(cand_rows, rank), (share_rows, rank)],
        mine, cand_high, cand_low, share_high, share_low,
        scratch=[(rank, half)],
        room=12,
    )

    def column_tops(
        mine_ref, other_ref, cand_high, cand_low, share_high, share_low, cand_part, share_part, w_ref, out, padded, rows
    ):
        chip, core, ref = (lax.axis_index(a) for a in ("chip", "core", "ref"))
        w = w_ref[...]
        moment = columns_at(other_ref[ca:, :], ref, ra, padded)
        factor = (own_lanes(cand_high, 1 - core), own_lanes(cand_low, 1 - core))
        grad_cand = cand_part[...] + rows_by_rows(factor, moment)
        moment = columns_at(other_ref[:ca, :], chip, ca, padded)
        factor = (own_lanes(share_high, 1 - core), own_lanes(share_low, 1 - core))
        grad_ref = share_part[...] + rows_by_rows(factor, moment)
        tall = jnp.maximum(
            jnp.max(jnp.abs(grad_cand), axis=0, keepdims=True), jnp.max(jnp.abs(grad_ref), axis=0, keepdims=True)
        )
        for lane in range(lanes):
            at = slice(lane * 128, (lane + 1) * 128)
            rows[lane * ca : (lane + 1) * ca, :] = mine_ref[:ca, at]
            rows[block_rows + lane * ra : block_rows + (lane + 1) * ra, :] = mine_ref[ca:, at]
        top = tall / w
        for e in range(chips):
            for d in range(refs):
                to = lax.rem(chip + chips - e, chips) * refs + lax.rem(ref + refs - d, refs)
                if e and d:
                    part = [rows[few * (d - 1) : few * d, :]]
                    part += [rows[block_rows + few * (e - 1) : block_rows + few * e, :]]
                elif e:
                    part = [rows[last:block_rows, :]]
                else:
                    part = [rows[block_rows + last : 2 * block_rows, :]]
                short = 2 * few - sum(p.shape[0] for p in part)
                part += [jnp.zeros((short, rank), f32)] if short else []
                out[pl.ds(to * tall_piece, tall_piece), :] = jnp.concatenate(part + [top], axis=0)

    (to_all,) = call(
        column_tops,
        [(chips * refs * tall_piece, 128)],
        mine,
        other,
        cand_high,
        cand_low,
        share_high,
        share_low,
        cand_cols_part,
        share_cols_part,
        weights_row,
        scratch=[(rank, half), (2 * block_rows, 128)],
        room=12,
    )
    to_all = to_all.reshape(chips * refs, tall_piece, 1, 128)
    got = lax.all_to_all(to_all, ("chip", "ref"), 0, 0).reshape(-1, 128)
    got_other = swap_core(got, cores)

    def mass_part(kernel_cand, kernel_ref, scale_cand, scale_ref, out):
        row_cand = rank / jnp.sum(kernel_cand * scale_cand, axis=1, keepdims=True)
        row_ref = rank / jnp.sum(kernel_ref * scale_ref, axis=1, keepdims=True)
        mass_cand = jnp.sum(row_cand * kernel_cand, axis=0, keepdims=True) / cand_total
        mass_ref = jnp.sum(row_ref * kernel_ref, axis=0, keepdims=True) / ref_total
        both = jnp.concatenate([mass_cand, mass_ref], axis=0)
        out[...] = jnp.broadcast_to(both[None], (everyone, 2, rank))

    def assemble(pieces_ref, own_ref, cand_half, ref_half, rows):
        chip, ref = lax.axis_index("chip"), lax.axis_index("ref")

        def piece(e, d, start, count):
            at = lax.rem(chip + e, chips) * refs + lax.rem(ref + d, refs)
            return pieces_ref[pl.ds(at * tall_piece + start, count), :]

        def spread(half_ref, at, columns):
            at = pl.ds(pl.multiple_of(at * columns, columns), columns)
            for lane in range(lanes):
                half_ref[at, lane * 128 : (lane + 1) * 128] = rows[lane * columns : (lane + 1) * columns, :]

        cand_half[pl.ds(pl.multiple_of(chip * ca, ca), ca), :] = own_ref[:ca, :]
        ref_half[pl.ds(pl.multiple_of(ref * ra, ra), ra), :] = own_ref[ca:, :]
        for e in range(1, chips):
            rows[last:, :] = piece(e, 0, 0, block_rows - last)
            for d in range(1, refs):
                rows[few * (d - 1) : few * d, :] = piece(e, d, 0, few)
            spread(cand_half, lax.rem(chip + e, chips), ca)
        for d in range(1, refs):
            rows[last:, :] = piece(0, d, 0, block_rows - last)
            for e in range(1, chips):
                rows[few * (e - 1) : few * e, :] = piece(e, d, few, few)
            spread(ref_half, lax.rem(ref + d, refs), ra)
        tops = pieces_ref[tall_piece - 1 : tall_piece, :]
        for i in range(1, chips * refs):
            tops = jnp.maximum(tops, pieces_ref[(i + 1) * tall_piece - 1 : (i + 1) * tall_piece, :])
        product = cand_half[...] * ref_half[...]
        folded = product[:, :128]
        for lane in range(1, lanes):
            folded = folded + product[:, lane * 128 : (lane + 1) * 128]
        return tops, jnp.sum(folded.T, axis=0, keepdims=True)

    def half_kernels(
        got_ref, own_ref, cand_high, cand_low, share_high, share_low,
        cand_half, cand_out, share_out, rows_out, ref_half, rows,
    ):
        chip, core = lax.axis_index("chip"), lax.axis_index("core")
        tops, inner = assemble(got_ref, own_ref, cand_half, ref_half, rows)
        rows_out[0:1, :] = tops
        rows_out[1:2, :] = inner
        cand_out[...] = rows_by_rows((own_lanes(cand_high, core), own_lanes(cand_low, core)), ref_half[...])
        at = pl.ds(pl.multiple_of(chip * ref_sub, ref_sub), ref_sub)
        lane = pl.ds(pl.multiple_of(core * half, half), half)
        share_out[...] = rows_by_rows((share_high[at, lane], share_low[at, lane]), cand_half[...])

    cand_half, cand_part, share_part, rows_part = call(
        half_kernels,
        [(rank, half), (cand_rows, rank), (ref_sub, rank), (8, rank)],
        got, mine, cand_high, cand_low, share_high, share_low,
        scratch=[(rank, half), (block_rows, 128)],
        room=12,
    )

    def first_kernels(
        got_ref, own_ref, cand_high, cand_low, cand_plan_ref, share_high, share_low, ref_plan_ref, w_ref,
        cand_half, cand_part, share_part, rows_part,
        cand_moment, full_cand, state, sub_cand, sub_ref, out, other_half, ref_half, rows,
    ):
        chip, core, ref = (lax.axis_index(a) for a in ("chip", "core", "ref"))
        tops, inner = assemble(got_ref, own_ref, other_half, ref_half, rows)
        tops = jnp.maximum(tops, rows_part[0:1, :])
        cand_moment[:, :half] = jnp.where(core == 0, cand_half[...], other_half[...])
        cand_moment[:, half:] = jnp.where(core == 0, other_half[...], cand_half[...])
        w = w_ref[...]
        grad_weights = -(inner + rows_part[1:2, :]) / (w * w)
        top = jnp.maximum(jnp.max(tops, axis=1, keepdims=True), largest(grad_weights)) + tiny_value
        kernel_weights = w * jnp.exp(-step_size * grad_weights / top)
        state[0:1, :] = kernel_weights
        state[1:2, :] = jnp.broadcast_to(top, (1, rank))
        state[2:8, :] = jnp.ones((6, rank), f32)
        factor = (own_lanes(cand_high, 1 - core), own_lanes(cand_low, 1 - core))
        grad = (cand_part[...] + rows_by_rows(factor, ref_half[...])) / w
        full_cand[...] = cand_plan_ref[...] * jnp.exp(-step_size * grad / top)
        kernel_cand = full_cand[pl.ds(pl.multiple_of(ref * cand_sub, cand_sub), cand_sub), :]
        at = pl.ds(pl.multiple_of(chip * ref_sub, ref_sub), ref_sub)
        lane = pl.ds(pl.multiple_of((1 - core) * half, half), half)
        grad = (share_part[...] + rows_by_rows((share_high[at, lane], share_low[at, lane]), other_half[...])) / w
        at = pl.ds(pl.multiple_of(core * share_rows + chip * ref_sub, ref_sub), ref_sub)
        kernel_ref = ref_plan_ref[at, :] * jnp.exp(-step_size * grad / top)
        sub_cand[...] = kernel_cand
        sub_ref[...] = kernel_ref
        ones = jnp.ones((1, rank), f32)
        mass_part(kernel_cand, kernel_ref, ones, ones, out)

    cand_moment, full_cand, state, sub_cand, sub_ref, out = call(
        first_kernels,
        [(rank, width), (cand_rows, rank), (8, rank), (cand_sub, rank), (ref_sub, rank), (everyone, 2, rank)],
        got_other, other, cand_high, cand_low, cand_plan, share_high, share_low, ref_plan, weights_row,
        cand_half, cand_part, share_part, rows_part,
        scratch=[(rank, half), (rank, half), (block_rows, 128)],
        room=12,
    )

    def update(mass_ref, state):
        mass = jnp.sum(mass_ref[...], axis=0)
        mass_cand, mass_ref = mass[0:1], mass[1:2]
        kernel_weights, scale_cand, scale_ref = state[0:1, :], state[2:3, :], state[3:4, :]
        new_weights = cube_root(kernel_weights * scale_cand * mass_cand * scale_ref * mass_ref)
        return new_weights, new_weights / mass_cand, new_weights / mass_ref

    def next_masses(mass_ref, state_ref, sub_cand_ref, sub_ref_ref, new_state, out):
        _, scale_cand, scale_ref = update(mass_ref, state_ref)
        new_state[...] = state_ref[...]
        new_state[2:3, :] = scale_cand
        new_state[3:4, :] = scale_ref
        mass_part(sub_cand_ref[...], sub_ref_ref[...], scale_cand, scale_ref, out)

    for _ in range(ITERS - 1):
        mass = lax.all_to_all(out, ("chip", "core", "ref"), 0, 0)
        state, out = call(next_masses, [(8, rank), (everyone, 2, rank)], mass, state, sub_cand, sub_ref)
    mass = lax.all_to_all(out, ("chip", "core", "ref"), 0, 0)

    def finish(
        mass_ref, cand_moment, state_ref, full_cand, ref_ref, ref_plan_ref, w_ref,
        cand_out, ref_out, w_out, cand_done, ref_done, w_done, sems,
    ):
        new_weights, scale_cand, scale_ref = update(mass_ref, state_ref)
        top = state_ref[1:2, :]
        kernel = full_cand[...]
        row = rank / jnp.sum(kernel * state_ref[2:3, :], axis=1, keepdims=True)
        cand_done[...] = row * kernel * scale_cand
        stores = [pltpu.make_async_copy(cand_done, cand_out, sems.at[0])]
        stores[0].start()
        w_done[...] = new_weights
        stores += [pltpu.make_async_copy(w_done, w_out, sems.at[1])]
        stores[1].start()
        grad = rows_by_rows(split(ref_ref[...]), cand_moment[...]) / w_ref[...]
        kernel = ref_plan_ref[...] * jnp.exp(-step_size * grad / top)
        row = rank / jnp.sum(kernel * state_ref[3:4, :], axis=1, keepdims=True)
        ref_done[...] = row * kernel * scale_ref
        stores += [pltpu.make_async_copy(ref_done, ref_out, sems.at[2])]
        stores[2].start()
        for c in stores:
            c.wait()

    new_cand_plan, new_ref_plan, new_weights = call(
        finish,
        [(cand_rows, rank), (ref_rows, rank), (1, rank)],
        mass, cand_moment, state, full_cand, ref_factor, ref_plan, weights_row,
        scratch=[(cand_rows, rank), (ref_rows, rank), (1, rank), dma((3,))],
        slow_outs=(0, 1, 2),
        room=8,
    )
    return new_cand_plan, new_ref_plan, new_weights.reshape(rank)


def on_device(*args):
    chips, cores, refs = (lax.axis_size(a) for a in ("chip", "core", "ref"))
    rank, width = args[4].shape[0], args[0].shape[1]
    rows = (args[0].shape[0] // refs, args[1].shape[0] // (chips * cores))
    tiled = cores == 2 and chips == refs and rank == 128 and rank % (8 * chips * refs) == 0 and width % (128 * cores) == 0
    tiled = tiled and all(n % 8 == 0 for n in rows)
    return (on_device_tiled if tiled else on_device_any)(*args)


def solution(mesh):
    cand, ref = mesh.shape["cand"], mesh.shape["ref"]
    cores = 2 if cand % 2 == 0 else 1
    finer = Mesh(mesh.devices.reshape(cand // cores, cores, ref), ("chip", "core", "ref"))
    rows = ("chip", "core")
    in_specs = (P(rows, None), P("ref", None), P(rows, None), P("ref", None), P())
    out_specs = (P(rows, None), P("ref", None), P())
    return jax.shard_map(on_device, mesh=finer, in_specs=in_specs, out_specs=out_specs, check_vma=False)
```

```python
import jax
import jax.numpy as jnp
from jax import lax
from jax.experimental import pallas as pl
from jax.experimental.pallas import tpu as pltpu
from jax.sharding import Mesh, PartitionSpec as P

ITERS = 3

step_size = 3.0
tiny_value = 1e-06

HIGH = lax.Precision.HIGH
f32 = jnp.float32


def dot_nt(left, right):
    return lax.dot_general(
        left, right, (((1,), (1,)), ((), ())), precision=HIGH, preferred_element_type=f32
    )


def dot_tn(left, right):
    return lax.dot_general(
        left, right, (((0,), (0,)), ((), ())), precision=HIGH, preferred_element_type=f32
    )


def partner_lists(count):
    if count & (count - 1) == 0:
        return [[(i, i ^ k) for i in range(count)] for k in range(1, count)]
    return [[(i, (i + k) % count) for i in range(count)] for k in range(1, count)]


def swap_core(array, core_count):
    if core_count == 1:
        return None
    return lax.ppermute(array, "core", [(0, 1), (1, 0)])


def share(array, axes, count):
    pieces = jnp.broadcast_to(array[None], (count,) + array.shape)
    return lax.all_to_all(pieces, axes, 0, 0)


def on_device_any(cand_factor, ref_factor, cand_plan, ref_plan, weights):
    chips, cores, refs = (lax.axis_size(a) for a in ("chip", "core", "ref"))
    chip, core, ref = (lax.axis_index(a) for a in ("chip", "core", "ref"))
    cand_rows, width = cand_factor.shape
    ref_rows = ref_factor.shape[0]
    rank = weights.shape[0]
    cand_total = cand_rows * chips * cores
    ref_total = ref_rows * refs
    half = width // cores
    cand_cols, ref_cols = rank // chips, rank // refs

    ref_half = lax.dynamic_slice_in_dim(ref_factor, core * half, half, 1)
    ref_part = dot_tn(ref_plan, ref_half) / ref_total
    blocks = ref_part.reshape(refs, ref_cols, half)
    ref_block = lax.dynamic_index_in_dim(blocks, ref, 0, False)
    arrived = []
    for pairs in partner_lists(refs):
        goes_to = jnp.array([b for _, b in pairs], jnp.int32)[ref]
        arrived.append(lax.ppermute(lax.dynamic_index_in_dim(blocks, goes_to, 0, False), "ref", pairs))

    cand_part = dot_tn(cand_plan, cand_factor) / cand_total
    mine = lax.dynamic_slice_in_dim(cand_part, core * half, half, 1)
    if cores > 1:
        mine = mine + swap_core(lax.dynamic_slice_in_dim(cand_part, (1 - core) * half, half, 1), cores)
    pieces = lax.all_to_all(mine.reshape(chips, cand_cols, half), "chip", 0, 0)
    cand_block = jnp.sum(pieces, axis=0)
    for piece in arrived:
        ref_block = ref_block + piece

    def whole_width(part):
        if cores == 1:
            return part
        other = swap_core(part, cores)
        low = jnp.where(core == 0, part, other)
        high = jnp.where(core == 0, other, part)
        return jnp.concatenate([low, high], axis=-1)

    both = whole_width(jnp.concatenate([cand_block, ref_block], axis=0))
    cand_cols_moment, ref_cols_moment = both[:cand_cols], both[cand_cols:]
    w_ref = lax.dynamic_slice_in_dim(weights, ref * ref_cols, ref_cols, 0)
    w_cand = lax.dynamic_slice_in_dim(weights, chip * cand_cols, cand_cols, 0)
    ref_share = lax.dynamic_slice_in_dim(ref_factor, core * (ref_rows // cores), ref_rows // cores, 0)
    local_top = jnp.maximum(
        jnp.max(jnp.abs(dot_nt(cand_factor, ref_cols_moment) / w_ref[None, :])),
        jnp.max(jnp.abs(dot_nt(ref_share, cand_cols_moment) / w_cand[None, :])),
    )

    if cand_cols % refs == 0 and ref_cols % chips == 0:
        a, b = cand_cols // refs, ref_cols // chips
        cand_piece = lax.dynamic_slice_in_dim(cand_block, ref * a, a, 0)
        ref_piece = lax.dynamic_slice_in_dim(ref_block, chip * b, b, 0)
        piece = jnp.concatenate([cand_piece, ref_piece, jnp.broadcast_to(local_top, (8, half))], axis=0)
        got = share(piece, ("chip", "ref"), chips * refs).reshape(chips, refs, a + b + 8, half)
        cand_m = got[:, :, :a].reshape(rank, half)
        ref_m = jnp.swapaxes(got[:, :, a : a + b], 0, 1).reshape(rank, half)
        tops = got[:, :, a + b :, :]
    else:
        a, b = half // refs, half // chips
        cand_piece = lax.dynamic_slice_in_dim(cand_block, ref * a, a, 1).reshape(-1)
        ref_piece = lax.dynamic_slice_in_dim(ref_block, chip * b, b, 1).reshape(-1)
        piece = jnp.concatenate([cand_piece, ref_piece, local_top[None]])
        got = share(piece, ("chip", "ref"), chips * refs).reshape(chips, refs, -1)
        n = cand_piece.shape[0]
        cand_m = got[:, :, :n].reshape(chips, refs, cand_cols, a).transpose(0, 2, 1, 3).reshape(rank, half)
        ref_m = got[:, :, n:-1].reshape(chips, refs, ref_cols, b).transpose(1, 2, 0, 3).reshape(rank, half)
        tops = got[:, :, -1:]
    top_here = jnp.max(tops)
    both = whole_width(jnp.concatenate([cand_m, ref_m, jnp.broadcast_to(top_here, (8, half))], axis=0))
    cand_moment, ref_moment = both[:rank], both[rank : 2 * rank]
    global_top = jnp.max(both[2 * rank :])

    grad_weights = -jnp.sum(cand_moment * ref_moment, axis=1) / (weights * weights)
    top = jnp.maximum(global_top, jnp.max(jnp.abs(grad_weights))) + tiny_value
    kernel_weights = weights * jnp.exp(-step_size * grad_weights / top)
    kernel_cand = cand_plan * jnp.exp(-step_size * (dot_nt(cand_factor, ref_moment) / weights[None, :]) / top)
    kernel_ref = ref_plan * jnp.exp(-step_size * (dot_nt(ref_factor, cand_moment) / weights[None, :]) / top)

    cand_sub = cand_rows // refs
    ref_sub = ref_rows // (chips * cores)
    mine_cand = lax.dynamic_slice_in_dim(kernel_cand, ref * cand_sub, cand_sub, 0)
    mine_ref = lax.dynamic_slice_in_dim(kernel_ref, (chip * cores + core) * ref_sub, ref_sub, 0)
    scale_cand = jnp.ones((rank,), f32)
    scale_ref = jnp.ones((rank,), f32)
    for _ in range(ITERS):
        last_cand, last_ref = scale_cand, scale_ref
        row_cand = rank / jnp.sum(mine_cand * scale_cand[None, :], axis=1, keepdims=True)
        row_ref = rank / jnp.sum(mine_ref * scale_ref[None, :], axis=1, keepdims=True)
        part = jnp.stack(
            [jnp.sum(row_cand * mine_cand, axis=0) / cand_total, jnp.sum(row_ref * mine_ref, axis=0) / ref_total]
        )
        mass = jnp.sum(share(part, ("chip", "core", "ref"), chips * cores * refs), axis=0)
        mass_cand, mass_ref = mass[0], mass[1]
        new_weights = jnp.cbrt(kernel_weights * scale_cand * mass_cand * scale_ref * mass_ref)
        scale_cand = new_weights / mass_cand
        scale_ref = new_weights / mass_ref
    row_cand = rank / jnp.sum(kernel_cand * last_cand[None, :], axis=1, keepdims=True)
    row_ref = rank / jnp.sum(kernel_ref * last_ref[None, :], axis=1, keepdims=True)
    new_cand_plan = row_cand * kernel_cand * scale_cand[None, :]
    new_ref_plan = row_ref * kernel_ref * scale_ref[None, :]
    return (new_cand_plan, new_ref_plan, new_weights)


load_steps = 4
ref_orders = ([2, 3, 1], [3, 1, 2])
chip_orders = ([3, 2, 1], [1, 3, 2])
bf16 = jnp.bfloat16


def split(x):
    high = x.astype(bf16)
    return high, (x - high.astype(f32)).astype(bf16)


def mxu(left, right, dims):
    return lax.dot_general(left, right, (dims, ((), ())), preferred_element_type=f32)


def rows_by_cols(left, right):
    lh, ll = split(left)
    rh, rl = split(right)
    m, nn = left.shape[0], ((1,), (0,))
    tall = mxu(jnp.concatenate([lh, ll], axis=0), rh, nn)
    return tall[:m] + (tall[m:] + mxu(lh, rl, nn))


def rows_by_rows(left, right):
    n = right.shape[0]
    lh, ll = left
    rh, rl = split(right)
    nt = ((1,), (1,))
    wide = mxu(lh, jnp.concatenate([rh, rl], axis=0), nt)
    return wide[:, :n] + (wide[:, n:] + mxu(ll, rh, nt))


FAST = pl.BlockSpec(memory_space=pltpu.VMEM)
SLOW = pl.BlockSpec(memory_space=pltpu.HBM)


def call(body, outs, *args, scratch=(), slow=(), slow_outs=(), short_outs=(), room=4):
    args = [pltpu.with_memory_space_constraint(a, pltpu.HBM) if i in slow else a for i, a in enumerate(args)]
    return pl.pallas_call(
        body,
        out_shape=[
            pltpu.HBM(s, f32) if i in slow_outs else jax.ShapeDtypeStruct(s, bf16 if i in short_outs else f32)
            for i, s in enumerate(outs)
        ],
        in_specs=[SLOW if i in slow else FAST for i in range(len(args))],
        out_specs=[SLOW if i in slow_outs else FAST for i in range(len(outs))],
        scratch_shapes=[pltpu.VMEM(s, f32) if isinstance(s, tuple) else s for s in scratch],
        compiler_params=pltpu.CompilerParams(vmem_limit_bytes=room << 20),
    )(*args)


def copies(pairs, sems):
    made = [pltpu.make_async_copy(src, dst, sems.at[i]) for i, (src, dst) in enumerate(pairs)]
    for c in made:
        c.start()
    return made


def largest(x):
    return jnp.max(jnp.max(jnp.abs(x), axis=0, keepdims=True), axis=1, keepdims=True)


def cube_root(x):
    return jnp.exp(jnp.log(x) * (1.0 / 3.0))


def on_device_tiled(cand_factor, ref_factor, cand_plan, ref_plan, weights):
    chips, cores, refs = (lax.axis_size(a) for a in ("chip", "core", "ref"))
    cand_rows, width = cand_factor.shape
    ref_rows = ref_factor.shape[0]
    rank = weights.shape[0]
    cand_total = cand_rows * chips * cores
    ref_total = ref_rows * refs
    half = width // cores
    ca, ra = rank // chips, rank // refs
    lanes = half // 128
    block_rows = lanes * ca
    few = -(-block_rows // (refs + 1))
    last = few * (refs - 1)
    tall_piece = 2 * few + 1
    cand_sub = cand_rows // refs
    ref_sub = ref_rows // (chips * cores)
    everyone = chips * cores * refs
    ref_steps = [[0] + (ref_orders[c] if refs == 4 else list(range(1, refs))) for c in range(cores)]
    chip_steps = [[0] + (chip_orders[c] if chips == 4 else list(range(1, chips))) for c in range(cores)]

    def step_at(steps_of, k, core):
        first, second = steps_of[0][k], steps_of[1][k]
        return first if first == second else jnp.where(core == 0, first, second)

    weights_row = weights[None, :]

    steps = load_steps
    step = cand_rows // steps
    dma = pltpu.SemaphoreType.DMA

    share_rows = ref_rows // cores

    def cand_parts(cand_hbm, cand_plan_hbm, keep, send, cand_high, cand_low, cand, cand_plan, sems):
        core = lax.axis_index("core")
        loads = copies(
            [(cand_plan_hbm, cand_plan)]
            + [(cand_hbm.at[pl.ds(i * step, step)], cand.at[pl.ds(i * step, step)]) for i in range(steps)],
            sems,
        )
        loads[0].wait()
        plan = jnp.concatenate(split(cand_plan[...].T), axis=0)
        nn = ((1,), (0,))
        total = None
        for i in range(steps):
            loads[1 + i].wait()
            rows = slice(i * step, (i + 1) * step)
            high, low = split(cand[rows, :])
            cand_high[rows, :], cand_low[rows, :] = high, low
            tall = mxu(plan[:, rows], high, nn)
            part = tall[:rank] + (tall[rank:] + mxu(plan[:rank, rows], low, nn))
            total = part if total is None else total + part
        total = total / cand_total
        keep[...] = jnp.where(core == 0, total[:, :half], total[:, half:])
        send[...] = jnp.where(core == 0, total[:, half:], total[:, :half])

    keep, send, cand_high, cand_low = call(
        cand_parts,
        [(rank, half)] * 2 + [(cand_rows, width)] * 2,
        cand_factor, cand_plan,
        scratch=[(cand_rows, width), (cand_rows, rank), dma((steps + 1,))],
        slow=(0, 1),
        short_outs=(2, 3),
        room=16,
    )
    came = swap_core(send, cores)

    def ref_parts(ref_in, ref_plan_in, share_high, share_low, *rest):
        blocks, whole = rest[:refs], rest[refs]
        core, ref = lax.axis_index("core"), lax.axis_index("ref")
        here = ref_in[:, pl.ds(pl.multiple_of(core * half, half), half)]
        whole[...] = rows_by_cols(ref_plan_in[...].T, here) / ref_total
        for k in range(refs):
            to = ref ^ step_at(ref_steps, k, core)
            blocks[k][...] = whole[pl.ds(pl.multiple_of(to * ra, ra), ra), :]
        share = ref_in[pl.ds(pl.multiple_of(core * share_rows, share_rows), share_rows), :]
        share_high[...], share_low[...] = split(share)

    share_high, share_low, *blocks = call(
        ref_parts,
        [(share_rows, width)] * 2 + [(ra, half)] * refs,
        ref_factor, ref_plan,
        scratch=[(rank, half)],
        short_outs=(0, 1),
        room=8,
    )
    blocks = [blocks[0]] + [
        lax.ppermute(
            blocks[k],
            ("core", "ref"),
            [(c * refs + i, c * refs + (i ^ ref_steps[c][k])) for c in range(cores) for i in range(refs)],
        )
        for k in range(1, refs)
    ]

    def chip_blocks(keep_ref, came_ref, *rest):
        outs, full = rest[:-1], rest[-1]
        chip, core = lax.axis_index("chip"), lax.axis_index("core")
        full[...] = keep_ref[...] + came_ref[...]
        for k in range(chips):
            to = chip ^ step_at(chip_steps, k, core)
            outs[k][...] = full[pl.ds(pl.multiple_of(to * ca, ca), ca), :]

    cand_blocks = call(chip_blocks, [(ca, half)] * chips, keep, came, scratch=[(rank, half)])
    cand_blocks = [cand_blocks[0]] + [
        lax.ppermute(
            cand_blocks[k],
            ("chip", "core"),
            [(i * cores + c, (i ^ chip_steps[c][k]) * cores + c) for c in range(cores) for i in range(chips)],
        )
        for k in range(1, chips)
    ]

    def own_blocks(*rest):
        out = rest[-1]
        for start, count, terms in ((0, ca, rest[:chips]), (ca, ra, rest[chips:-1])):
            total = terms[0][...]
            for term in terms[1:]:
                total = total + term[...]
            out[start : start + count, :] = total

    (mine,) = call(own_blocks, [(ca + ra, half)], *cand_blocks, *blocks)
    other = swap_core(mine, cores)

    def columns_at(moment, at, columns, padded):
        padded[...] = jnp.zeros_like(padded)
        padded[pl.ds(pl.multiple_of(at * columns, columns), columns), :] = moment
        return padded[...]

    def own_lanes(factor, core):
        return factor[:, pl.ds(pl.multiple_of(core * half, half), half)]

    def half_columns(mine_ref, cand_high, cand_low, share_high, share_low, cand_out, share_out, padded):
        chip, core, ref = (lax.axis_index(a) for a in ("chip", "core", "ref"))
        moment = columns_at(mine_ref[ca:, :], ref, ra, padded)
        cand_out[...] = rows_by_rows((own_lanes(cand_high, core), own_lanes(cand_low, core)), moment)
        moment = columns_at(mine_ref[:ca, :], chip, ca, padded)
        share_out[...] = rows_by_rows((own_lanes(share_high, core), own_lanes(share_low, core)), moment)

    cand_cols_part, share_cols_part = call(
        half_columns,
        [(cand_rows, rank), (share_rows, rank)],
        mine, cand_high, cand_low, share_high, share_low,
        scratch=[(rank, half)],
        room=12,
    )

    def column_tops(
        mine_ref, other_ref, cand_high, cand_low, share_high, share_low, cand_part, share_part, w_ref, out, padded, rows
    ):
        chip, core, ref = (lax.axis_index(a) for a in ("chip", "core", "ref"))
        w = w_ref[...]
        moment = columns_at(other_ref[ca:, :], ref, ra, padded)
        factor = (own_lanes(cand_high, 1 - core), own_lanes(cand_low, 1 - core))
        grad_cand = cand_part[...] + rows_by_rows(factor, moment)
        moment = columns_at(other_ref[:ca, :], chip, ca, padded)
        factor = (own_lanes(share_high, 1 - core), own_lanes(share_low, 1 - core))
        grad_ref = share_part[...] + rows_by_rows(factor, moment)
        tall = jnp.maximum(
            jnp.max(jnp.abs(grad_cand), axis=0, keepdims=True), jnp.max(jnp.abs(grad_ref), axis=0, keepdims=True)
        )
        for lane in range(lanes):
            at = slice(lane * 128, (lane + 1) * 128)
            rows[lane * ca : (lane + 1) * ca, :] = mine_ref[:ca, at]
            rows[block_rows + lane * ra : block_rows + (lane + 1) * ra, :] = mine_ref[ca:, at]
        top = tall / w
        for e in range(chips):
            for d in range(refs):
                to = lax.rem(chip + chips - e, chips) * refs + lax.rem(ref + refs - d, refs)
                if e and d:
                    part = [rows[few * (d - 1) : few * d, :]]
                    part += [rows[block_rows + few * (e - 1) : block_rows + few * e, :]]
                elif e:
                    part = [rows[last:block_rows, :]]
                else:
                    part = [rows[block_rows + last : 2 * block_rows, :]]
                short = 2 * few - sum(p.shape[0] for p in part)
                part += [jnp.zeros((short, rank), f32)] if short else []
                out[pl.ds(to * tall_piece, tall_piece), :] = jnp.concatenate(part + [top], axis=0)

    (to_all,) = call(
        column_tops,
        [(chips * refs * tall_piece, 128)],
        mine,
        other,
        cand_high,
        cand_low,
        share_high,
        share_low,
        cand_cols_part,
        share_cols_part,
        weights_row,
        scratch=[(rank, half), (2 * block_rows, 128)],
        room=12,
    )
    to_all = to_all.reshape(chips * refs, tall_piece, 1, 128)
    got = lax.all_to_all(to_all, ("chip", "ref"), 0, 0).reshape(-1, 128)
    got_other = swap_core(got, cores)

    def mass_part(kernel_cand, kernel_ref, scale_cand, scale_ref, out):
        row_cand = rank / jnp.sum(kernel_cand * scale_cand, axis=1, keepdims=True)
        row_ref = rank / jnp.sum(kernel_ref * scale_ref, axis=1, keepdims=True)
        mass_cand = jnp.sum(row_cand * kernel_cand, axis=0, keepdims=True) / cand_total
        mass_ref = jnp.sum(row_ref * kernel_ref, axis=0, keepdims=True) / ref_total
        both = jnp.concatenate([mass_cand, mass_ref], axis=0)
        out[...] = jnp.broadcast_to(both[None], (everyone, 2, rank))

    def assemble(pieces_ref, own_ref, cand_half, ref_half, rows):
        chip, ref = lax.axis_index("chip"), lax.axis_index("ref")

        def piece(e, d, start, count):
            at = lax.rem(chip + e, chips) * refs + lax.rem(ref + d, refs)
            return pieces_ref[pl.ds(at * tall_piece + start, count), :]

        def spread(half_ref, at, columns):
            at = pl.ds(pl.multiple_of(at * columns, columns), columns)
            for lane in range(lanes):
                half_ref[at, lane * 128 : (lane + 1) * 128] = rows[lane * columns : (lane + 1) * columns, :]

        cand_half[pl.ds(pl.multiple_of(chip * ca, ca), ca), :] = own_ref[:ca, :]
        ref_half[pl.ds(pl.multiple_of(ref * ra, ra), ra), :] = own_ref[ca:, :]
        for e in range(1, chips):
            rows[last:, :] = piece(e, 0, 0, block_rows - last)
            for d in range(1, refs):
                rows[few * (d - 1) : few * d, :] = piece(e, d, 0, few)
            spread(cand_half, lax.rem(chip + e, chips), ca)
        for d in range(1, refs):
            rows[last:, :] = piece(0, d, 0, block_rows - last)
            for e in range(1, chips):
                rows[few * (e - 1) : few * e, :] = piece(e, d, few, few)
            spread(ref_half, lax.rem(ref + d, refs), ra)
        tops = pieces_ref[tall_piece - 1 : tall_piece, :]
        for i in range(1, chips * refs):
            tops = jnp.maximum(tops, pieces_ref[(i + 1) * tall_piece - 1 : (i + 1) * tall_piece, :])
        product = cand_half[...] * ref_half[...]
        folded = product[:, :128]
        for lane in range(1, lanes):
            folded = folded + product[:, lane * 128 : (lane + 1) * 128]
        return tops, jnp.sum(folded.T, axis=0, keepdims=True)

    def half_kernels(
        got_ref, own_ref, cand_high, cand_low, share_high, share_low,
        cand_half, cand_out, share_out, rows_out, ref_half, rows,
    ):
        chip, core = lax.axis_index("chip"), lax.axis_index("core")
        tops, inner = assemble(got_ref, own_ref, cand_half, ref_half, rows)
        rows_out[0:1, :] = tops
        rows_out[1:2, :] = inner
        cand_out[...] = rows_by_rows((own_lanes(cand_high, core), own_lanes(cand_low, core)), ref_half[...])
        at = pl.ds(pl.multiple_of(chip * ref_sub, ref_sub), ref_sub)
        lane = pl.ds(pl.multiple_of(core * half, half), half)
        share_out[...] = rows_by_rows((share_high[at, lane], share_low[at, lane]), cand_half[...])

    cand_half, cand_part, share_part, rows_part = call(
        half_kernels,
        [(rank, half), (cand_rows, rank), (ref_sub, rank), (8, rank)],
        got, mine, cand_high, cand_low, share_high, share_low,
        scratch=[(rank, half), (block_rows, 128)],
        room=12,
    )

    def first_kernels(
        got_ref, own_ref, cand_high, cand_low, cand_plan_ref, share_high, share_low, ref_plan_ref, w_ref,
        cand_half, cand_part, share_part, rows_part,
        cand_moment, full_cand, state, sub_cand, sub_ref, out, other_half, ref_half, rows,
    ):
        chip, core, ref = (lax.axis_index(a) for a in ("chip", "core", "ref"))
        tops, inner = assemble(got_ref, own_ref, other_half, ref_half, rows)
        tops = jnp.maximum(tops, rows_part[0:1, :])
        cand_moment[:, :half] = jnp.where(core == 0, cand_half[...], other_half[...])
        cand_moment[:, half:] = jnp.where(core == 0, other_half[...], cand_half[...])
        w = w_ref[...]
        grad_weights = -(inner + rows_part[1:2, :]) / (w * w)
        top = jnp.maximum(jnp.max(tops, axis=1, keepdims=True), largest(grad_weights)) + tiny_value
        kernel_weights = w * jnp.exp(-step_size * grad_weights / top)
        state[0:1, :] = kernel_weights
        state[1:2, :] = jnp.broadcast_to(top, (1, rank))
        state[2:8, :] = jnp.ones((6, rank), f32)
        factor = (own_lanes(cand_high, 1 - core), own_lanes(cand_low, 1 - core))
        grad = (cand_part[...] + rows_by_rows(factor, ref_half[...])) / w
        full_cand[...] = cand_plan_ref[...] * jnp.exp(-step_size * grad / top)
        kernel_cand = full_cand[pl.ds(pl.multiple_of(ref * cand_sub, cand_sub), cand_sub), :]
        at = pl.ds(pl.multiple_of(chip * ref_sub, ref_sub), ref_sub)
        lane = pl.ds(pl.multiple_of((1 - core) * half, half), half)
        grad = (share_part[...] + rows_by_rows((share_high[at, lane], share_low[at, lane]), other_half[...])) / w
        at = pl.ds(pl.multiple_of(core * share_rows + chip * ref_sub, ref_sub), ref_sub)
        kernel_ref = ref_plan_ref[at, :] * jnp.exp(-step_size * grad / top)
        sub_cand[...] = kernel_cand
        sub_ref[...] = kernel_ref
        ones = jnp.ones((1, rank), f32)
        mass_part(kernel_cand, kernel_ref, ones, ones, out)

    cand_moment, full_cand, state, sub_cand, sub_ref, out = call(
        first_kernels,
        [(rank, width), (cand_rows, rank), (8, rank), (cand_sub, rank), (ref_sub, rank), (everyone, 2, rank)],
        got_other, other, cand_high, cand_low, cand_plan, share_high, share_low, ref_plan, weights_row,
        cand_half, cand_part, share_part, rows_part,
        scratch=[(rank, half), (rank, half), (block_rows, 128)],
        room=12,
    )

    def update(mass_ref, state):
        mass = jnp.sum(mass_ref[...], axis=0)
        mass_cand, mass_ref = mass[0:1], mass[1:2]
        kernel_weights, scale_cand, scale_ref = state[0:1, :], state[2:3, :], state[3:4, :]
        new_weights = cube_root(kernel_weights * scale_cand * mass_cand * scale_ref * mass_ref)
        return new_weights, new_weights / mass_cand, new_weights / mass_ref

    def next_masses(mass_ref, state_ref, sub_cand_ref, sub_ref_ref, new_state, out):
        _, scale_cand, scale_ref = update(mass_ref, state_ref)
        new_state[...] = state_ref[...]
        new_state[2:3, :] = scale_cand
        new_state[3:4, :] = scale_ref
        mass_part(sub_cand_ref[...], sub_ref_ref[...], scale_cand, scale_ref, out)

    for _ in range(ITERS - 1):
        mass = lax.all_to_all(out, ("chip", "core", "ref"), 0, 0)
        state, out = call(next_masses, [(8, rank), (everyone, 2, rank)], mass, state, sub_cand, sub_ref)
    mass = lax.all_to_all(out, ("chip", "core", "ref"), 0, 0)

    def finish(
        mass_ref, cand_moment, state_ref, full_cand, ref_ref, ref_plan_ref, w_ref,
        cand_out, ref_out, w_out, cand_done, ref_done, w_done, sems,
    ):
        new_weights, scale_cand, scale_ref = update(mass_ref, state_ref)
        top = state_ref[1:2, :]
        kernel = full_cand[...]
        row = rank / jnp.sum(kernel * state_ref[2:3, :], axis=1, keepdims=True)
        cand_done[...] = row * kernel * scale_cand
        stores = [pltpu.make_async_copy(cand_done, cand_out, sems.at[0])]
        stores[0].start()
        w_done[...] = new_weights
        stores += [pltpu.make_async_copy(w_done, w_out, sems.at[1])]
        stores[1].start()
        grad = rows_by_rows(split(ref_ref[...]), cand_moment[...]) / w_ref[...]
        kernel = ref_plan_ref[...] * jnp.exp(-step_size * grad / top)
        row = rank / jnp.sum(kernel * state_ref[3:4, :], axis=1, keepdims=True)
        ref_done[...] = row * kernel * scale_ref
        stores += [pltpu.make_async_copy(ref_done, ref_out, sems.at[2])]
        stores[2].start()
        for c in stores:
            c.wait()

    new_cand_plan, new_ref_plan, new_weights = call(
        finish,
        [(cand_rows, rank), (ref_rows, rank), (1, rank)],
        mass, cand_moment, state, full_cand, ref_factor, ref_plan, weights_row,
        scratch=[(cand_rows, rank), (ref_rows, rank), (1, rank), dma((3,))],
        slow_outs=(0, 1, 2),
        room=8,
    )
    return new_cand_plan, new_ref_plan, new_weights.reshape(rank)


def on_device(*args):
    chips, cores, refs = (lax.axis_size(a) for a in ("chip", "core", "ref"))
    rank, width = args[4].shape[0], args[0].shape[1]
    rows = (args[0].shape[0] // refs, args[1].shape[0] // (chips * cores))
    tiled = cores == 2 and chips == refs and rank == 128 and rank % (8 * chips * refs) == 0 and width % (128 * cores) == 0
    tiled = tiled and all(n % 8 == 0 for n in rows)
    return (on_device_tiled if tiled else on_device_any)(*args)


def solution(mesh):
    cand, ref = mesh.shape["cand"], mesh.shape["ref"]
    cores = 2 if cand % 2 == 0 else 1
    finer = Mesh(mesh.devices.reshape(cand // cores, cores, ref), ("chip", "core", "ref"))
    rows = ("chip", "core")
    in_specs = (P(rows, None), P("ref", None), P(rows, None), P("ref", None), P())
    out_specs = (P(rows, None), P("ref", None), P())
    return jax.shard_map(on_device, mesh=finer, in_specs=in_specs, out_specs=out_specs, check_vma=False)
```

```python
import jax
import jax.numpy as jnp
from jax import lax
from jax.experimental import pallas as pl
from jax.experimental.pallas import tpu as pltpu
from jax.sharding import Mesh, PartitionSpec as P

ITERS = 3

step_size = 3.0
tiny_value = 1e-06

HIGH = lax.Precision.HIGH
f32 = jnp.float32


def dot_nt(left, right):
    return lax.dot_general(
        left, right, (((1,), (1,)), ((), ())), precision=HIGH, preferred_element_type=f32
    )


def dot_tn(left, right):
    return lax.dot_general(
        left, right, (((0,), (0,)), ((), ())), precision=HIGH, preferred_element_type=f32
    )


def partner_lists(count):
    if count & (count - 1) == 0:
        return [[(i, i ^ k) for i in range(count)] for k in range(1, count)]
    return [[(i, (i + k) % count) for i in range(count)] for k in range(1, count)]


def swap_core(array, core_count):
    if core_count == 1:
        return None
    return lax.ppermute(array, "core", [(0, 1), (1, 0)])


def share(array, axes, count):
    pieces = jnp.broadcast_to(array[None], (count,) + array.shape)
    return lax.all_to_all(pieces, axes, 0, 0)


def on_device_any(cand_factor, ref_factor, cand_plan, ref_plan, weights):
    chips, cores, refs = (lax.axis_size(a) for a in ("chip", "core", "ref"))
    chip, core, ref = (lax.axis_index(a) for a in ("chip", "core", "ref"))
    cand_rows, width = cand_factor.shape
    ref_rows = ref_factor.shape[0]
    rank = weights.shape[0]
    cand_total = cand_rows * chips * cores
    ref_total = ref_rows * refs
    half = width // cores
    cand_cols, ref_cols = rank // chips, rank // refs

    ref_half = lax.dynamic_slice_in_dim(ref_factor, core * half, half, 1)
    ref_part = dot_tn(ref_plan, ref_half) / ref_total
    blocks = ref_part.reshape(refs, ref_cols, half)
    ref_block = lax.dynamic_index_in_dim(blocks, ref, 0, False)
    arrived = []
    for pairs in partner_lists(refs):
        goes_to = jnp.array([b for _, b in pairs], jnp.int32)[ref]
        arrived.append(lax.ppermute(lax.dynamic_index_in_dim(blocks, goes_to, 0, False), "ref", pairs))

    cand_part = dot_tn(cand_plan, cand_factor) / cand_total
    mine = lax.dynamic_slice_in_dim(cand_part, core * half, half, 1)
    if cores > 1:
        mine = mine + swap_core(lax.dynamic_slice_in_dim(cand_part, (1 - core) * half, half, 1), cores)
    pieces = lax.all_to_all(mine.reshape(chips, cand_cols, half), "chip", 0, 0)
    cand_block = jnp.sum(pieces, axis=0)
    for piece in arrived:
        ref_block = ref_block + piece

    def whole_width(part):
        if cores == 1:
            return part
        other = swap_core(part, cores)
        low = jnp.where(core == 0, part, other)
        high = jnp.where(core == 0, other, part)
        return jnp.concatenate([low, high], axis=-1)

    both = whole_width(jnp.concatenate([cand_block, ref_block], axis=0))
    cand_cols_moment, ref_cols_moment = both[:cand_cols], both[cand_cols:]
    w_ref = lax.dynamic_slice_in_dim(weights, ref * ref_cols, ref_cols, 0)
    w_cand = lax.dynamic_slice_in_dim(weights, chip * cand_cols, cand_cols, 0)
    ref_share = lax.dynamic_slice_in_dim(ref_factor, core * (ref_rows // cores), ref_rows // cores, 0)
    local_top = jnp.maximum(
        jnp.max(jnp.abs(dot_nt(cand_factor, ref_cols_moment) / w_ref[None, :])),
        jnp.max(jnp.abs(dot_nt(ref_share, cand_cols_moment) / w_cand[None, :])),
    )

    if cand_cols % refs == 0 and ref_cols % chips == 0:
        a, b = cand_cols // refs, ref_cols // chips
        cand_piece = lax.dynamic_slice_in_dim(cand_block, ref * a, a, 0)
        ref_piece = lax.dynamic_slice_in_dim(ref_block, chip * b, b, 0)
        piece = jnp.concatenate([cand_piece, ref_piece, jnp.broadcast_to(local_top, (8, half))], axis=0)
        got = share(piece, ("chip", "ref"), chips * refs).reshape(chips, refs, a + b + 8, half)
        cand_m = got[:, :, :a].reshape(rank, half)
        ref_m = jnp.swapaxes(got[:, :, a : a + b], 0, 1).reshape(rank, half)
        tops = got[:, :, a + b :, :]
    else:
        a, b = half // refs, half // chips
        cand_piece = lax.dynamic_slice_in_dim(cand_block, ref * a, a, 1).reshape(-1)
        ref_piece = lax.dynamic_slice_in_dim(ref_block, chip * b, b, 1).reshape(-1)
        piece = jnp.concatenate([cand_piece, ref_piece, local_top[None]])
        got = share(piece, ("chip", "ref"), chips * refs).reshape(chips, refs, -1)
        n = cand_piece.shape[0]
        cand_m = got[:, :, :n].reshape(chips, refs, cand_cols, a).transpose(0, 2, 1, 3).reshape(rank, half)
        ref_m = got[:, :, n:-1].reshape(chips, refs, ref_cols, b).transpose(1, 2, 0, 3).reshape(rank, half)
        tops = got[:, :, -1:]
    top_here = jnp.max(tops)
    both = whole_width(jnp.concatenate([cand_m, ref_m, jnp.broadcast_to(top_here, (8, half))], axis=0))
    cand_moment, ref_moment = both[:rank], both[rank : 2 * rank]
    global_top = jnp.max(both[2 * rank :])

    grad_weights = -jnp.sum(cand_moment * ref_moment, axis=1) / (weights * weights)
    top = jnp.maximum(global_top, jnp.max(jnp.abs(grad_weights))) + tiny_value
    kernel_weights = weights * jnp.exp(-step_size * grad_weights / top)
    kernel_cand = cand_plan * jnp.exp(-step_size * (dot_nt(cand_factor, ref_moment) / weights[None, :]) / top)
    kernel_ref = ref_plan * jnp.exp(-step_size * (dot_nt(ref_factor, cand_moment) / weights[None, :]) / top)

    cand_sub = cand_rows // refs
    ref_sub = ref_rows // (chips * cores)
    mine_cand = lax.dynamic_slice_in_dim(kernel_cand, ref * cand_sub, cand_sub, 0)
    mine_ref = lax.dynamic_slice_in_dim(kernel_ref, (chip * cores + core) * ref_sub, ref_sub, 0)
    scale_cand = jnp.ones((rank,), f32)
    scale_ref = jnp.ones((rank,), f32)
    for _ in range(ITERS):
        last_cand, last_ref = scale_cand, scale_ref
        row_cand = rank / jnp.sum(mine_cand * scale_cand[None, :], axis=1, keepdims=True)
        row_ref = rank / jnp.sum(mine_ref * scale_ref[None, :], axis=1, keepdims=True)
        part = jnp.stack(
            [jnp.sum(row_cand * mine_cand, axis=0) / cand_total, jnp.sum(row_ref * mine_ref, axis=0) / ref_total]
        )
        mass = jnp.sum(share(part, ("chip", "core", "ref"), chips * cores * refs), axis=0)
        mass_cand, mass_ref = mass[0], mass[1]
        new_weights = jnp.cbrt(kernel_weights * scale_cand * mass_cand * scale_ref * mass_ref)
        scale_cand = new_weights / mass_cand
        scale_ref = new_weights / mass_ref
    row_cand = rank / jnp.sum(kernel_cand * last_cand[None, :], axis=1, keepdims=True)
    row_ref = rank / jnp.sum(kernel_ref * last_ref[None, :], axis=1, keepdims=True)
    new_cand_plan = row_cand * kernel_cand * scale_cand[None, :]
    new_ref_plan = row_ref * kernel_ref * scale_ref[None, :]
    return (new_cand_plan, new_ref_plan, new_weights)


load_steps = 2
ref_orders = ([2, 3, 1], [3, 1, 2])
chip_orders = ([3, 2, 1], [1, 3, 2])
bf16 = jnp.bfloat16


def split(x):
    high = x.astype(bf16)
    return high, (x - high.astype(f32)).astype(bf16)


def mxu(left, right, dims):
    return lax.dot_general(left, right, (dims, ((), ())), preferred_element_type=f32)


def rows_by_cols(left, right):
    lh, ll = split(left)
    rh, rl = split(right)
    m, nn = left.shape[0], ((1,), (0,))
    tall = mxu(jnp.concatenate([lh, ll], axis=0), rh, nn)
    return tall[:m] + (tall[m:] + mxu(lh, rl, nn))


def rows_by_rows(left, right):
    n = right.shape[0]
    lh, ll = left
    rh, rl = split(right)
    nt = ((1,), (1,))
    wide = mxu(lh, jnp.concatenate([rh, rl], axis=0), nt)
    return wide[:, :n] + (wide[:, n:] + mxu(ll, rh, nt))


FAST = pl.BlockSpec(memory_space=pltpu.VMEM)
SLOW = pl.BlockSpec(memory_space=pltpu.HBM)


def call(body, outs, *args, scratch=(), slow=(), slow_outs=(), short_outs=(), room=4):
    args = [pltpu.with_memory_space_constraint(a, pltpu.HBM) if i in slow else a for i, a in enumerate(args)]
    return pl.pallas_call(
        body,
        out_shape=[
            pltpu.HBM(s, f32) if i in slow_outs else jax.ShapeDtypeStruct(s, bf16 if i in short_outs else f32)
            for i, s in enumerate(outs)
        ],
        in_specs=[SLOW if i in slow else FAST for i in range(len(args))],
        out_specs=[SLOW if i in slow_outs else FAST for i in range(len(outs))],
        scratch_shapes=[pltpu.VMEM(s, f32) if isinstance(s, tuple) else s for s in scratch],
        compiler_params=pltpu.CompilerParams(vmem_limit_bytes=room << 20),
    )(*args)


def copies(pairs, sems):
    made = [pltpu.make_async_copy(src, dst, sems.at[i]) for i, (src, dst) in enumerate(pairs)]
    for c in made:
        c.start()
    return made


def largest(x):
    return jnp.max(jnp.max(jnp.abs(x), axis=0, keepdims=True), axis=1, keepdims=True)


def cube_root(x):
    return jnp.exp(jnp.log(x) * (1.0 / 3.0))


def on_device_tiled(cand_factor, ref_factor, cand_plan, ref_plan, weights):
    chips, cores, refs = (lax.axis_size(a) for a in ("chip", "core", "ref"))
    cand_rows, width = cand_factor.shape
    ref_rows = ref_factor.shape[0]
    rank = weights.shape[0]
    cand_total = cand_rows * chips * cores
    ref_total = ref_rows * refs
    half = width // cores
    ca, ra = rank // chips, rank // refs
    lanes = half // 128
    block_rows = lanes * ca
    few = -(-block_rows // (refs + 1))
    last = few * (refs - 1)
    tall_piece = 2 * few + 1
    cand_sub = cand_rows // refs
    ref_sub = ref_rows // (chips * cores)
    everyone = chips * cores * refs
    ref_steps = [[0] + (ref_orders[c] if refs == 4 else list(range(1, refs))) for c in range(cores)]
    chip_steps = [[0] + (chip_orders[c] if chips == 4 else list(range(1, chips))) for c in range(cores)]

    def step_at(steps_of, k, core):
        first, second = steps_of[0][k], steps_of[1][k]
        return first if first == second else jnp.where(core == 0, first, second)

    weights_row = weights[None, :]

    steps = load_steps
    step = cand_rows // steps
    dma = pltpu.SemaphoreType.DMA

    share_rows = ref_rows // cores

    def cand_parts(cand_hbm, cand_plan_hbm, keep, send, cand_high, cand_low, cand, cand_plan, sems):
        core = lax.axis_index("core")
        loads = copies(
            [(cand_plan_hbm, cand_plan)]
            + [(cand_hbm.at[pl.ds(i * step, step)], cand.at[pl.ds(i * step, step)]) for i in range(steps)],
            sems,
        )
        loads[0].wait()
        plan = jnp.concatenate(split(cand_plan[...].T), axis=0)
        nn = ((1,), (0,))
        total = None
        for i in range(steps):
            loads[1 + i].wait()
            rows = slice(i * step, (i + 1) * step)
            high, low = split(cand[rows, :])
            cand_high[rows, :], cand_low[rows, :] = high, low
            tall = mxu(plan[:, rows], high, nn)
            part = tall[:rank] + (tall[rank:] + mxu(plan[:rank, rows], low, nn))
            total = part if total is None else total + part
        total = total / cand_total
        keep[...] = jnp.where(core == 0, total[:, :half], total[:, half:])
        send[...] = jnp.where(core == 0, total[:, half:], total[:, :half])

    keep, send, cand_high, cand_low = call(
        cand_parts,
        [(rank, half)] * 2 + [(cand_rows, width)] * 2,
        cand_factor, cand_plan,
        scratch=[(cand_rows, width), (cand_rows, rank), dma((steps + 1,))],
        slow=(0, 1),
        short_outs=(2, 3),
        room=16,
    )
    came = swap_core(send, cores)

    def ref_parts(ref_in, ref_plan_in, *rest):
        blocks, whole = rest[:refs], rest[refs]
        core, ref = lax.axis_index("core"), lax.axis_index("ref")
        here = ref_in[:, pl.ds(pl.multiple_of(core * half, half), half)]
        whole[...] = rows_by_cols(ref_plan_in[...].T, here) / ref_total
        for k in range(refs):
            to = ref ^ step_at(ref_steps, k, core)
            blocks[k][...] = whole[pl.ds(pl.multiple_of(to * ra, ra), ra), :]

    blocks = call(
        ref_parts,
        [(ra, half)] * refs,
        ref_factor, ref_plan,
        scratch=[(rank, half)],
        room=8,
    )
    blocks = [blocks[0]] + [
        lax.ppermute(
            blocks[k],
            ("core", "ref"),
            [(c * refs + i, c * refs + (i ^ ref_steps[c][k])) for c in range(cores) for i in range(refs)],
        )
        for k in range(1, refs)
    ]

    def share_parts(ref_in, share_high, share_low):
        core = lax.axis_index("core")
        share = ref_in[pl.ds(pl.multiple_of(core * share_rows, share_rows), share_rows), :]
        share_high[...], share_low[...] = split(share)

    share_high, share_low = call(share_parts, [(share_rows, width)] * 2, ref_factor, short_outs=(0, 1), room=8)

    def chip_blocks(keep_ref, came_ref, *rest):
        outs, full = rest[:-1], rest[-1]
        chip, core = lax.axis_index("chip"), lax.axis_index("core")
        full[...] = keep_ref[...] + came_ref[...]
        for k in range(chips):
            to = chip ^ step_at(chip_steps, k, core)
            outs[k][...] = full[pl.ds(pl.multiple_of(to * ca, ca), ca), :]

    cand_blocks = call(chip_blocks, [(ca, half)] * chips, keep, came, scratch=[(rank, half)])
    cand_blocks = [cand_blocks[0]] + [
        lax.ppermute(
            cand_blocks[k],
            ("chip", "core"),
            [(i * cores + c, (i ^ chip_steps[c][k]) * cores + c) for c in range(cores) for i in range(chips)],
        )
        for k in range(1, chips)
    ]

    def own_blocks(*rest):
        out = rest[-1]
        for start, count, terms in ((0, ca, rest[:chips]), (ca, ra, rest[chips:-1])):
            total = terms[0][...]
            for term in terms[1:]:
                total = total + term[...]
            out[start : start + count, :] = total

    (mine,) = call(own_blocks, [(ca + ra, half)], *cand_blocks, *blocks)
    other = swap_core(mine, cores)

    def columns_at(moment, at, columns, padded):
        padded[...] = jnp.zeros_like(padded)
        padded[pl.ds(pl.multiple_of(at * columns, columns), columns), :] = moment
        return padded[...]

    def own_lanes(factor, core):
        return factor[:, pl.ds(pl.multiple_of(core * half, half), half)]

    def half_columns(mine_ref, cand_high, cand_low, share_high, share_low, cand_out, share_out, padded):
        chip, core, ref = (lax.axis_index(a) for a in ("chip", "core", "ref"))
        moment = columns_at(mine_ref[ca:, :], ref, ra, padded)
        cand_out[...] = rows_by_rows((own_lanes(cand_high, core), own_lanes(cand_low, core)), moment)
        moment = columns_at(mine_ref[:ca, :], chip, ca, padded)
        share_out[...] = rows_by_rows((own_lanes(share_high, core), own_lanes(share_low, core)), moment)

    cand_cols_part, share_cols_part = call(
        half_columns,
        [(cand_rows, rank), (share_rows, rank)],
        mine, cand_high, cand_low, share_high, share_low,
        scratch=[(rank, half)],
        room=12,
    )

    def column_tops(
        mine_ref, other_ref, cand_high, cand_low, share_high, share_low, cand_part, share_part, w_ref, out, padded, rows
    ):
        chip, core, ref = (lax.axis_index(a) for a in ("chip", "core", "ref"))
        w = w_ref[...]
        moment = columns_at(other_ref[ca:, :], ref, ra, padded)
        factor = (own_lanes(cand_high, 1 - core), own_lanes(cand_low, 1 - core))
        grad_cand = cand_part[...] + rows_by_rows(factor, moment)
        moment = columns_at(other_ref[:ca, :], chip, ca, padded)
        factor = (own_lanes(share_high, 1 - core), own_lanes(share_low, 1 - core))
        grad_ref = share_part[...] + rows_by_rows(factor, moment)
        tall = jnp.maximum(
            jnp.max(jnp.abs(grad_cand), axis=0, keepdims=True), jnp.max(jnp.abs(grad_ref), axis=0, keepdims=True)
        )
        for lane in range(lanes):
            at = slice(lane * 128, (lane + 1) * 128)
            rows[lane * ca : (lane + 1) * ca, :] = mine_ref[:ca, at]
            rows[block_rows + lane * ra : block_rows + (lane + 1) * ra, :] = mine_ref[ca:, at]
        top = tall / w
        for e in range(chips):
            for d in range(refs):
                to = lax.rem(chip + chips - e, chips) * refs + lax.rem(ref + refs - d, refs)
                if e and d:
                    part = [rows[few * (d - 1) : few * d, :]]
                    part += [rows[block_rows + few * (e - 1) : block_rows + few * e, :]]
                elif e:
                    part = [rows[last:block_rows, :]]
                else:
                    part = [rows[block_rows + last : 2 * block_rows, :]]
                short = 2 * few - sum(p.shape[0] for p in part)
                part += [jnp.zeros((short, rank), f32)] if short else []
                out[pl.ds(to * tall_piece, tall_piece), :] = jnp.concatenate(part + [top], axis=0)

    (to_all,) = call(
        column_tops,
        [(chips * refs * tall_piece, 128)],
        mine,
        other,
        cand_high,
        cand_low,
        share_high,
        share_low,
        cand_cols_part,
        share_cols_part,
        weights_row,
        scratch=[(rank, half), (2 * block_rows, 128)],
        room=12,
    )
    to_all = to_all.reshape(chips * refs, tall_piece, 1, 128)
    got = lax.all_to_all(to_all, ("chip", "ref"), 0, 0).reshape(-1, 128)
    got_other = swap_core(got, cores)

    def mass_part(kernel_cand, kernel_ref, scale_cand, scale_ref, out):
        row_cand = rank / jnp.sum(kernel_cand * scale_cand, axis=1, keepdims=True)
        row_ref = rank / jnp.sum(kernel_ref * scale_ref, axis=1, keepdims=True)
        mass_cand = jnp.sum(row_cand * kernel_cand, axis=0, keepdims=True) / cand_total
        mass_ref = jnp.sum(row_ref * kernel_ref, axis=0, keepdims=True) / ref_total
        both = jnp.concatenate([mass_cand, mass_ref], axis=0)
        out[...] = jnp.broadcast_to(both[None], (everyone, 2, rank))

    def assemble(pieces_ref, own_ref, cand_half, ref_half, rows):
        chip, ref = lax.axis_index("chip"), lax.axis_index("ref")

        def piece(e, d, start, count):
            at = lax.rem(chip + e, chips) * refs + lax.rem(ref + d, refs)
            return pieces_ref[pl.ds(at * tall_piece + start, count), :]

        def spread(half_ref, at, columns):
            at = pl.ds(pl.multiple_of(at * columns, columns), columns)
            for lane in range(lanes):
                half_ref[at, lane * 128 : (lane + 1) * 128] = rows[lane * columns : (lane + 1) * columns, :]

        cand_half[pl.ds(pl.multiple_of(chip * ca, ca), ca), :] = own_ref[:ca, :]
        ref_half[pl.ds(pl.multiple_of(ref * ra, ra), ra), :] = own_ref[ca:, :]
        for e in range(1, chips):
            rows[last:, :] = piece(e, 0, 0, block_rows - last)
            for d in range(1, refs):
                rows[few * (d - 1) : few * d, :] = piece(e, d, 0, few)
            spread(cand_half, lax.rem(chip + e, chips), ca)
        for d in range(1, refs):
            rows[last:, :] = piece(0, d, 0, block_rows - last)
            for e in range(1, chips):
                rows[few * (e - 1) : few * e, :] = piece(e, d, few, few)
            spread(ref_half, lax.rem(ref + d, refs), ra)
        tops = pieces_ref[tall_piece - 1 : tall_piece, :]
        for i in range(1, chips * refs):
            tops = jnp.maximum(tops, pieces_ref[(i + 1) * tall_piece - 1 : (i + 1) * tall_piece, :])
        product = cand_half[...] * ref_half[...]
        folded = product[:, :128]
        for lane in range(1, lanes):
            folded = folded + product[:, lane * 128 : (lane + 1) * 128]
        return tops, jnp.sum(folded.T, axis=0, keepdims=True)

    def half_kernels(
        got_ref, own_ref, cand_high, cand_low, share_high, share_low,
        cand_half, cand_out, share_out, rows_out, ref_half, rows,
    ):
        chip, core = lax.axis_index("chip"), lax.axis_index("core")
        tops, inner = assemble(got_ref, own_ref, cand_half, ref_half, rows)
        rows_out[0:1, :] = tops
        rows_out[1:2, :] = inner
        cand_out[...] = rows_by_rows((own_lanes(cand_high, core), own_lanes(cand_low, core)), ref_half[...])
        at = pl.ds(pl.multiple_of(chip * ref_sub, ref_sub), ref_sub)
        lane = pl.ds(pl.multiple_of(core * half, half), half)
        share_out[...] = rows_by_rows((share_high[at, lane], share_low[at, lane]), cand_half[...])

    cand_half, cand_part, share_part, rows_part = call(
        half_kernels,
        [(rank, half), (cand_rows, rank), (ref_sub, rank), (8, rank)],
        got, mine, cand_high, cand_low, share_high, share_low,
        scratch=[(rank, half), (block_rows, 128)],
        room=12,
    )

    def first_kernels(
        got_ref, own_ref, cand_high, cand_low, cand_plan_ref, share_high, share_low, ref_plan_ref, w_ref,
        cand_half, cand_part, share_part, rows_part,
        cand_moment, full_cand, state, sub_cand, sub_ref, out, other_half, ref_half, rows,
    ):
        chip, core, ref = (lax.axis_index(a) for a in ("chip", "core", "ref"))
        tops, inner = assemble(got_ref, own_ref, other_half, ref_half, rows)
        tops = jnp.maximum(tops, rows_part[0:1, :])
        cand_moment[:, :half] = jnp.where(core == 0, cand_half[...], other_half[...])
        cand_moment[:, half:] = jnp.where(core == 0, other_half[...], cand_half[...])
        w = w_ref[...]
        grad_weights = -(inner + rows_part[1:2, :]) / (w * w)
        top = jnp.maximum(jnp.max(tops, axis=1, keepdims=True), largest(grad_weights)) + tiny_value
        kernel_weights = w * jnp.exp(-step_size * grad_weights / top)
        state[0:1, :] = kernel_weights
        state[1:2, :] = jnp.broadcast_to(top, (1, rank))
        state[2:8, :] = jnp.ones((6, rank), f32)
        factor = (own_lanes(cand_high, 1 - core), own_lanes(cand_low, 1 - core))
        grad = (cand_part[...] + rows_by_rows(factor, ref_half[...])) / w
        full_cand[...] = cand_plan_ref[...] * jnp.exp(-step_size * grad / top)
        kernel_cand = full_cand[pl.ds(pl.multiple_of(ref * cand_sub, cand_sub), cand_sub), :]
        at = pl.ds(pl.multiple_of(chip * ref_sub, ref_sub), ref_sub)
        lane = pl.ds(pl.multiple_of((1 - core) * half, half), half)
        grad = (share_part[...] + rows_by_rows((share_high[at, lane], share_low[at, lane]), other_half[...])) / w
        at = pl.ds(pl.multiple_of(core * share_rows + chip * ref_sub, ref_sub), ref_sub)
        kernel_ref = ref_plan_ref[at, :] * jnp.exp(-step_size * grad / top)
        sub_cand[...] = kernel_cand
        sub_ref[...] = kernel_ref
        ones = jnp.ones((1, rank), f32)
        mass_part(kernel_cand, kernel_ref, ones, ones, out)

    cand_moment, full_cand, state, sub_cand, sub_ref, out = call(
        first_kernels,
        [(rank, width), (cand_rows, rank), (8, rank), (cand_sub, rank), (ref_sub, rank), (everyone, 2, rank)],
        got_other, other, cand_high, cand_low, cand_plan, share_high, share_low, ref_plan, weights_row,
        cand_half, cand_part, share_part, rows_part,
        scratch=[(rank, half), (rank, half), (block_rows, 128)],
        room=12,
    )

    def update(mass_ref, state):
        mass = jnp.sum(mass_ref[...], axis=0)
        mass_cand, mass_ref = mass[0:1], mass[1:2]
        kernel_weights, scale_cand, scale_ref = state[0:1, :], state[2:3, :], state[3:4, :]
        new_weights = cube_root(kernel_weights * scale_cand * mass_cand * scale_ref * mass_ref)
        return new_weights, new_weights / mass_cand, new_weights / mass_ref

    def next_masses(mass_ref, state_ref, sub_cand_ref, sub_ref_ref, new_state, out):
        _, scale_cand, scale_ref = update(mass_ref, state_ref)
        new_state[...] = state_ref[...]
        new_state[2:3, :] = scale_cand
        new_state[3:4, :] = scale_ref
        mass_part(sub_cand_ref[...], sub_ref_ref[...], scale_cand, scale_ref, out)

    for _ in range(ITERS - 1):
        mass = lax.all_to_all(out, ("chip", "core", "ref"), 0, 0)
        state, out = call(next_masses, [(8, rank), (everyone, 2, rank)], mass, state, sub_cand, sub_ref)
    mass = lax.all_to_all(out, ("chip", "core", "ref"), 0, 0)

    def finish(
        mass_ref, cand_moment, state_ref, full_cand, ref_ref, ref_plan_ref, w_ref,
        cand_out, ref_out, w_out, cand_done, ref_done, w_done, sems,
    ):
        new_weights, scale_cand, scale_ref = update(mass_ref, state_ref)
        top = state_ref[1:2, :]
        kernel = full_cand[...]
        row = rank / jnp.sum(kernel * state_ref[2:3, :], axis=1, keepdims=True)
        cand_done[...] = row * kernel * scale_cand
        stores = [pltpu.make_async_copy(cand_done, cand_out, sems.at[0])]
        stores[0].start()
        w_done[...] = new_weights
        stores += [pltpu.make_async_copy(w_done, w_out, sems.at[1])]
        stores[1].start()
        grad = rows_by_rows(split(ref_ref[...]), cand_moment[...]) / w_ref[...]
        kernel = ref_plan_ref[...] * jnp.exp(-step_size * grad / top)
        row = rank / jnp.sum(kernel * state_ref[3:4, :], axis=1, keepdims=True)
        ref_done[...] = row * kernel * scale_ref
        stores += [pltpu.make_async_copy(ref_done, ref_out, sems.at[2])]
        stores[2].start()
        for c in stores:
            c.wait()

    new_cand_plan, new_ref_plan, new_weights = call(
        finish,
        [(cand_rows, rank), (ref_rows, rank), (1, rank)],
        mass, cand_moment, state, full_cand, ref_factor, ref_plan, weights_row,
        scratch=[(cand_rows, rank), (ref_rows, rank), (1, rank), dma((3,))],
        slow_outs=(0, 1, 2),
        room=8,
    )
    return new_cand_plan, new_ref_plan, new_weights.reshape(rank)


def on_device(*args):
    chips, cores, refs = (lax.axis_size(a) for a in ("chip", "core", "ref"))
    rank, width = args[4].shape[0], args[0].shape[1]
    rows = (args[0].shape[0] // refs, args[1].shape[0] // (chips * cores))
    tiled = cores == 2 and chips == refs and rank == 128 and rank % (8 * chips * refs) == 0 and width % (128 * cores) == 0
    tiled = tiled and all(n % 8 == 0 for n in rows)
    return (on_device_tiled if tiled else on_device_any)(*args)


def solution(mesh):
    cand, ref = mesh.shape["cand"], mesh.shape["ref"]
    cores = 2 if cand % 2 == 0 else 1
    finer = Mesh(mesh.devices.reshape(cand // cores, cores, ref), ("chip", "core", "ref"))
    rows = ("chip", "core")
    in_specs = (P(rows, None), P("ref", None), P(rows, None), P("ref", None), P())
    out_specs = (P(rows, None), P("ref", None), P())
    return jax.shard_map(on_device, mesh=finer, in_specs=in_specs, out_specs=out_specs, check_vma=False)
```

```python
import jax
import jax.numpy as jnp
from jax import lax
from jax.experimental import pallas as pl
from jax.experimental.pallas import tpu as pltpu
from jax.sharding import Mesh, PartitionSpec as P

ITERS = 3

step_size = 3.0
tiny_value = 1e-06

HIGH = lax.Precision.HIGH
f32 = jnp.float32


def dot_nt(left, right):
    return lax.dot_general(
        left, right, (((1,), (1,)), ((), ())), precision=HIGH, preferred_element_type=f32
    )


def dot_tn(left, right):
    return lax.dot_general(
        left, right, (((0,), (0,)), ((), ())), precision=HIGH, preferred_element_type=f32
    )


def partner_lists(count):
    if count & (count - 1) == 0:
        return [[(i, i ^ k) for i in range(count)] for k in range(1, count)]
    return [[(i, (i + k) % count) for i in range(count)] for k in range(1, count)]


def swap_core(array, core_count):
    if core_count == 1:
        return None
    return lax.ppermute(array, "core", [(0, 1), (1, 0)])


def share(array, axes, count):
    pieces = jnp.broadcast_to(array[None], (count,) + array.shape)
    return lax.all_to_all(pieces, axes, 0, 0)


def on_device_any(cand_factor, ref_factor, cand_plan, ref_plan, weights):
    chips, cores, refs = (lax.axis_size(a) for a in ("chip", "core", "ref"))
    chip, core, ref = (lax.axis_index(a) for a in ("chip", "core", "ref"))
    cand_rows, width = cand_factor.shape
    ref_rows = ref_factor.shape[0]
    rank = weights.shape[0]
    cand_total = cand_rows * chips * cores
    ref_total = ref_rows * refs
    half = width // cores
    cand_cols, ref_cols = rank // chips, rank // refs

    ref_half = lax.dynamic_slice_in_dim(ref_factor, core * half, half, 1)
    ref_part = dot_tn(ref_plan, ref_half) / ref_total
    blocks = ref_part.reshape(refs, ref_cols, half)
    ref_block = lax.dynamic_index_in_dim(blocks, ref, 0, False)
    arrived = []
    for pairs in partner_lists(refs):
        goes_to = jnp.array([b for _, b in pairs], jnp.int32)[ref]
        arrived.append(lax.ppermute(lax.dynamic_index_in_dim(blocks, goes_to, 0, False), "ref", pairs))

    cand_part = dot_tn(cand_plan, cand_factor) / cand_total
    mine = lax.dynamic_slice_in_dim(cand_part, core * half, half, 1)
    if cores > 1:
        mine = mine + swap_core(lax.dynamic_slice_in_dim(cand_part, (1 - core) * half, half, 1), cores)
    pieces = lax.all_to_all(mine.reshape(chips, cand_cols, half), "chip", 0, 0)
    cand_block = jnp.sum(pieces, axis=0)
    for piece in arrived:
        ref_block = ref_block + piece

    def whole_width(part):
        if cores == 1:
            return part
        other = swap_core(part, cores)
        low = jnp.where(core == 0, part, other)
        high = jnp.where(core == 0, other, part)
        return jnp.concatenate([low, high], axis=-1)

    both = whole_width(jnp.concatenate([cand_block, ref_block], axis=0))
    cand_cols_moment, ref_cols_moment = both[:cand_cols], both[cand_cols:]
    w_ref = lax.dynamic_slice_in_dim(weights, ref * ref_cols, ref_cols, 0)
    w_cand = lax.dynamic_slice_in_dim(weights, chip * cand_cols, cand_cols, 0)
    ref_share = lax.dynamic_slice_in_dim(ref_factor, core * (ref_rows // cores), ref_rows // cores, 0)
    local_top = jnp.maximum(
        jnp.max(jnp.abs(dot_nt(cand_factor, ref_cols_moment) / w_ref[None, :])),
        jnp.max(jnp.abs(dot_nt(ref_share, cand_cols_moment) / w_cand[None, :])),
    )

    if cand_cols % refs == 0 and ref_cols % chips == 0:
        a, b = cand_cols // refs, ref_cols // chips
        cand_piece = lax.dynamic_slice_in_dim(cand_block, ref * a, a, 0)
        ref_piece = lax.dynamic_slice_in_dim(ref_block, chip * b, b, 0)
        piece = jnp.concatenate([cand_piece, ref_piece, jnp.broadcast_to(local_top, (8, half))], axis=0)
        got = share(piece, ("chip", "ref"), chips * refs).reshape(chips, refs, a + b + 8, half)
        cand_m = got[:, :, :a].reshape(rank, half)
        ref_m = jnp.swapaxes(got[:, :, a : a + b], 0, 1).reshape(rank, half)
        tops = got[:, :, a + b :, :]
    else:
        a, b = half // refs, half // chips
        cand_piece = lax.dynamic_slice_in_dim(cand_block, ref * a, a, 1).reshape(-1)
        ref_piece = lax.dynamic_slice_in_dim(ref_block, chip * b, b, 1).reshape(-1)
        piece = jnp.concatenate([cand_piece, ref_piece, local_top[None]])
        got = share(piece, ("chip", "ref"), chips * refs).reshape(chips, refs, -1)
        n = cand_piece.shape[0]
        cand_m = got[:, :, :n].reshape(chips, refs, cand_cols, a).transpose(0, 2, 1, 3).reshape(rank, half)
        ref_m = got[:, :, n:-1].reshape(chips, refs, ref_cols, b).transpose(1, 2, 0, 3).reshape(rank, half)
        tops = got[:, :, -1:]
    top_here = jnp.max(tops)
    both = whole_width(jnp.concatenate([cand_m, ref_m, jnp.broadcast_to(top_here, (8, half))], axis=0))
    cand_moment, ref_moment = both[:rank], both[rank : 2 * rank]
    global_top = jnp.max(both[2 * rank :])

    grad_weights = -jnp.sum(cand_moment * ref_moment, axis=1) / (weights * weights)
    top = jnp.maximum(global_top, jnp.max(jnp.abs(grad_weights))) + tiny_value
    kernel_weights = weights * jnp.exp(-step_size * grad_weights / top)
    kernel_cand = cand_plan * jnp.exp(-step_size * (dot_nt(cand_factor, ref_moment) / weights[None, :]) / top)
    kernel_ref = ref_plan * jnp.exp(-step_size * (dot_nt(ref_factor, cand_moment) / weights[None, :]) / top)

    cand_sub = cand_rows // refs
    ref_sub = ref_rows // (chips * cores)
    mine_cand = lax.dynamic_slice_in_dim(kernel_cand, ref * cand_sub, cand_sub, 0)
    mine_ref = lax.dynamic_slice_in_dim(kernel_ref, (chip * cores + core) * ref_sub, ref_sub, 0)
    scale_cand = jnp.ones((rank,), f32)
    scale_ref = jnp.ones((rank,), f32)
    for _ in range(ITERS):
        last_cand, last_ref = scale_cand, scale_ref
        row_cand = rank / jnp.sum(mine_cand * scale_cand[None, :], axis=1, keepdims=True)
        row_ref = rank / jnp.sum(mine_ref * scale_ref[None, :], axis=1, keepdims=True)
        part = jnp.stack(
            [jnp.sum(row_cand * mine_cand, axis=0) / cand_total, jnp.sum(row_ref * mine_ref, axis=0) / ref_total]
        )
        mass = jnp.sum(share(part, ("chip", "core", "ref"), chips * cores * refs), axis=0)
        mass_cand, mass_ref = mass[0], mass[1]
        new_weights = jnp.cbrt(kernel_weights * scale_cand * mass_cand * scale_ref * mass_ref)
        scale_cand = new_weights / mass_cand
        scale_ref = new_weights / mass_ref
    row_cand = rank / jnp.sum(kernel_cand * last_cand[None, :], axis=1, keepdims=True)
    row_ref = rank / jnp.sum(kernel_ref * last_ref[None, :], axis=1, keepdims=True)
    new_cand_plan = row_cand * kernel_cand * scale_cand[None, :]
    new_ref_plan = row_ref * kernel_ref * scale_ref[None, :]
    return (new_cand_plan, new_ref_plan, new_weights)


load_steps = 2
ref_orders = ([2, 3, 1], [3, 1, 2])
chip_orders = ([3, 2, 1], [1, 3, 2])
bf16 = jnp.bfloat16


def split(x):
    high = x.astype(bf16)
    return high, (x - high.astype(f32)).astype(bf16)


def mxu(left, right, dims):
    return lax.dot_general(left, right, (dims, ((), ())), preferred_element_type=f32)


def rows_by_cols(left, right):
    lh, ll = split(left)
    rh, rl = split(right)
    m, nn = left.shape[0], ((1,), (0,))
    tall = mxu(jnp.concatenate([lh, ll], axis=0), rh, nn)
    return tall[:m] + (tall[m:] + mxu(lh, rl, nn))


def rows_by_rows(left, right):
    n = right.shape[0]
    lh, ll = left
    rh, rl = split(right)
    nt = ((1,), (1,))
    wide = mxu(lh, jnp.concatenate([rh, rl], axis=0), nt)
    return wide[:, :n] + (wide[:, n:] + mxu(ll, rh, nt))


FAST = pl.BlockSpec(memory_space=pltpu.VMEM)
SLOW = pl.BlockSpec(memory_space=pltpu.HBM)


def call(body, outs, *args, scratch=(), slow=(), slow_outs=(), short_outs=(), room=4):
    args = [pltpu.with_memory_space_constraint(a, pltpu.HBM) if i in slow else a for i, a in enumerate(args)]
    return pl.pallas_call(
        body,
        out_shape=[
            pltpu.HBM(s, f32) if i in slow_outs else jax.ShapeDtypeStruct(s, bf16 if i in short_outs else f32)
            for i, s in enumerate(outs)
        ],
        in_specs=[SLOW if i in slow else FAST for i in range(len(args))],
        out_specs=[SLOW if i in slow_outs else FAST for i in range(len(outs))],
        scratch_shapes=[pltpu.VMEM(s, f32) if isinstance(s, tuple) else s for s in scratch],
        compiler_params=pltpu.CompilerParams(vmem_limit_bytes=room << 20),
    )(*args)


def copies(pairs, sems):
    made = [pltpu.make_async_copy(src, dst, sems.at[i]) for i, (src, dst) in enumerate(pairs)]
    for c in made:
        c.start()
    return made


def largest(x):
    return jnp.max(jnp.max(jnp.abs(x), axis=0, keepdims=True), axis=1, keepdims=True)


def cube_root(x):
    return jnp.exp(jnp.log(x) * (1.0 / 3.0))


def on_device_tiled(cand_factor, ref_factor, cand_plan, ref_plan, weights):
    chips, cores, refs = (lax.axis_size(a) for a in ("chip", "core", "ref"))
    cand_rows, width = cand_factor.shape
    ref_rows = ref_factor.shape[0]
    rank = weights.shape[0]
    cand_total = cand_rows * chips * cores
    ref_total = ref_rows * refs
    half = width // cores
    ca, ra = rank // chips, rank // refs
    lanes = half // 128
    block_rows = lanes * ca
    few = -(-block_rows // (refs + 1))
    last = few * (refs - 1)
    tall_piece = 2 * few + 1
    cand_sub = cand_rows // refs
    ref_sub = ref_rows // (chips * cores)
    everyone = chips * cores * refs
    ref_steps = [[0] + (ref_orders[c] if refs == 4 else list(range(1, refs))) for c in range(cores)]
    chip_steps = [[0] + (chip_orders[c] if chips == 4 else list(range(1, chips))) for c in range(cores)]

    def step_at(steps_of, k, core):
        first, second = steps_of[0][k], steps_of[1][k]
        return first if first == second else jnp.where(core == 0, first, second)

    weights_row = weights[None, :]

    steps = load_steps
    step = cand_rows // steps
    dma = pltpu.SemaphoreType.DMA

    share_rows = ref_rows // cores

    def cand_parts(cand_hbm, cand_plan_hbm, keep, send, cand_high, cand_low, cand, cand_plan, sems):
        core = lax.axis_index("core")
        loads = copies(
            [(cand_plan_hbm, cand_plan)]
            + [(cand_hbm.at[pl.ds(i * step, step)], cand.at[pl.ds(i * step, step)]) for i in range(steps)],
            sems,
        )
        loads[0].wait()
        plan = jnp.concatenate(split(cand_plan[...].T), axis=0)
        nn = ((1,), (0,))
        total = None
        for i in range(steps):
            loads[1 + i].wait()
            rows = slice(i * step, (i + 1) * step)
            high, low = split(cand[rows, :])
            cand_high[rows, :], cand_low[rows, :] = high, low
            tall = mxu(plan[:, rows], high, nn)
            part = tall[:rank] + (tall[rank:] + mxu(plan[:rank, rows], low, nn))
            total = part if total is None else total + part
        total = total / cand_total
        keep[...] = jnp.where(core == 0, total[:, :half], total[:, half:])
        send[...] = jnp.where(core == 0, total[:, half:], total[:, :half])

    keep, send, cand_high, cand_low = call(
        cand_parts,
        [(rank, half)] * 2 + [(cand_rows, width)] * 2,
        cand_factor, cand_plan,
        scratch=[(cand_rows, width), (cand_rows, rank), dma((steps + 1,))],
        slow=(0, 1),
        short_outs=(2, 3),
        room=16,
    )
    came = swap_core(send, cores)

    def ref_parts(ref_in, ref_plan_in, *rest):
        blocks, whole = rest[:refs], rest[refs]
        core, ref = lax.axis_index("core"), lax.axis_index("ref")
        here = ref_in[:, pl.ds(pl.multiple_of(core * half, half), half)]
        whole[...] = rows_by_cols(ref_plan_in[...].T, here) / ref_total
        for k in range(refs):
            to = ref ^ step_at(ref_steps, k, core)
            blocks[k][...] = whole[pl.ds(pl.multiple_of(to * ra, ra), ra), :]

    blocks = call(
        ref_parts,
        [(ra, half)] * refs,
        ref_factor, ref_plan,
        scratch=[(rank, half)],
        room=8,
    )
    blocks = [blocks[0]] + [
        lax.ppermute(
            blocks[k],
            ("core", "ref"),
            [(c * refs + i, c * refs + (i ^ ref_steps[c][k])) for c in range(cores) for i in range(refs)],
        )
        for k in range(1, refs)
    ]

    def share_parts(ref_in, share_high, share_low):
        core = lax.axis_index("core")
        share = ref_in[pl.ds(pl.multiple_of(core * share_rows, share_rows), share_rows), :]
        share_high[...], share_low[...] = split(share)

    share_high, share_low = call(share_parts, [(share_rows, width)] * 2, ref_factor, short_outs=(0, 1), room=8)

    def chip_blocks(keep_ref, came_ref, *rest):
        outs, full = rest[:-1], rest[-1]
        chip, core = lax.axis_index("chip"), lax.axis_index("core")
        full[...] = keep_ref[...] + came_ref[...]
        for k in range(chips):
            to = chip ^ step_at(chip_steps, k, core)
            outs[k][...] = full[pl.ds(pl.multiple_of(to * ca, ca), ca), :]

    cand_blocks = call(chip_blocks, [(ca, half)] * chips, keep, came, scratch=[(rank, half)])
    cand_blocks = [cand_blocks[0]] + [
        lax.ppermute(
            cand_blocks[k],
            ("chip", "core"),
            [(i * cores + c, (i ^ chip_steps[c][k]) * cores + c) for c in range(cores) for i in range(chips)],
        )
        for k in range(1, chips)
    ]

    def own_blocks(*rest):
        out = rest[-1]
        for start, count, terms in ((0, ca, rest[:chips]), (ca, ra, rest[chips:-1])):
            total = terms[0][...]
            for term in terms[1:]:
                total = total + term[...]
            out[start : start + count, :] = total

    (mine,) = call(own_blocks, [(ca + ra, half)], *cand_blocks, *blocks)
    other = swap_core(mine, cores)

    def columns_at(moment, at, columns, padded):
        padded[...] = jnp.zeros_like(padded)
        padded[pl.ds(pl.multiple_of(at * columns, columns), columns), :] = moment
        return padded[...]

    def own_lanes(factor, core):
        return factor[:, pl.ds(pl.multiple_of(core * half, half), half)]

    def half_columns(mine_ref, cand_high, cand_low, share_high, share_low, cand_out, share_out, out, padded, rows):
        chip, core, ref = (lax.axis_index(a) for a in ("chip", "core", "ref"))
        moment = columns_at(mine_ref[ca:, :], ref, ra, padded)
        cand_out[...] = rows_by_rows((own_lanes(cand_high, core), own_lanes(cand_low, core)), moment)
        moment = columns_at(mine_ref[:ca, :], chip, ca, padded)
        share_out[...] = rows_by_rows((own_lanes(share_high, core), own_lanes(share_low, core)), moment)
        for lane in range(lanes):
            at = slice(lane * 128, (lane + 1) * 128)
            rows[lane * ca : (lane + 1) * ca, :] = mine_ref[:ca, at]
            rows[block_rows + lane * ra : block_rows + (lane + 1) * ra, :] = mine_ref[ca:, at]
        for e in range(chips):
            for d in range(refs):
                to = lax.rem(chip + chips - e, chips) * refs + lax.rem(ref + refs - d, refs)
                if e and d:
                    part = [rows[few * (d - 1) : few * d, :]]
                    part += [rows[block_rows + few * (e - 1) : block_rows + few * e, :]]
                elif e:
                    part = [rows[last:block_rows, :]]
                else:
                    part = [rows[block_rows + last : 2 * block_rows, :]]
                short = 2 * few - sum(p.shape[0] for p in part)
                part += [jnp.zeros((short, rank), f32)] if short else []
                out[pl.ds(to * tall_piece, 2 * few), :] = jnp.concatenate(part, axis=0)
        for i in range(chips * refs):
            out[(i + 1) * tall_piece - 1 : (i + 1) * tall_piece, :] = jnp.zeros((1, rank), f32)

    cand_cols_part, share_cols_part, data = call(
        half_columns,
        [(cand_rows, rank), (share_rows, rank), (chips * refs * tall_piece, 128)],
        mine, cand_high, cand_low, share_high, share_low,
        scratch=[(rank, half), (2 * block_rows, 128)],
        room=12,
    )

    def column_tops(
        mine_ref, other_ref, cand_high, cand_low, share_high, share_low, cand_part, share_part, data_ref, w_ref, out, padded
    ):
        chip, core, ref = (lax.axis_index(a) for a in ("chip", "core", "ref"))
        w = w_ref[...]
        moment = columns_at(other_ref[ca:, :], ref, ra, padded)
        factor = (own_lanes(cand_high, 1 - core), own_lanes(cand_low, 1 - core))
        grad_cand = cand_part[...] + rows_by_rows(factor, moment)
        moment = columns_at(other_ref[:ca, :], chip, ca, padded)
        factor = (own_lanes(share_high, 1 - core), own_lanes(share_low, 1 - core))
        grad_ref = share_part[...] + rows_by_rows(factor, moment)
        tall = jnp.maximum(
            jnp.max(jnp.abs(grad_cand), axis=0, keepdims=True), jnp.max(jnp.abs(grad_ref), axis=0, keepdims=True)
        )
        top = tall / w
        out[...] = data_ref[...]
        for i in range(chips * refs):
            out[(i + 1) * tall_piece - 1 : (i + 1) * tall_piece, :] = top

    (to_all,) = call(
        column_tops,
        [(chips * refs * tall_piece, 128)],
        mine,
        other,
        cand_high,
        cand_low,
        share_high,
        share_low,
        cand_cols_part,
        share_cols_part,
        data,
        weights_row,
        scratch=[(rank, half)],
        room=12,
    )
    to_all = to_all.reshape(chips * refs, tall_piece, 1, 128)
    got = lax.all_to_all(to_all, ("chip", "ref"), 0, 0).reshape(-1, 128)
    got_other = swap_core(got, cores)

    def mass_part(kernel_cand, kernel_ref, scale_cand, scale_ref, out):
        row_cand = rank / jnp.sum(kernel_cand * scale_cand, axis=1, keepdims=True)
        row_ref = rank / jnp.sum(kernel_ref * scale_ref, axis=1, keepdims=True)
        mass_cand = jnp.sum(row_cand * kernel_cand, axis=0, keepdims=True) / cand_total
        mass_ref = jnp.sum(row_ref * kernel_ref, axis=0, keepdims=True) / ref_total
        both = jnp.concatenate([mass_cand, mass_ref], axis=0)
        out[...] = jnp.broadcast_to(both[None], (everyone, 2, rank))

    def assemble(pieces_ref, own_ref, cand_half, ref_half, rows):
        chip, ref = lax.axis_index("chip"), lax.axis_index("ref")

        def piece(e, d, start, count):
            at = lax.rem(chip + e, chips) * refs + lax.rem(ref + d, refs)
            return pieces_ref[pl.ds(at * tall_piece + start, count), :]

        def spread(half_ref, at, columns):
            at = pl.ds(pl.multiple_of(at * columns, columns), columns)
            for lane in range(lanes):
                half_ref[at, lane * 128 : (lane + 1) * 128] = rows[lane * columns : (lane + 1) * columns, :]

        cand_half[pl.ds(pl.multiple_of(chip * ca, ca), ca), :] = own_ref[:ca, :]
        ref_half[pl.ds(pl.multiple_of(ref * ra, ra), ra), :] = own_ref[ca:, :]
        for e in range(1, chips):
            rows[last:, :] = piece(e, 0, 0, block_rows - last)
            for d in range(1, refs):
                rows[few * (d - 1) : few * d, :] = piece(e, d, 0, few)
            spread(cand_half, lax.rem(chip + e, chips), ca)
        for d in range(1, refs):
            rows[last:, :] = piece(0, d, 0, block_rows - last)
            for e in range(1, chips):
                rows[few * (e - 1) : few * e, :] = piece(e, d, few, few)
            spread(ref_half, lax.rem(ref + d, refs), ra)
        tops = pieces_ref[tall_piece - 1 : tall_piece, :]
        for i in range(1, chips * refs):
            tops = jnp.maximum(tops, pieces_ref[(i + 1) * tall_piece - 1 : (i + 1) * tall_piece, :])
        product = cand_half[...] * ref_half[...]
        folded = product[:, :128]
        for lane in range(1, lanes):
            folded = folded + product[:, lane * 128 : (lane + 1) * 128]
        return tops, jnp.sum(folded.T, axis=0, keepdims=True)

    def half_kernels(
        got_ref, own_ref, cand_high, cand_low, share_high, share_low,
        cand_half, cand_out, share_out, rows_out, ref_half, rows,
    ):
        chip, core = lax.axis_index("chip"), lax.axis_index("core")
        tops, inner = assemble(got_ref, own_ref, cand_half, ref_half, rows)
        rows_out[0:1, :] = tops
        rows_out[1:2, :] = inner
        cand_out[...] = rows_by_rows((own_lanes(cand_high, core), own_lanes(cand_low, core)), ref_half[...])
        at = pl.ds(pl.multiple_of(chip * ref_sub, ref_sub), ref_sub)
        lane = pl.ds(pl.multiple_of(core * half, half), half)
        share_out[...] = rows_by_rows((share_high[at, lane], share_low[at, lane]), cand_half[...])

    cand_half, cand_part, share_part, rows_part = call(
        half_kernels,
        [(rank, half), (cand_rows, rank), (ref_sub, rank), (8, rank)],
        got, mine, cand_high, cand_low, share_high, share_low,
        scratch=[(rank, half), (block_rows, 128)],
        room=12,
    )

    def first_kernels(
        got_ref, own_ref, cand_high, cand_low, cand_plan_ref, share_high, share_low, ref_plan_ref, w_ref,
        cand_half, cand_part, share_part, rows_part,
        cand_moment, full_cand, state, sub_cand, sub_ref, out, other_half, ref_half, rows,
    ):
        chip, core, ref = (lax.axis_index(a) for a in ("chip", "core", "ref"))
        tops, inner = assemble(got_ref, own_ref, other_half, ref_half, rows)
        tops = jnp.maximum(tops, rows_part[0:1, :])
        cand_moment[:, :half] = jnp.where(core == 0, cand_half[...], other_half[...])
        cand_moment[:, half:] = jnp.where(core == 0, other_half[...], cand_half[...])
        w = w_ref[...]
        grad_weights = -(inner + rows_part[1:2, :]) / (w * w)
        top = jnp.maximum(jnp.max(tops, axis=1, keepdims=True), largest(grad_weights)) + tiny_value
        kernel_weights = w * jnp.exp(-step_size * grad_weights / top)
        state[0:1, :] = kernel_weights
        state[1:2, :] = jnp.broadcast_to(top, (1, rank))
        state[2:8, :] = jnp.ones((6, rank), f32)
        factor = (own_lanes(cand_high, 1 - core), own_lanes(cand_low, 1 - core))
        grad = (cand_part[...] + rows_by_rows(factor, ref_half[...])) / w
        full_cand[...] = cand_plan_ref[...] * jnp.exp(-step_size * grad / top)
        kernel_cand = full_cand[pl.ds(pl.multiple_of(ref * cand_sub, cand_sub), cand_sub), :]
        at = pl.ds(pl.multiple_of(chip * ref_sub, ref_sub), ref_sub)
        lane = pl.ds(pl.multiple_of((1 - core) * half, half), half)
        grad = (share_part[...] + rows_by_rows((share_high[at, lane], share_low[at, lane]), other_half[...])) / w
        at = pl.ds(pl.multiple_of(core * share_rows + chip * ref_sub, ref_sub), ref_sub)
        kernel_ref = ref_plan_ref[at, :] * jnp.exp(-step_size * grad / top)
        sub_cand[...] = kernel_cand
        sub_ref[...] = kernel_ref
        ones = jnp.ones((1, rank), f32)
        mass_part(kernel_cand, kernel_ref, ones, ones, out)

    cand_moment, full_cand, state, sub_cand, sub_ref, out = call(
        first_kernels,
        [(rank, width), (cand_rows, rank), (8, rank), (cand_sub, rank), (ref_sub, rank), (everyone, 2, rank)],
        got_other, other, cand_high, cand_low, cand_plan, share_high, share_low, ref_plan, weights_row,
        cand_half, cand_part, share_part, rows_part,
        scratch=[(rank, half), (rank, half), (block_rows, 128)],
        room=12,
    )

    def update(mass_ref, state):
        mass = jnp.sum(mass_ref[...], axis=0)
        mass_cand, mass_ref = mass[0:1], mass[1:2]
        kernel_weights, scale_cand, scale_ref = state[0:1, :], state[2:3, :], state[3:4, :]
        new_weights = cube_root(kernel_weights * scale_cand * mass_cand * scale_ref * mass_ref)
        return new_weights, new_weights / mass_cand, new_weights / mass_ref

    def next_masses(mass_ref, state_ref, sub_cand_ref, sub_ref_ref, new_state, out):
        _, scale_cand, scale_ref = update(mass_ref, state_ref)
        new_state[...] = state_ref[...]
        new_state[2:3, :] = scale_cand
        new_state[3:4, :] = scale_ref
        mass_part(sub_cand_ref[...], sub_ref_ref[...], scale_cand, scale_ref, out)

    for _ in range(ITERS - 1):
        mass = lax.all_to_all(out, ("chip", "core", "ref"), 0, 0)
        state, out = call(next_masses, [(8, rank), (everyone, 2, rank)], mass, state, sub_cand, sub_ref)
    mass = lax.all_to_all(out, ("chip", "core", "ref"), 0, 0)

    def finish(
        mass_ref, cand_moment, state_ref, full_cand, ref_ref, ref_plan_ref, w_ref,
        cand_out, ref_out, w_out, cand_done, ref_done, w_done, sems,
    ):
        new_weights, scale_cand, scale_ref = update(mass_ref, state_ref)
        top = state_ref[1:2, :]
        kernel = full_cand[...]
        row = rank / jnp.sum(kernel * state_ref[2:3, :], axis=1, keepdims=True)
        cand_done[...] = row * kernel * scale_cand
        stores = [pltpu.make_async_copy(cand_done, cand_out, sems.at[0])]
        stores[0].start()
        w_done[...] = new_weights
        stores += [pltpu.make_async_copy(w_done, w_out, sems.at[1])]
        stores[1].start()
        grad = rows_by_rows(split(ref_ref[...]), cand_moment[...]) / w_ref[...]
        kernel = ref_plan_ref[...] * jnp.exp(-step_size * grad / top)
        row = rank / jnp.sum(kernel * state_ref[3:4, :], axis=1, keepdims=True)
        ref_done[...] = row * kernel * scale_ref
        stores += [pltpu.make_async_copy(ref_done, ref_out, sems.at[2])]
        stores[2].start()
        for c in stores:
            c.wait()

    new_cand_plan, new_ref_plan, new_weights = call(
        finish,
        [(cand_rows, rank), (ref_rows, rank), (1, rank)],
        mass, cand_moment, state, full_cand, ref_factor, ref_plan, weights_row,
        scratch=[(cand_rows, rank), (ref_rows, rank), (1, rank), dma((3,))],
        slow_outs=(0, 1, 2),
        room=8,
    )
    return new_cand_plan, new_ref_plan, new_weights.reshape(rank)


def on_device(*args):
    chips, cores, refs = (lax.axis_size(a) for a in ("chip", "core", "ref"))
    rank, width = args[4].shape[0], args[0].shape[1]
    rows = (args[0].shape[0] // refs, args[1].shape[0] // (chips * cores))
    tiled = cores == 2 and chips == refs and rank == 128 and rank % (8 * chips * refs) == 0 and width % (128 * cores) == 0
    tiled = tiled and all(n % 8 == 0 for n in rows)
    return (on_device_tiled if tiled else on_device_any)(*args)


def solution(mesh):
    cand, ref = mesh.shape["cand"], mesh.shape["ref"]
    cores = 2 if cand % 2 == 0 else 1
    finer = Mesh(mesh.devices.reshape(cand // cores, cores, ref), ("chip", "core", "ref"))
    rows = ("chip", "core")
    in_specs = (P(rows, None), P("ref", None), P(rows, None), P("ref", None), P())
    out_specs = (P(rows, None), P("ref", None), P())
    return jax.shard_map(on_device, mesh=finer, in_specs=in_specs, out_specs=out_specs, check_vma=False)
```

```python
import jax
import jax.numpy as jnp
from jax import lax
from jax.experimental import pallas as pl
from jax.experimental.pallas import tpu as pltpu
from jax.sharding import Mesh, PartitionSpec as P

ITERS = 3

step_size = 3.0
tiny_value = 1e-06

HIGH = lax.Precision.HIGH
f32 = jnp.float32


def dot_nt(left, right):
    return lax.dot_general(
        left, right, (((1,), (1,)), ((), ())), precision=HIGH, preferred_element_type=f32
    )


def dot_tn(left, right):
    return lax.dot_general(
        left, right, (((0,), (0,)), ((), ())), precision=HIGH, preferred_element_type=f32
    )


def partner_lists(count):
    if count & (count - 1) == 0:
        return [[(i, i ^ k) for i in range(count)] for k in range(1, count)]
    return [[(i, (i + k) % count) for i in range(count)] for k in range(1, count)]


def swap_core(array, core_count):
    if core_count == 1:
        return None
    return lax.ppermute(array, "core", [(0, 1), (1, 0)])


def share(array, axes, count):
    pieces = jnp.broadcast_to(array[None], (count,) + array.shape)
    return lax.all_to_all(pieces, axes, 0, 0)


def on_device_any(cand_factor, ref_factor, cand_plan, ref_plan, weights):
    chips, cores, refs = (lax.axis_size(a) for a in ("chip", "core", "ref"))
    chip, core, ref = (lax.axis_index(a) for a in ("chip", "core", "ref"))
    cand_rows, width = cand_factor.shape
    ref_rows = ref_factor.shape[0]
    rank = weights.shape[0]
    cand_total = cand_rows * chips * cores
    ref_total = ref_rows * refs
    half = width // cores
    cand_cols, ref_cols = rank // chips, rank // refs

    ref_half = lax.dynamic_slice_in_dim(ref_factor, core * half, half, 1)
    ref_part = dot_tn(ref_plan, ref_half) / ref_total
    blocks = ref_part.reshape(refs, ref_cols, half)
    ref_block = lax.dynamic_index_in_dim(blocks, ref, 0, False)
    arrived = []
    for pairs in partner_lists(refs):
        goes_to = jnp.array([b for _, b in pairs], jnp.int32)[ref]
        arrived.append(lax.ppermute(lax.dynamic_index_in_dim(blocks, goes_to, 0, False), "ref", pairs))

    cand_part = dot_tn(cand_plan, cand_factor) / cand_total
    mine = lax.dynamic_slice_in_dim(cand_part, core * half, half, 1)
    if cores > 1:
        mine = mine + swap_core(lax.dynamic_slice_in_dim(cand_part, (1 - core) * half, half, 1), cores)
    pieces = lax.all_to_all(mine.reshape(chips, cand_cols, half), "chip", 0, 0)
    cand_block = jnp.sum(pieces, axis=0)
    for piece in arrived:
        ref_block = ref_block + piece

    def whole_width(part):
        if cores == 1:
            return part
        other = swap_core(part, cores)
        low = jnp.where(core == 0, part, other)
        high = jnp.where(core == 0, other, part)
        return jnp.concatenate([low, high], axis=-1)

    both = whole_width(jnp.concatenate([cand_block, ref_block], axis=0))
    cand_cols_moment, ref_cols_moment = both[:cand_cols], both[cand_cols:]
    w_ref = lax.dynamic_slice_in_dim(weights, ref * ref_cols, ref_cols, 0)
    w_cand = lax.dynamic_slice_in_dim(weights, chip * cand_cols, cand_cols, 0)
    ref_share = lax.dynamic_slice_in_dim(ref_factor, core * (ref_rows // cores), ref_rows // cores, 0)
    local_top = jnp.maximum(
        jnp.max(jnp.abs(dot_nt(cand_factor, ref_cols_moment) / w_ref[None, :])),
        jnp.max(jnp.abs(dot_nt(ref_share, cand_cols_moment) / w_cand[None, :])),
    )

    if cand_cols % refs == 0 and ref_cols % chips == 0:
        a, b = cand_cols // refs, ref_cols // chips
        cand_piece = lax.dynamic_slice_in_dim(cand_block, ref * a, a, 0)
        ref_piece = lax.dynamic_slice_in_dim(ref_block, chip * b, b, 0)
        piece = jnp.concatenate([cand_piece, ref_piece, jnp.broadcast_to(local_top, (8, half))], axis=0)
        got = share(piece, ("chip", "ref"), chips * refs).reshape(chips, refs, a + b + 8, half)
        cand_m = got[:, :, :a].reshape(rank, half)
        ref_m = jnp.swapaxes(got[:, :, a : a + b], 0, 1).reshape(rank, half)
        tops = got[:, :, a + b :, :]
    else:
        a, b = half // refs, half // chips
        cand_piece = lax.dynamic_slice_in_dim(cand_block, ref * a, a, 1).reshape(-1)
        ref_piece = lax.dynamic_slice_in_dim(ref_block, chip * b, b, 1).reshape(-1)
        piece = jnp.concatenate([cand_piece, ref_piece, local_top[None]])
        got = share(piece, ("chip", "ref"), chips * refs).reshape(chips, refs, -1)
        n = cand_piece.shape[0]
        cand_m = got[:, :, :n].reshape(chips, refs, cand_cols, a).transpose(0, 2, 1, 3).reshape(rank, half)
        ref_m = got[:, :, n:-1].reshape(chips, refs, ref_cols, b).transpose(1, 2, 0, 3).reshape(rank, half)
        tops = got[:, :, -1:]
    top_here = jnp.max(tops)
    both = whole_width(jnp.concatenate([cand_m, ref_m, jnp.broadcast_to(top_here, (8, half))], axis=0))
    cand_moment, ref_moment = both[:rank], both[rank : 2 * rank]
    global_top = jnp.max(both[2 * rank :])

    grad_weights = -jnp.sum(cand_moment * ref_moment, axis=1) / (weights * weights)
    top = jnp.maximum(global_top, jnp.max(jnp.abs(grad_weights))) + tiny_value
    kernel_weights = weights * jnp.exp(-step_size * grad_weights / top)
    kernel_cand = cand_plan * jnp.exp(-step_size * (dot_nt(cand_factor, ref_moment) / weights[None, :]) / top)
    kernel_ref = ref_plan * jnp.exp(-step_size * (dot_nt(ref_factor, cand_moment) / weights[None, :]) / top)

    cand_sub = cand_rows // refs
    ref_sub = ref_rows // (chips * cores)
    mine_cand = lax.dynamic_slice_in_dim(kernel_cand, ref * cand_sub, cand_sub, 0)
    mine_ref = lax.dynamic_slice_in_dim(kernel_ref, (chip * cores + core) * ref_sub, ref_sub, 0)
    scale_cand = jnp.ones((rank,), f32)
    scale_ref = jnp.ones((rank,), f32)
    for _ in range(ITERS):
        last_cand, last_ref = scale_cand, scale_ref
        row_cand = rank / jnp.sum(mine_cand * scale_cand[None, :], axis=1, keepdims=True)
        row_ref = rank / jnp.sum(mine_ref * scale_ref[None, :], axis=1, keepdims=True)
        part = jnp.stack(
            [jnp.sum(row_cand * mine_cand, axis=0) / cand_total, jnp.sum(row_ref * mine_ref, axis=0) / ref_total]
        )
        mass = jnp.sum(share(part, ("chip", "core", "ref"), chips * cores * refs), axis=0)
        mass_cand, mass_ref = mass[0], mass[1]
        new_weights = jnp.cbrt(kernel_weights * scale_cand * mass_cand * scale_ref * mass_ref)
        scale_cand = new_weights / mass_cand
        scale_ref = new_weights / mass_ref
    row_cand = rank / jnp.sum(kernel_cand * last_cand[None, :], axis=1, keepdims=True)
    row_ref = rank / jnp.sum(kernel_ref * last_ref[None, :], axis=1, keepdims=True)
    new_cand_plan = row_cand * kernel_cand * scale_cand[None, :]
    new_ref_plan = row_ref * kernel_ref * scale_ref[None, :]
    return (new_cand_plan, new_ref_plan, new_weights)


load_steps = 2
ref_orders = ([2, 3, 1], [3, 1, 2])
chip_orders = ([3, 2, 1], [1, 3, 2])
bf16 = jnp.bfloat16


def split(x):
    high = x.astype(bf16)
    return high, (x - high.astype(f32)).astype(bf16)


def mxu(left, right, dims):
    return lax.dot_general(left, right, (dims, ((), ())), preferred_element_type=f32)


def rows_by_cols(left, right):
    lh, ll = split(left)
    rh, rl = split(right)
    m, nn = left.shape[0], ((1,), (0,))
    tall = mxu(jnp.concatenate([lh, ll], axis=0), rh, nn)
    return tall[:m] + (tall[m:] + mxu(lh, rl, nn))


def rows_by_rows(left, right):
    n = right.shape[0]
    lh, ll = left
    rh, rl = split(right)
    nt = ((1,), (1,))
    wide = mxu(lh, jnp.concatenate([rh, rl], axis=0), nt)
    return wide[:, :n] + (wide[:, n:] + mxu(ll, rh, nt))


FAST = pl.BlockSpec(memory_space=pltpu.VMEM)
SLOW = pl.BlockSpec(memory_space=pltpu.HBM)


def call(body, outs, *args, scratch=(), slow=(), slow_outs=(), short_outs=(), room=4):
    args = [pltpu.with_memory_space_constraint(a, pltpu.HBM) if i in slow else a for i, a in enumerate(args)]
    return pl.pallas_call(
        body,
        out_shape=[
            pltpu.HBM(s, f32) if i in slow_outs else jax.ShapeDtypeStruct(s, bf16 if i in short_outs else f32)
            for i, s in enumerate(outs)
        ],
        in_specs=[SLOW if i in slow else FAST for i in range(len(args))],
        out_specs=[SLOW if i in slow_outs else FAST for i in range(len(outs))],
        scratch_shapes=[pltpu.VMEM(s, f32) if isinstance(s, tuple) else s for s in scratch],
        compiler_params=pltpu.CompilerParams(vmem_limit_bytes=room << 20),
    )(*args)


def copies(pairs, sems):
    made = [pltpu.make_async_copy(src, dst, sems.at[i]) for i, (src, dst) in enumerate(pairs)]
    for c in made:
        c.start()
    return made


def largest(x):
    return jnp.max(jnp.max(jnp.abs(x), axis=0, keepdims=True), axis=1, keepdims=True)


def cube_root(x):
    return jnp.exp(jnp.log(x) * (1.0 / 3.0))


def on_device_tiled(cand_factor, ref_factor, cand_plan, ref_plan, weights):
    chips, cores, refs = (lax.axis_size(a) for a in ("chip", "core", "ref"))
    cand_rows, width = cand_factor.shape
    ref_rows = ref_factor.shape[0]
    rank = weights.shape[0]
    cand_total = cand_rows * chips * cores
    ref_total = ref_rows * refs
    half = width // cores
    ca, ra = rank // chips, rank // refs
    lanes = half // 128
    block_rows = lanes * ca
    few = -(-block_rows // (refs + 1))
    last = few * (refs - 1)
    tall_piece = 2 * few + 1
    cand_sub = cand_rows // refs
    ref_sub = ref_rows // (chips * cores)
    everyone = chips * cores * refs
    ref_steps = [[0] + (ref_orders[c] if refs == 4 else list(range(1, refs))) for c in range(cores)]
    chip_steps = [[0] + (chip_orders[c] if chips == 4 else list(range(1, chips))) for c in range(cores)]

    def step_at(steps_of, k, core):
        first, second = steps_of[0][k], steps_of[1][k]
        return first if first == second else jnp.where(core == 0, first, second)

    weights_row = weights[None, :]

    steps = load_steps
    step = cand_rows // steps
    dma = pltpu.SemaphoreType.DMA

    share_rows = ref_rows // cores

    def cand_parts(cand_hbm, cand_plan_hbm, keep, send, cand_high, cand_low, cand, cand_plan, sems):
        core = lax.axis_index("core")
        loads = copies(
            [(cand_plan_hbm, cand_plan)]
            + [(cand_hbm.at[pl.ds(i * step, step)], cand.at[pl.ds(i * step, step)]) for i in range(steps)],
            sems,
        )
        loads[0].wait()
        plan = jnp.concatenate(split(cand_plan[...].T), axis=0)
        nn = ((1,), (0,))
        total = None
        for i in range(steps):
            loads[1 + i].wait()
            rows = slice(i * step, (i + 1) * step)
            high, low = split(cand[rows, :])
            cand_high[rows, :], cand_low[rows, :] = high, low
            tall = mxu(plan[:, rows], high, nn)
            part = tall[:rank] + (tall[rank:] + mxu(plan[:rank, rows], low, nn))
            total = part if total is None else total + part
        total = total / cand_total
        keep[...] = jnp.where(core == 0, total[:, :half], total[:, half:])
        send[...] = jnp.where(core == 0, total[:, half:], total[:, :half])

    keep, send, cand_high, cand_low = call(
        cand_parts,
        [(rank, half)] * 2 + [(cand_rows, width)] * 2,
        cand_factor, cand_plan,
        scratch=[(cand_rows, width), (cand_rows, rank), dma((steps + 1,))],
        slow=(0, 1),
        short_outs=(2, 3),
        room=16,
    )
    came = swap_core(send, cores)

    def ref_parts(ref_in, ref_plan_in, *rest):
        blocks, whole = rest[:refs], rest[refs]
        core, ref = lax.axis_index("core"), lax.axis_index("ref")
        here = ref_in[:, pl.ds(pl.multiple_of(core * half, half), half)]
        whole[...] = rows_by_cols(ref_plan_in[...].T, here) / ref_total
        for k in range(refs):
            to = ref ^ step_at(ref_steps, k, core)
            blocks[k][...] = whole[pl.ds(pl.multiple_of(to * ra, ra), ra), :]

    blocks = call(
        ref_parts,
        [(ra, half)] * refs,
        ref_factor, ref_plan,
        scratch=[(rank, half)],
        room=8,
    )
    blocks = [blocks[0]] + [
        lax.ppermute(
            blocks[k],
            ("core", "ref"),
            [(c * refs + i, c * refs + (i ^ ref_steps[c][k])) for c in range(cores) for i in range(refs)],
        )
        for k in range(1, refs)
    ]

    def share_parts(ref_in, share_high, share_low):
        core = lax.axis_index("core")
        share = ref_in[pl.ds(pl.multiple_of(core * share_rows, share_rows), share_rows), :]
        share_high[...], share_low[...] = split(share)

    share_high, share_low = call(share_parts, [(share_rows, width)] * 2, ref_factor, short_outs=(0, 1), room=8)

    def chip_blocks(keep_ref, came_ref, *rest):
        outs, full = rest[:-1], rest[-1]
        chip, core = lax.axis_index("chip"), lax.axis_index("core")
        full[...] = keep_ref[...] + came_ref[...]
        for k in range(chips):
            to = chip ^ step_at(chip_steps, k, core)
            outs[k][...] = full[pl.ds(pl.multiple_of(to * ca, ca), ca), :]

    cand_blocks = call(chip_blocks, [(ca, half)] * chips, keep, came, scratch=[(rank, half)])
    cand_blocks = [cand_blocks[0]] + [
        lax.ppermute(
            cand_blocks[k],
            ("chip", "core"),
            [(i * cores + c, (i ^ chip_steps[c][k]) * cores + c) for c in range(cores) for i in range(chips)],
        )
        for k in range(1, chips)
    ]

    def own_blocks(*rest):
        out = rest[-1]
        for start, count, terms in ((0, ca, rest[:chips]), (ca, ra, rest[chips:-1])):
            total = terms[0][...]
            for term in terms[1:]:
                total = total + term[...]
            out[start : start + count, :] = total

    (mine,) = call(own_blocks, [(ca + ra, half)], *cand_blocks, *blocks)
    other = swap_core(mine, cores)

    def columns_at(moment, at, columns, padded):
        padded[...] = jnp.zeros_like(padded)
        padded[pl.ds(pl.multiple_of(at * columns, columns), columns), :] = moment
        return padded[...]

    def own_lanes(factor, core):
        return factor[:, pl.ds(pl.multiple_of(core * half, half), half)]

    def half_columns(mine_ref, cand_high, cand_low, share_high, share_low, cand_out, share_out, out, padded, rows):
        chip, core, ref = (lax.axis_index(a) for a in ("chip", "core", "ref"))
        moment = columns_at(mine_ref[ca:, :], ref, ra, padded)
        cand_out[...] = rows_by_rows((own_lanes(cand_high, core), own_lanes(cand_low, core)), moment)
        moment = columns_at(mine_ref[:ca, :], chip, ca, padded)
        share_out[...] = rows_by_rows((own_lanes(share_high, core), own_lanes(share_low, core)), moment)
        for lane in range(lanes):
            at = slice(lane * 128, (lane + 1) * 128)
            rows[lane * ca : (lane + 1) * ca, :] = mine_ref[:ca, at]
            rows[block_rows + lane * ra : block_rows + (lane + 1) * ra, :] = mine_ref[ca:, at]
        for e in range(chips):
            for d in range(refs):
                to = lax.rem(chip + chips - e, chips) * refs + lax.rem(ref + refs - d, refs)
                if e and d:
                    part = [rows[few * (d - 1) : few * d, :]]
                    part += [rows[block_rows + few * (e - 1) : block_rows + few * e, :]]
                elif e:
                    part = [rows[last:block_rows, :]]
                else:
                    part = [rows[block_rows + last : 2 * block_rows, :]]
                short = 2 * few - sum(p.shape[0] for p in part)
                part += [jnp.zeros((short, rank), f32)] if short else []
                out[pl.ds(to * tall_piece, 2 * few), :] = jnp.concatenate(part, axis=0)
        for i in range(chips * refs):
            out[(i + 1) * tall_piece - 1 : (i + 1) * tall_piece, :] = jnp.zeros((1, rank), f32)

    cand_cols_part, share_cols_part, data = call(
        half_columns,
        [(cand_rows, rank), (share_rows, rank), (chips * refs * tall_piece, 128)],
        mine, cand_high, cand_low, share_high, share_low,
        scratch=[(rank, half), (2 * block_rows, 128)],
        room=12,
    )

    def column_tops(
        mine_ref, other_ref, cand_high, cand_low, share_high, share_low, cand_part, share_part, data_ref, w_ref, out, padded
    ):
        chip, core, ref = (lax.axis_index(a) for a in ("chip", "core", "ref"))
        w = w_ref[...]
        moment = columns_at(other_ref[ca:, :], ref, ra, padded)
        factor = (own_lanes(cand_high, 1 - core), own_lanes(cand_low, 1 - core))
        grad_cand = cand_part[...] + rows_by_rows(factor, moment)
        moment = columns_at(other_ref[:ca, :], chip, ca, padded)
        factor = (own_lanes(share_high, 1 - core), own_lanes(share_low, 1 - core))
        grad_ref = share_part[...] + rows_by_rows(factor, moment)
        tall = jnp.maximum(
            jnp.max(jnp.abs(grad_cand), axis=0, keepdims=True), jnp.max(jnp.abs(grad_ref), axis=0, keepdims=True)
        )
        top = tall / w
        out[...] = data_ref[...]
        for i in range(chips * refs):
            out[(i + 1) * tall_piece - 1 : (i + 1) * tall_piece, :] = top

    (to_all,) = call(
        column_tops,
        [(chips * refs * tall_piece, 128)],
        mine,
        other,
        cand_high,
        cand_low,
        share_high,
        share_low,
        cand_cols_part,
        share_cols_part,
        data,
        weights_row,
        scratch=[(rank, half)],
        room=12,
    )
    to_all = to_all.reshape(chips * refs, tall_piece, 1, 128)
    got = lax.all_to_all(to_all, ("chip", "ref"), 0, 0).reshape(-1, 128)
    got_other = swap_core(got, cores)

    def mass_part(kernel_cand, kernel_ref, scale_cand, scale_ref, out):
        row_cand = rank / jnp.sum(kernel_cand * scale_cand, axis=1, keepdims=True)
        row_ref = rank / jnp.sum(kernel_ref * scale_ref, axis=1, keepdims=True)
        mass_cand = jnp.sum(row_cand * kernel_cand, axis=0, keepdims=True) / cand_total
        mass_ref = jnp.sum(row_ref * kernel_ref, axis=0, keepdims=True) / ref_total
        both = jnp.concatenate([mass_cand, mass_ref], axis=0)
        out[...] = jnp.broadcast_to(both[None], (everyone, 2, rank))

    def assemble(pieces_ref, own_ref, cand_half, ref_half, rows):
        chip, ref = lax.axis_index("chip"), lax.axis_index("ref")

        def piece(e, d, start, count):
            at = lax.rem(chip + e, chips) * refs + lax.rem(ref + d, refs)
            return pieces_ref[pl.ds(at * tall_piece + start, count), :]

        def spread(half_ref, at, columns):
            at = pl.ds(pl.multiple_of(at * columns, columns), columns)
            for lane in range(lanes):
                half_ref[at, lane * 128 : (lane + 1) * 128] = rows[lane * columns : (lane + 1) * columns, :]

        cand_half[pl.ds(pl.multiple_of(chip * ca, ca), ca), :] = own_ref[:ca, :]
        ref_half[pl.ds(pl.multiple_of(ref * ra, ra), ra), :] = own_ref[ca:, :]
        for e in range(1, chips):
            rows[last:, :] = piece(e, 0, 0, block_rows - last)
            for d in range(1, refs):
                rows[few * (d - 1) : few * d, :] = piece(e, d, 0, few)
            spread(cand_half, lax.rem(chip + e, chips), ca)
        for d in range(1, refs):
            rows[last:, :] = piece(0, d, 0, block_rows - last)
            for e in range(1, chips):
                rows[few * (e - 1) : few * e, :] = piece(e, d, few, few)
            spread(ref_half, lax.rem(ref + d, refs), ra)
        tops = pieces_ref[tall_piece - 1 : tall_piece, :]
        for i in range(1, chips * refs):
            tops = jnp.maximum(tops, pieces_ref[(i + 1) * tall_piece - 1 : (i + 1) * tall_piece, :])
        product = cand_half[...] * ref_half[...]
        folded = product[:, :128]
        for lane in range(1, lanes):
            folded = folded + product[:, lane * 128 : (lane + 1) * 128]
        return tops, jnp.sum(folded.T, axis=0, keepdims=True)

    def half_kernels(
        got_ref, own_ref, cand_high, cand_low, share_high, share_low,
        cand_half, cand_out, share_out, rows_out, ref_half, rows,
    ):
        chip, core = lax.axis_index("chip"), lax.axis_index("core")
        tops, inner = assemble(got_ref, own_ref, cand_half, ref_half, rows)
        rows_out[0:1, :] = tops
        rows_out[1:2, :] = inner
        cand_out[...] = rows_by_rows((own_lanes(cand_high, core), own_lanes(cand_low, core)), ref_half[...])
        at = pl.ds(pl.multiple_of(chip * ref_sub, ref_sub), ref_sub)
        lane = pl.ds(pl.multiple_of(core * half, half), half)
        share_out[...] = rows_by_rows((share_high[at, lane], share_low[at, lane]), cand_half[...])

    cand_half, cand_part, share_part, rows_part = call(
        half_kernels,
        [(rank, half), (cand_rows, rank), (ref_sub, rank), (8, rank)],
        got, mine, cand_high, cand_low, share_high, share_low,
        scratch=[(rank, half), (block_rows, 128)],
        room=12,
    )

    def first_kernels(
        got_ref, own_ref, cand_high, cand_low, cand_plan_ref, share_high, share_low, ref_plan_ref, w_ref,
        cand_half, cand_part, share_part, rows_part,
        cand_moment, full_cand, state, sub_cand, sub_ref, out, other_half, ref_half, rows,
    ):
        chip, core, ref = (lax.axis_index(a) for a in ("chip", "core", "ref"))
        tops, inner = assemble(got_ref, own_ref, other_half, ref_half, rows)
        tops = jnp.maximum(tops, rows_part[0:1, :])
        cand_moment[:, pl.ds(pl.multiple_of(core * half, half), half)] = cand_half[...]
        cand_moment[:, pl.ds(pl.multiple_of((1 - core) * half, half), half)] = other_half[...]
        w = w_ref[...]
        grad_weights = -(inner + rows_part[1:2, :]) / (w * w)
        top = jnp.maximum(jnp.max(tops, axis=1, keepdims=True), largest(grad_weights)) + tiny_value
        kernel_weights = w * jnp.exp(-step_size * grad_weights / top)
        state[0:1, :] = kernel_weights
        state[1:2, :] = jnp.broadcast_to(top, (1, rank))
        state[2:8, :] = jnp.ones((6, rank), f32)
        factor = (own_lanes(cand_high, 1 - core), own_lanes(cand_low, 1 - core))
        grad = (cand_part[...] + rows_by_rows(factor, ref_half[...])) / w
        full_cand[...] = cand_plan_ref[...] * jnp.exp(-step_size * grad / top)
        kernel_cand = full_cand[pl.ds(pl.multiple_of(ref * cand_sub, cand_sub), cand_sub), :]
        at = pl.ds(pl.multiple_of(chip * ref_sub, ref_sub), ref_sub)
        lane = pl.ds(pl.multiple_of((1 - core) * half, half), half)
        grad = (share_part[...] + rows_by_rows((share_high[at, lane], share_low[at, lane]), other_half[...])) / w
        at = pl.ds(pl.multiple_of(core * share_rows + chip * ref_sub, ref_sub), ref_sub)
        kernel_ref = ref_plan_ref[at, :] * jnp.exp(-step_size * grad / top)
        sub_cand[...] = kernel_cand
        sub_ref[...] = kernel_ref
        ones = jnp.ones((1, rank), f32)
        mass_part(kernel_cand, kernel_ref, ones, ones, out)

    cand_moment, full_cand, state, sub_cand, sub_ref, out = call(
        first_kernels,
        [(rank, width), (cand_rows, rank), (8, rank), (cand_sub, rank), (ref_sub, rank), (everyone, 2, rank)],
        got_other, other, cand_high, cand_low, cand_plan, share_high, share_low, ref_plan, weights_row,
        cand_half, cand_part, share_part, rows_part,
        scratch=[(rank, half), (rank, half), (block_rows, 128)],
        room=12,
    )

    def update(mass_ref, state):
        mass = jnp.sum(mass_ref[...], axis=0)
        mass_cand, mass_ref = mass[0:1], mass[1:2]
        kernel_weights, scale_cand, scale_ref = state[0:1, :], state[2:3, :], state[3:4, :]
        new_weights = cube_root(kernel_weights * scale_cand * mass_cand * scale_ref * mass_ref)
        return new_weights, new_weights / mass_cand, new_weights / mass_ref

    def next_masses(mass_ref, state_ref, sub_cand_ref, sub_ref_ref, new_state, out):
        _, scale_cand, scale_ref = update(mass_ref, state_ref)
        new_state[...] = state_ref[...]
        new_state[2:3, :] = scale_cand
        new_state[3:4, :] = scale_ref
        mass_part(sub_cand_ref[...], sub_ref_ref[...], scale_cand, scale_ref, out)

    for _ in range(ITERS - 1):
        mass = lax.all_to_all(out, ("chip", "core", "ref"), 0, 0)
        state, out = call(next_masses, [(8, rank), (everyone, 2, rank)], mass, state, sub_cand, sub_ref)
    mass = lax.all_to_all(out, ("chip", "core", "ref"), 0, 0)

    def finish(
        mass_ref, cand_moment, state_ref, full_cand, ref_ref, ref_plan_ref, w_ref,
        cand_out, ref_out, w_out, cand_done, ref_done, w_done, sems,
    ):
        new_weights, scale_cand, scale_ref = update(mass_ref, state_ref)
        top = state_ref[1:2, :]
        kernel = full_cand[...]
        row = rank / jnp.sum(kernel * state_ref[2:3, :], axis=1, keepdims=True)
        cand_done[...] = row * kernel * scale_cand
        stores = [pltpu.make_async_copy(cand_done, cand_out, sems.at[0])]
        stores[0].start()
        w_done[...] = new_weights
        stores += [pltpu.make_async_copy(w_done, w_out, sems.at[1])]
        stores[1].start()
        grad = rows_by_rows(split(ref_ref[...]), cand_moment[...]) / w_ref[...]
        kernel = ref_plan_ref[...] * jnp.exp(-step_size * grad / top)
        row = rank / jnp.sum(kernel * state_ref[3:4, :], axis=1, keepdims=True)
        ref_done[...] = row * kernel * scale_ref
        stores += [pltpu.make_async_copy(ref_done, ref_out, sems.at[2])]
        stores[2].start()
        for c in stores:
            c.wait()

    new_cand_plan, new_ref_plan, new_weights = call(
        finish,
        [(cand_rows, rank), (ref_rows, rank), (1, rank)],
        mass, cand_moment, state, full_cand, ref_factor, ref_plan, weights_row,
        scratch=[(cand_rows, rank), (ref_rows, rank), (1, rank), dma((3,))],
        slow_outs=(0, 1, 2),
        room=8,
    )
    return new_cand_plan, new_ref_plan, new_weights.reshape(rank)


def on_device(*args):
    chips, cores, refs = (lax.axis_size(a) for a in ("chip", "core", "ref"))
    rank, width = args[4].shape[0], args[0].shape[1]
    rows = (args[0].shape[0] // refs, args[1].shape[0] // (chips * cores))
    tiled = cores == 2 and chips == refs and rank == 128 and rank % (8 * chips * refs) == 0 and width % (128 * cores) == 0
    tiled = tiled and all(n % 8 == 0 for n in rows)
    return (on_device_tiled if tiled else on_device_any)(*args)


def solution(mesh):
    cand, ref = mesh.shape["cand"], mesh.shape["ref"]
    cores = 2 if cand % 2 == 0 else 1
    finer = Mesh(mesh.devices.reshape(cand // cores, cores, ref), ("chip", "core", "ref"))
    rows = ("chip", "core")
    in_specs = (P(rows, None), P("ref", None), P(rows, None), P("ref", None), P())
    out_specs = (P(rows, None), P("ref", None), P())
    return jax.shard_map(on_device, mesh=finer, in_specs=in_specs, out_specs=out_specs, check_vma=False)
```

```python
import jax
import jax.numpy as jnp
from jax import lax
from jax.experimental import pallas as pl
from jax.experimental.pallas import tpu as pltpu
from jax.sharding import Mesh, PartitionSpec as P

ITERS = 3

step_size = 3.0
tiny_value = 1e-06

HIGH = lax.Precision.HIGH
f32 = jnp.float32


def dot_nt(left, right):
    return lax.dot_general(
        left, right, (((1,), (1,)), ((), ())), precision=HIGH, preferred_element_type=f32
    )


def dot_tn(left, right):
    return lax.dot_general(
        left, right, (((0,), (0,)), ((), ())), precision=HIGH, preferred_element_type=f32
    )


def partner_lists(count):
    if count & (count - 1) == 0:
        return [[(i, i ^ k) for i in range(count)] for k in range(1, count)]
    return [[(i, (i + k) % count) for i in range(count)] for k in range(1, count)]


def swap_core(array, core_count):
    if core_count == 1:
        return None
    return lax.ppermute(array, "core", [(0, 1), (1, 0)])


def share(array, axes, count):
    pieces = jnp.broadcast_to(array[None], (count,) + array.shape)
    return lax.all_to_all(pieces, axes, 0, 0)


def on_device_any(cand_factor, ref_factor, cand_plan, ref_plan, weights):
    chips, cores, refs = (lax.axis_size(a) for a in ("chip", "core", "ref"))
    chip, core, ref = (lax.axis_index(a) for a in ("chip", "core", "ref"))
    cand_rows, width = cand_factor.shape
    ref_rows = ref_factor.shape[0]
    rank = weights.shape[0]
    cand_total = cand_rows * chips * cores
    ref_total = ref_rows * refs
    half = width // cores
    cand_cols, ref_cols = rank // chips, rank // refs

    ref_half = lax.dynamic_slice_in_dim(ref_factor, core * half, half, 1)
    ref_part = dot_tn(ref_plan, ref_half) / ref_total
    blocks = ref_part.reshape(refs, ref_cols, half)
    ref_block = lax.dynamic_index_in_dim(blocks, ref, 0, False)
    arrived = []
    for pairs in partner_lists(refs):
        goes_to = jnp.array([b for _, b in pairs], jnp.int32)[ref]
        arrived.append(lax.ppermute(lax.dynamic_index_in_dim(blocks, goes_to, 0, False), "ref", pairs))

    cand_part = dot_tn(cand_plan, cand_factor) / cand_total
    mine = lax.dynamic_slice_in_dim(cand_part, core * half, half, 1)
    if cores > 1:
        mine = mine + swap_core(lax.dynamic_slice_in_dim(cand_part, (1 - core) * half, half, 1), cores)
    pieces = lax.all_to_all(mine.reshape(chips, cand_cols, half), "chip", 0, 0)
    cand_block = jnp.sum(pieces, axis=0)
    for piece in arrived:
        ref_block = ref_block + piece

    def whole_width(part):
        if cores == 1:
            return part
        other = swap_core(part, cores)
        low = jnp.where(core == 0, part, other)
        high = jnp.where(core == 0, other, part)
        return jnp.concatenate([low, high], axis=-1)

    both = whole_width(jnp.concatenate([cand_block, ref_block], axis=0))
    cand_cols_moment, ref_cols_moment = both[:cand_cols], both[cand_cols:]
    w_ref = lax.dynamic_slice_in_dim(weights, ref * ref_cols, ref_cols, 0)
    w_cand = lax.dynamic_slice_in_dim(weights, chip * cand_cols, cand_cols, 0)
    ref_share = lax.dynamic_slice_in_dim(ref_factor, core * (ref_rows // cores), ref_rows // cores, 0)
    local_top = jnp.maximum(
        jnp.max(jnp.abs(dot_nt(cand_factor, ref_cols_moment) / w_ref[None, :])),
        jnp.max(jnp.abs(dot_nt(ref_share, cand_cols_moment) / w_cand[None, :])),
    )

    if cand_cols % refs == 0 and ref_cols % chips == 0:
        a, b = cand_cols // refs, ref_cols // chips
        cand_piece = lax.dynamic_slice_in_dim(cand_block, ref * a, a, 0)
        ref_piece = lax.dynamic_slice_in_dim(ref_block, chip * b, b, 0)
        piece = jnp.concatenate([cand_piece, ref_piece, jnp.broadcast_to(local_top, (8, half))], axis=0)
        got = share(piece, ("chip", "ref"), chips * refs).reshape(chips, refs, a + b + 8, half)
        cand_m = got[:, :, :a].reshape(rank, half)
        ref_m = jnp.swapaxes(got[:, :, a : a + b], 0, 1).reshape(rank, half)
        tops = got[:, :, a + b :, :]
    else:
        a, b = half // refs, half // chips
        cand_piece = lax.dynamic_slice_in_dim(cand_block, ref * a, a, 1).reshape(-1)
        ref_piece = lax.dynamic_slice_in_dim(ref_block, chip * b, b, 1).reshape(-1)
        piece = jnp.concatenate([cand_piece, ref_piece, local_top[None]])
        got = share(piece, ("chip", "ref"), chips * refs).reshape(chips, refs, -1)
        n = cand_piece.shape[0]
        cand_m = got[:, :, :n].reshape(chips, refs, cand_cols, a).transpose(0, 2, 1, 3).reshape(rank, half)
        ref_m = got[:, :, n:-1].reshape(chips, refs, ref_cols, b).transpose(1, 2, 0, 3).reshape(rank, half)
        tops = got[:, :, -1:]
    top_here = jnp.max(tops)
    both = whole_width(jnp.concatenate([cand_m, ref_m, jnp.broadcast_to(top_here, (8, half))], axis=0))
    cand_moment, ref_moment = both[:rank], both[rank : 2 * rank]
    global_top = jnp.max(both[2 * rank :])

    grad_weights = -jnp.sum(cand_moment * ref_moment, axis=1) / (weights * weights)
    top = jnp.maximum(global_top, jnp.max(jnp.abs(grad_weights))) + tiny_value
    kernel_weights = weights * jnp.exp(-step_size * grad_weights / top)
    kernel_cand = cand_plan * jnp.exp(-step_size * (dot_nt(cand_factor, ref_moment) / weights[None, :]) / top)
    kernel_ref = ref_plan * jnp.exp(-step_size * (dot_nt(ref_factor, cand_moment) / weights[None, :]) / top)

    cand_sub = cand_rows // refs
    ref_sub = ref_rows // (chips * cores)
    mine_cand = lax.dynamic_slice_in_dim(kernel_cand, ref * cand_sub, cand_sub, 0)
    mine_ref = lax.dynamic_slice_in_dim(kernel_ref, (chip * cores + core) * ref_sub, ref_sub, 0)
    scale_cand = jnp.ones((rank,), f32)
    scale_ref = jnp.ones((rank,), f32)
    for _ in range(ITERS):
        last_cand, last_ref = scale_cand, scale_ref
        row_cand = rank / jnp.sum(mine_cand * scale_cand[None, :], axis=1, keepdims=True)
        row_ref = rank / jnp.sum(mine_ref * scale_ref[None, :], axis=1, keepdims=True)
        part = jnp.stack(
            [jnp.sum(row_cand * mine_cand, axis=0) / cand_total, jnp.sum(row_ref * mine_ref, axis=0) / ref_total]
        )
        mass = jnp.sum(share(part, ("chip", "core", "ref"), chips * cores * refs), axis=0)
        mass_cand, mass_ref = mass[0], mass[1]
        new_weights = jnp.cbrt(kernel_weights * scale_cand * mass_cand * scale_ref * mass_ref)
        scale_cand = new_weights / mass_cand
        scale_ref = new_weights / mass_ref
    row_cand = rank / jnp.sum(kernel_cand * last_cand[None, :], axis=1, keepdims=True)
    row_ref = rank / jnp.sum(kernel_ref * last_ref[None, :], axis=1, keepdims=True)
    new_cand_plan = row_cand * kernel_cand * scale_cand[None, :]
    new_ref_plan = row_ref * kernel_ref * scale_ref[None, :]
    return (new_cand_plan, new_ref_plan, new_weights)


load_steps = 2
ref_orders = ([2, 3, 1], [3, 1, 2])
chip_orders = ([1, 3, 2], [3, 2, 1])
bf16 = jnp.bfloat16


def split(x):
    high = x.astype(bf16)
    return high, (x - high.astype(f32)).astype(bf16)


def mxu(left, right, dims):
    return lax.dot_general(left, right, (dims, ((), ())), preferred_element_type=f32)


def rows_by_cols(left, right):
    lh, ll = split(left)
    rh, rl = split(right)
    m, nn = left.shape[0], ((1,), (0,))
    tall = mxu(jnp.concatenate([lh, ll], axis=0), rh, nn)
    return tall[:m] + (tall[m:] + mxu(lh, rl, nn))


def rows_by_rows(left, right):
    n = right.shape[0]
    lh, ll = left
    rh, rl = split(right)
    nt = ((1,), (1,))
    wide = mxu(lh, jnp.concatenate([rh, rl], axis=0), nt)
    return wide[:, :n] + (wide[:, n:] + mxu(ll, rh, nt))


FAST = pl.BlockSpec(memory_space=pltpu.VMEM)
SLOW = pl.BlockSpec(memory_space=pltpu.HBM)


def call(body, outs, *args, scratch=(), slow=(), slow_outs=(), short_outs=(), room=4):
    args = [pltpu.with_memory_space_constraint(a, pltpu.HBM) if i in slow else a for i, a in enumerate(args)]
    return pl.pallas_call(
        body,
        out_shape=[
            pltpu.HBM(s, f32) if i in slow_outs else jax.ShapeDtypeStruct(s, bf16 if i in short_outs else f32)
            for i, s in enumerate(outs)
        ],
        in_specs=[SLOW if i in slow else FAST for i in range(len(args))],
        out_specs=[SLOW if i in slow_outs else FAST for i in range(len(outs))],
        scratch_shapes=[pltpu.VMEM(s, f32) if isinstance(s, tuple) else s for s in scratch],
        compiler_params=pltpu.CompilerParams(vmem_limit_bytes=room << 20),
    )(*args)


def copies(pairs, sems):
    made = [pltpu.make_async_copy(src, dst, sems.at[i]) for i, (src, dst) in enumerate(pairs)]
    for c in made:
        c.start()
    return made


def largest(x):
    return jnp.max(jnp.max(jnp.abs(x), axis=0, keepdims=True), axis=1, keepdims=True)


def cube_root(x):
    return jnp.exp(jnp.log(x) * (1.0 / 3.0))


def on_device_tiled(cand_factor, ref_factor, cand_plan, ref_plan, weights):
    chips, cores, refs = (lax.axis_size(a) for a in ("chip", "core", "ref"))
    cand_rows, width = cand_factor.shape
    ref_rows = ref_factor.shape[0]
    rank = weights.shape[0]
    cand_total = cand_rows * chips * cores
    ref_total = ref_rows * refs
    half = width // cores
    ca, ra = rank // chips, rank // refs
    lanes = half // 128
    block_rows = lanes * ca
    few = -(-block_rows // (refs + 1))
    last = few * (refs - 1)
    tall_piece = 2 * few + 1
    cand_sub = cand_rows // refs
    ref_sub = ref_rows // (chips * cores)
    everyone = chips * cores * refs
    ref_steps = [[0] + (ref_orders[c] if refs == 4 else list(range(1, refs))) for c in range(cores)]
    chip_steps = [[0] + (chip_orders[c] if chips == 4 else list(range(1, chips))) for c in range(cores)]

    def step_at(steps_of, k, core):
        first, second = steps_of[0][k], steps_of[1][k]
        return first if first == second else jnp.where(core == 0, first, second)

    weights_row = weights[None, :]

    steps = load_steps
    step = cand_rows // steps
    dma = pltpu.SemaphoreType.DMA

    share_rows = ref_rows // cores

    def cand_parts(cand_hbm, cand_plan_hbm, keep, send, cand_high, cand_low, cand, cand_plan, sems):
        core = lax.axis_index("core")
        loads = copies(
            [(cand_plan_hbm, cand_plan)]
            + [(cand_hbm.at[pl.ds(i * step, step)], cand.at[pl.ds(i * step, step)]) for i in range(steps)],
            sems,
        )
        loads[0].wait()
        plan = jnp.concatenate(split(cand_plan[...].T), axis=0)
        nn = ((1,), (0,))
        total = None
        for i in range(steps):
            loads[1 + i].wait()
            rows = slice(i * step, (i + 1) * step)
            high, low = split(cand[rows, :])
            cand_high[rows, :], cand_low[rows, :] = high, low
            tall = mxu(plan[:, rows], high, nn)
            part = tall[:rank] + (tall[rank:] + mxu(plan[:rank, rows], low, nn))
            total = part if total is None else total + part
        total = total / cand_total
        keep[...] = jnp.where(core == 0, total[:, :half], total[:, half:])
        send[...] = jnp.where(core == 0, total[:, half:], total[:, :half])

    keep, send, cand_high, cand_low = call(
        cand_parts,
        [(rank, half)] * 2 + [(cand_rows, width)] * 2,
        cand_factor, cand_plan,
        scratch=[(cand_rows, width), (cand_rows, rank), dma((steps + 1,))],
        slow=(0, 1),
        short_outs=(2, 3),
        room=16,
    )
    came = swap_core(send, cores)

    def ref_parts(ref_in, ref_plan_in, *rest):
        blocks, whole = rest[:refs], rest[refs]
        core, ref = lax.axis_index("core"), lax.axis_index("ref")
        here = ref_in[:, pl.ds(pl.multiple_of(core * half, half), half)]
        whole[...] = rows_by_cols(ref_plan_in[...].T, here) / ref_total
        for k in range(refs):
            to = ref ^ step_at(ref_steps, k, core)
            blocks[k][...] = whole[pl.ds(pl.multiple_of(to * ra, ra), ra), :]

    blocks = call(
        ref_parts,
        [(ra, half)] * refs,
        ref_factor, ref_plan,
        scratch=[(rank, half)],
        room=8,
    )
    blocks = [blocks[0]] + [
        lax.ppermute(
            blocks[k],
            ("core", "ref"),
            [(c * refs + i, c * refs + (i ^ ref_steps[c][k])) for c in range(cores) for i in range(refs)],
        )
        for k in range(1, refs)
    ]

    def share_parts(ref_in, share_high, share_low):
        core = lax.axis_index("core")
        share = ref_in[pl.ds(pl.multiple_of(core * share_rows, share_rows), share_rows), :]
        share_high[...], share_low[...] = split(share)

    share_high, share_low = call(share_parts, [(share_rows, width)] * 2, ref_factor, short_outs=(0, 1), room=8)

    def chip_blocks(keep_ref, came_ref, *rest):
        outs, full = rest[:-1], rest[-1]
        chip, core = lax.axis_index("chip"), lax.axis_index("core")
        full[...] = keep_ref[...] + came_ref[...]
        for k in range(chips):
            to = chip ^ step_at(chip_steps, k, core)
            outs[k][...] = full[pl.ds(pl.multiple_of(to * ca, ca), ca), :]

    cand_blocks = call(chip_blocks, [(ca, half)] * chips, keep, came, scratch=[(rank, half)])
    cand_blocks = [cand_blocks[0]] + [
        lax.ppermute(
            cand_blocks[k],
            ("chip", "core"),
            [(i * cores + c, (i ^ chip_steps[c][k]) * cores + c) for c in range(cores) for i in range(chips)],
        )
        for k in range(1, chips)
    ]

    def own_blocks(*rest):
        out = rest[-1]
        for start, count, terms in ((0, ca, rest[:chips]), (ca, ra, rest[chips:-1])):
            total = terms[0][...]
            for term in terms[1:]:
                total = total + term[...]
            out[start : start + count, :] = total

    (mine,) = call(own_blocks, [(ca + ra, half)], *cand_blocks, *blocks)
    other = swap_core(mine, cores)

    def columns_at(moment, at, columns, padded):
        padded[...] = jnp.zeros_like(padded)
        padded[pl.ds(pl.multiple_of(at * columns, columns), columns), :] = moment
        return padded[...]

    def own_lanes(factor, core):
        return factor[:, pl.ds(pl.multiple_of(core * half, half), half)]

    def half_columns(mine_ref, cand_high, cand_low, share_high, share_low, cand_out, share_out, out, padded, rows):
        chip, core, ref = (lax.axis_index(a) for a in ("chip", "core", "ref"))
        moment = columns_at(mine_ref[ca:, :], ref, ra, padded)
        cand_out[...] = rows_by_rows((own_lanes(cand_high, core), own_lanes(cand_low, core)), moment)
        moment = columns_at(mine_ref[:ca, :], chip, ca, padded)
        share_out[...] = rows_by_rows((own_lanes(share_high, core), own_lanes(share_low, core)), moment)
        for lane in range(lanes):
            at = slice(lane * 128, (lane + 1) * 128)
            rows[lane * ca : (lane + 1) * ca, :] = mine_ref[:ca, at]
            rows[block_rows + lane * ra : block_rows + (lane + 1) * ra, :] = mine_ref[ca:, at]
        for e in range(chips):
            for d in range(refs):
                to = lax.rem(chip + chips - e, chips) * refs + lax.rem(ref + refs - d, refs)
                if e and d:
                    part = [rows[few * (d - 1) : few * d, :]]
                    part += [rows[block_rows + few * (e - 1) : block_rows + few * e, :]]
                elif e:
                    part = [rows[last:block_rows, :]]
                else:
                    part = [rows[block_rows + last : 2 * block_rows, :]]
                short = 2 * few - sum(p.shape[0] for p in part)
                part += [jnp.zeros((short, rank), f32)] if short else []
                out[pl.ds(to * tall_piece, 2 * few), :] = jnp.concatenate(part, axis=0)
        for i in range(chips * refs):
            out[(i + 1) * tall_piece - 1 : (i + 1) * tall_piece, :] = jnp.zeros((1, rank), f32)

    cand_cols_part, share_cols_part, data = call(
        half_columns,
        [(cand_rows, rank), (share_rows, rank), (chips * refs * tall_piece, 128)],
        mine, cand_high, cand_low, share_high, share_low,
        scratch=[(rank, half), (2 * block_rows, 128)],
        room=12,
    )

    def column_tops(
        mine_ref, other_ref, cand_high, cand_low, share_high, share_low, cand_part, share_part, data_ref, w_ref, out, padded
    ):
        chip, core, ref = (lax.axis_index(a) for a in ("chip", "core", "ref"))
        w = w_ref[...]
        moment = columns_at(other_ref[ca:, :], ref, ra, padded)
        factor = (own_lanes(cand_high, 1 - core), own_lanes(cand_low, 1 - core))
        grad_cand = cand_part[...] + rows_by_rows(factor, moment)
        moment = columns_at(other_ref[:ca, :], chip, ca, padded)
        factor = (own_lanes(share_high, 1 - core), own_lanes(share_low, 1 - core))
        grad_ref = share_part[...] + rows_by_rows(factor, moment)
        tall = jnp.maximum(
            jnp.max(jnp.abs(grad_cand), axis=0, keepdims=True), jnp.max(jnp.abs(grad_ref), axis=0, keepdims=True)
        )
        top = tall / w
        out[...] = data_ref[...]
        for i in range(chips * refs):
            out[(i + 1) * tall_piece - 1 : (i + 1) * tall_piece, :] = top

    (to_all,) = call(
        column_tops,
        [(chips * refs * tall_piece, 128)],
        mine,
        other,
        cand_high,
        cand_low,
        share_high,
        share_low,
        cand_cols_part,
        share_cols_part,
        data,
        weights_row,
        scratch=[(rank, half)],
        room=12,
    )
    to_all = to_all.reshape(chips * refs, tall_piece, 1, 128)
    got = lax.all_to_all(to_all, ("chip", "ref"), 0, 0).reshape(-1, 128)
    got_other = swap_core(got, cores)

    def mass_part(kernel_cand, kernel_ref, scale_cand, scale_ref, out):
        row_cand = rank / jnp.sum(kernel_cand * scale_cand, axis=1, keepdims=True)
        row_ref = rank / jnp.sum(kernel_ref * scale_ref, axis=1, keepdims=True)
        mass_cand = jnp.sum(row_cand * kernel_cand, axis=0, keepdims=True) / cand_total
        mass_ref = jnp.sum(row_ref * kernel_ref, axis=0, keepdims=True) / ref_total
        both = jnp.concatenate([mass_cand, mass_ref], axis=0)
        out[...] = jnp.broadcast_to(both[None], (everyone, 2, rank))

    def assemble(pieces_ref, own_ref, cand_half, ref_half, rows):
        chip, ref = lax.axis_index("chip"), lax.axis_index("ref")

        def piece(e, d, start, count):
            at = lax.rem(chip + e, chips) * refs + lax.rem(ref + d, refs)
            return pieces_ref[pl.ds(at * tall_piece + start, count), :]

        def spread(half_ref, at, columns):
            at = pl.ds(pl.multiple_of(at * columns, columns), columns)
            for lane in range(lanes):
                half_ref[at, lane * 128 : (lane + 1) * 128] = rows[lane * columns : (lane + 1) * columns, :]

        cand_half[pl.ds(pl.multiple_of(chip * ca, ca), ca), :] = own_ref[:ca, :]
        ref_half[pl.ds(pl.multiple_of(ref * ra, ra), ra), :] = own_ref[ca:, :]
        for e in range(1, chips):
            rows[last:, :] = piece(e, 0, 0, block_rows - last)
            for d in range(1, refs):
                rows[few * (d - 1) : few * d, :] = piece(e, d, 0, few)
            spread(cand_half, lax.rem(chip + e, chips), ca)
        for d in range(1, refs):
            rows[last:, :] = piece(0, d, 0, block_rows - last)
            for e in range(1, chips):
                rows[few * (e - 1) : few * e, :] = piece(e, d, few, few)
            spread(ref_half, lax.rem(ref + d, refs), ra)
        tops = pieces_ref[tall_piece - 1 : tall_piece, :]
        for i in range(1, chips * refs):
            tops = jnp.maximum(tops, pieces_ref[(i + 1) * tall_piece - 1 : (i + 1) * tall_piece, :])
        product = cand_half[...] * ref_half[...]
        folded = product[:, :128]
        for lane in range(1, lanes):
            folded = folded + product[:, lane * 128 : (lane + 1) * 128]
        return tops, jnp.sum(folded.T, axis=0, keepdims=True)

    def half_kernels(
        got_ref, own_ref, cand_high, cand_low, share_high, share_low,
        cand_half, cand_out, share_out, rows_out, ref_half, rows,
    ):
        chip, core = lax.axis_index("chip"), lax.axis_index("core")
        tops, inner = assemble(got_ref, own_ref, cand_half, ref_half, rows)
        rows_out[0:1, :] = tops
        rows_out[1:2, :] = inner
        cand_out[...] = rows_by_rows((own_lanes(cand_high, core), own_lanes(cand_low, core)), ref_half[...])
        at = pl.ds(pl.multiple_of(chip * ref_sub, ref_sub), ref_sub)
        lane = pl.ds(pl.multiple_of(core * half, half), half)
        share_out[...] = rows_by_rows((share_high[at, lane], share_low[at, lane]), cand_half[...])

    cand_half, cand_part, share_part, rows_part = call(
        half_kernels,
        [(rank, half), (cand_rows, rank), (ref_sub, rank), (8, rank)],
        got, mine, cand_high, cand_low, share_high, share_low,
        scratch=[(rank, half), (block_rows, 128)],
        room=12,
    )

    def first_kernels(
        got_ref, own_ref, cand_high, cand_low, cand_plan_ref, share_high, share_low, ref_plan_ref, w_ref,
        cand_half, cand_part, share_part, rows_part,
        cand_moment, full_cand, state, sub_cand, sub_ref, out, other_half, ref_half, rows,
    ):
        chip, core, ref = (lax.axis_index(a) for a in ("chip", "core", "ref"))
        tops, inner = assemble(got_ref, own_ref, other_half, ref_half, rows)
        tops = jnp.maximum(tops, rows_part[0:1, :])
        cand_moment[:, :half] = jnp.where(core == 0, cand_half[...], other_half[...])
        cand_moment[:, half:] = jnp.where(core == 0, other_half[...], cand_half[...])
        w = w_ref[...]
        grad_weights = -(inner + rows_part[1:2, :]) / (w * w)
        top = jnp.maximum(jnp.max(tops, axis=1, keepdims=True), largest(grad_weights)) + tiny_value
        kernel_weights = w * jnp.exp(-step_size * grad_weights / top)
        state[0:1, :] = kernel_weights
        state[1:2, :] = jnp.broadcast_to(top, (1, rank))
        state[2:8, :] = jnp.ones((6, rank), f32)
        factor = (own_lanes(cand_high, 1 - core), own_lanes(cand_low, 1 - core))
        grad = (cand_part[...] + rows_by_rows(factor, ref_half[...])) / w
        full_cand[...] = cand_plan_ref[...] * jnp.exp(-step_size * grad / top)
        kernel_cand = full_cand[pl.ds(pl.multiple_of(ref * cand_sub, cand_sub), cand_sub), :]
        at = pl.ds(pl.multiple_of(chip * ref_sub, ref_sub), ref_sub)
        lane = pl.ds(pl.multiple_of((1 - core) * half, half), half)
        grad = (share_part[...] + rows_by_rows((share_high[at, lane], share_low[at, lane]), other_half[...])) / w
        at = pl.ds(pl.multiple_of(core * share_rows + chip * ref_sub, ref_sub), ref_sub)
        kernel_ref = ref_plan_ref[at, :] * jnp.exp(-step_size * grad / top)
        sub_cand[...] = kernel_cand
        sub_ref[...] = kernel_ref
        ones = jnp.ones((1, rank), f32)
        mass_part(kernel_cand, kernel_ref, ones, ones, out)

    cand_moment, full_cand, state, sub_cand, sub_ref, out = call(
        first_kernels,
        [(rank, width), (cand_rows, rank), (8, rank), (cand_sub, rank), (ref_sub, rank), (everyone, 2, rank)],
        got_other, other, cand_high, cand_low, cand_plan, share_high, share_low, ref_plan, weights_row,
        cand_half, cand_part, share_part, rows_part,
        scratch=[(rank, half), (rank, half), (block_rows, 128)],
        room=12,
    )

    def update(mass_ref, state):
        mass = jnp.sum(mass_ref[...], axis=0)
        mass_cand, mass_ref = mass[0:1], mass[1:2]
        kernel_weights, scale_cand, scale_ref = state[0:1, :], state[2:3, :], state[3:4, :]
        new_weights = cube_root(kernel_weights * scale_cand * mass_cand * scale_ref * mass_ref)
        return new_weights, new_weights / mass_cand, new_weights / mass_ref

    def next_masses(mass_ref, state_ref, sub_cand_ref, sub_ref_ref, new_state, out):
        _, scale_cand, scale_ref = update(mass_ref, state_ref)
        new_state[...] = state_ref[...]
        new_state[2:3, :] = scale_cand
        new_state[3:4, :] = scale_ref
        mass_part(sub_cand_ref[...], sub_ref_ref[...], scale_cand, scale_ref, out)

    for _ in range(ITERS - 1):
        mass = lax.all_to_all(out, ("chip", "core", "ref"), 0, 0)
        state, out = call(next_masses, [(8, rank), (everyone, 2, rank)], mass, state, sub_cand, sub_ref)
    mass = lax.all_to_all(out, ("chip", "core", "ref"), 0, 0)

    def finish(
        mass_ref, cand_moment, state_ref, full_cand, ref_ref, ref_plan_ref, w_ref,
        cand_out, ref_out, w_out, cand_done, ref_done, w_done, sems,
    ):
        new_weights, scale_cand, scale_ref = update(mass_ref, state_ref)
        top = state_ref[1:2, :]
        kernel = full_cand[...]
        row = rank / jnp.sum(kernel * state_ref[2:3, :], axis=1, keepdims=True)
        cand_done[...] = row * kernel * scale_cand
        stores = [pltpu.make_async_copy(cand_done, cand_out, sems.at[0])]
        stores[0].start()
        w_done[...] = new_weights
        stores += [pltpu.make_async_copy(w_done, w_out, sems.at[1])]
        stores[1].start()
        grad = rows_by_rows(split(ref_ref[...]), cand_moment[...]) / w_ref[...]
        kernel = ref_plan_ref[...] * jnp.exp(-step_size * grad / top)
        row = rank / jnp.sum(kernel * state_ref[3:4, :], axis=1, keepdims=True)
        ref_done[...] = row * kernel * scale_ref
        stores += [pltpu.make_async_copy(ref_done, ref_out, sems.at[2])]
        stores[2].start()
        for c in stores:
            c.wait()

    new_cand_plan, new_ref_plan, new_weights = call(
        finish,
        [(cand_rows, rank), (ref_rows, rank), (1, rank)],
        mass, cand_moment, state, full_cand, ref_factor, ref_plan, weights_row,
        scratch=[(cand_rows, rank), (ref_rows, rank), (1, rank), dma((3,))],
        slow_outs=(0, 1, 2),
        room=8,
    )
    return new_cand_plan, new_ref_plan, new_weights.reshape(rank)


def on_device(*args):
    chips, cores, refs = (lax.axis_size(a) for a in ("chip", "core", "ref"))
    rank, width = args[4].shape[0], args[0].shape[1]
    rows = (args[0].shape[0] // refs, args[1].shape[0] // (chips * cores))
    tiled = cores == 2 and chips == refs and rank == 128 and rank % (8 * chips * refs) == 0 and width % (128 * cores) == 0
    tiled = tiled and all(n % 8 == 0 for n in rows)
    return (on_device_tiled if tiled else on_device_any)(*args)


def solution(mesh):
    cand, ref = mesh.shape["cand"], mesh.shape["ref"]
    cores = 2 if cand % 2 == 0 else 1
    finer = Mesh(mesh.devices.reshape(cand // cores, cores, ref), ("chip", "core", "ref"))
    rows = ("chip", "core")
    in_specs = (P(rows, None), P("ref", None), P(rows, None), P("ref", None), P())
    out_specs = (P(rows, None), P("ref", None), P())
    return jax.shard_map(on_device, mesh=finer, in_specs=in_specs, out_specs=out_specs, check_vma=False)
```
